32 devices in a mesh: tm: 2 (over core), lat: 16 (over z, y, x).
Axes of the slice: x: 2, y: 2, z: 4, core: 2. Of those that a mesh axis runs over, the one named last changes fastest.
Arguments:
- spectral_state: float32 [4, 16, 2, 16, 256], P('tm', 'lat'), may hold values from -6 to 6
- legendre: bfloat16 [16, 16, 16], P('lat'), may hold values from -1.5 to 1.5
- wave_slots: int32 [16], replicated, may hold values from 0 to 15, each once
- lat_order: int32 [16], replicated, may hold values from 0 to 15, each once
- quad_weights: float32 [16], replicated, may hold values from 0.2 to 1
- available: int32 [4, 8, 16, 256], P('tm', None, 'lat'), may hold values 0 or 1
- targets: float32 [4, 4, 8], P('tm'), may hold values from -6 to 6
- w_first: float32 [256, 384], replicated, may hold values from -0.375 to 0.375
- w_mid: float32 [384, 384], replicated, may hold values from -0.3125 to 0.3125
- w_last: float32 [384, 256], replicated, may hold values from -0.3125 to 0.3125
- norm_bias: float32 [2, 1024], replicated, may hold values from -0.3 to 0.3
- mean_first: float32 [256, 384], replicated, may hold values from -0.00061035156 to 0.00061035156
- mean_mid: float32 [384, 384], replicated, may hold values from -0.00061035156 to 0.00061035156
- mean_last: float32 [384, 256], replicated, may hold values from -0.00061035156 to 0.00061035156
- mean_bias: float32 [2, 1024], replicated, may hold values from -0.00061035156 to 0.00061035156
- square_first: float32 [256, 384], replicated, may hold values from 3e-10 to 3e-08
- square_mid: float32 [384, 384], replicated, may hold values from 3e-10 to 3e-08
- square_last: float32 [384, 256], replicated, may hold values from 3e-10 to 3e-08
- square_bias: float32 [2, 1024], replicated, may hold values from 3e-10 to 3e-08
Outputs:
- loss: float32 [], replicated
- grad_norm: float32 [], replicated
- master_first: float32 [256, 384], replicated
- master_mid: float32 [384, 384], replicated
- master_last: float32 [384, 256], replicated
- master_bias: float32 [2, 1024], replicated
- new_mean_first: float32 [256, 384], replicated
- new_mean_mid: float32 [384, 384], replicated
- new_mean_last: float32 [384, 256], replicated
- new_mean_bias: float32 [2, 1024], replicated
- new_square_first: float32 [256, 384], replicated
- new_square_mid: float32 [384, 384], replicated
- new_square_last: float32 [384, 256], replicated
- new_square_bias: float32 [2, 1024], replicated
- half_first: bfloat16 [256, 384], replicated
- half_mid: bfloat16 [384, 384], replicated
- half_last: bfloat16 [384, 256], replicated
- half_bias: bfloat16 [2, 1024], replicated
The draws below stay inside these ranges and needn't reach their ends.
Inputs may be any that keep to these rules, and one draw needn't show every extreme that they name: `wave_slots`: each wavenumber 0 to 15 stands in one slot; slot j lies on the device of index j // 1 of lat. `lat_order`: each latitude stands in one grid row.
All inputs are finite; a program needn't handle non-finite values. No bound on the sum of `available` on one device may be relied on, other than what follows from the above.
Results may differ from the reference program's by a relative error of at most 0.0082.
Values may be sent and summed in bfloat16 or wider, within the bound.
No kernel may reach another device: no remote copies, remote signals or barrier semaphores. Data moves between devices by JAX's collectives and lax.ppermute only.
A program may use at most 128 MiB of HBM per device.

```python
import math
import jax
import jax.numpy as jnp
from jax import lax

FIELDS = 8
LEVELS = 32
CHANNELS = 256
HIDDEN_SIZE = 384
LONGITUDES = 256
LATITUDES = 16
WAVES = 16
DEGREES = 16
TIMES = 4
STEPS = 4


def place_ends(drawn, rng, low, high):
    shape = drawn.shape
    index_at = [jax.random.randint(jax.random.fold_in(rng, axis), (), 0, shape[axis]) for axis in range(len(shape))]
    drawn = drawn.at[tuple(index_at)].set(low)
    longest = shape.index(max(shape))
    index_at[longest] = (index_at[longest] + 1) % shape[longest]
    return drawn.at[tuple(index_at)].set(high)


def shard_levels(rng, extent, split, low, high):
    factor_of = 1.0
    for dim, blocks in split:
        draws = jax.random.uniform(jax.random.fold_in(jax.random.fold_in(rng, 6), dim), (blocks,), jnp.float32, low / len(split), high / len(split))
        factor_of = factor_of * jnp.repeat(jnp.exp(draws), extent[dim] // blocks).reshape((-1,) + (1,) * (len(extent) - 1 - dim))
    return factor_of


def scatter_about(rng, extent, width, most, pieces=(), kind=jnp.bfloat16):
    level = shard_levels(rng, extent, pieces, -0.22, 0.18) if pieces else 1.0
    values = jax.random.normal(rng, extent, jnp.float32) * width * level
    return jnp.minimum(jnp.maximum(values, -most), most).astype(kind)


def setup_inputs(seed: int = 0) -> dict:
    key_of = jax.random.split(jax.random.key(seed), 20)
    return {
        "spectral_state": scatter_about(key_of[0], (TIMES, WAVES, 2, DEGREES, CHANNELS), 1.0, 6.0, ((0, 2), (1, 16)), jnp.float32),
        "legendre": scatter_about(key_of[1], (WAVES, DEGREES, LATITUDES), DEGREES ** -0.5, 1.5, ((0, 16),)),
        "wave_slots": jax.random.permutation(key_of[2], WAVES).astype(jnp.int32),
        "lat_order": jax.random.permutation(key_of[3], LATITUDES).astype(jnp.int32),
        "quad_weights": jnp.clip(jnp.exp(jax.random.uniform(key_of[4], (LATITUDES,), jnp.float32, math.log(0.2), math.log(1.0))), 0.2, 1.0),
        "available": place_ends((jax.random.randint(key_of[5], (TIMES, FIELDS, LATITUDES, LONGITUDES), 0, 10) < 9).astype(jnp.int32), jax.random.fold_in(key_of[5], 1), 0, 1),
        "targets": scatter_about(key_of[6], (TIMES, STEPS, FIELDS), 1.0, 6.0, ((0, 2),), jnp.float32),
        "w_first": scatter_about(key_of[7], (CHANNELS, HIDDEN_SIZE), CHANNELS ** -0.5, 0.375, (), jnp.float32),
        "w_mid": scatter_about(key_of[8], (HIDDEN_SIZE, HIDDEN_SIZE), HIDDEN_SIZE ** -0.5, 0.3125, (), jnp.float32),
        "w_last": scatter_about(key_of[9], (HIDDEN_SIZE, CHANNELS), HIDDEN_SIZE ** -0.5, 0.3125, (), jnp.float32),
        "norm_bias": scatter_about(key_of[10], (2, CHANNELS + 2 * HIDDEN_SIZE), 0.05, 0.3, (), jnp.float32),
        "mean_first": scatter_about(key_of[11], (CHANNELS, HIDDEN_SIZE), 0.0001, 0.00061035156, (), jnp.float32),
        "mean_mid": scatter_about(key_of[12], (HIDDEN_SIZE, HIDDEN_SIZE), 0.0001, 0.00061035156, (), jnp.float32),
        "mean_last": scatter_about(key_of[13], (HIDDEN_SIZE, CHANNELS), 0.0001, 0.00061035156, (), jnp.float32),
        "mean_bias": scatter_about(key_of[14], (2, CHANNELS + 2 * HIDDEN_SIZE), 0.0001, 0.00061035156, (), jnp.float32),
        "square_first": jnp.clip(jnp.exp(jax.random.uniform(key_of[15], (CHANNELS, HIDDEN_SIZE), jnp.float32, math.log(2.999999970665357e-10), math.log(2.999999892949745e-08))), 2.999999970665357e-10, 2.999999892949745e-08),
        "square_mid": jnp.clip(jnp.exp(jax.random.uniform(key_of[16], (HIDDEN_SIZE, HIDDEN_SIZE), jnp.float32, math.log(2.999999970665357e-10), math.log(2.999999892949745e-08))), 2.999999970665357e-10, 2.999999892949745e-08),
        "square_last": jnp.clip(jnp.exp(jax.random.uniform(key_of[17], (HIDDEN_SIZE, CHANNELS), jnp.float32, math.log(2.999999970665357e-10), math.log(2.999999892949745e-08))), 2.999999970665357e-10, 2.999999892949745e-08),
        "square_bias": jnp.clip(jnp.exp(jax.random.uniform(key_of[18], (2, CHANNELS + 2 * HIDDEN_SIZE), jnp.float32, math.log(2.999999970665357e-10), math.log(2.999999892949745e-08))), 2.999999970665357e-10, 2.999999892949745e-08),
    }


EPS_NORM = 1e-05
STEP_SCALE = 0.5
CLIP_NORM = 1.0
LEARN_RATE = 0.01
BETA_ONE = 0.9
BETA_TWO = 0.95
EPS_ADAM = 1e-08
DECAY = 0.1
HIGH = lax.Precision.HIGHEST

@jax.custom_vjp
def low(v):
    return lax.optimization_barrier(v.astype(jnp.bfloat16)).astype(jnp.float32)

@jax.custom_vjp
def low_back(v):
    return v

def low_keep(v):
    return (low(v), None)

def low_pass(kept, grad):
    return (grad,)

def back_keep(v):
    return (v, None)

def back_low(kept, grad):
    return (low(grad),)
low.defvjp(low_keep, low_pass)
low_back.defvjp(back_keep, back_low)

def wave_tables(wave_slots):
    product = wave_slots[:, None] * jnp.arange(LONGITUDES, dtype=jnp.int32)[None, :] % LONGITUDES
    phase = product.astype(jnp.float32) * (2.0 * math.pi / LONGITUDES)
    inverse = jnp.stack([jnp.cos(phase), -jnp.sin(phase)], axis=1)
    scale = jnp.where(wave_slots == 0, 1.0, 2.0).astype(jnp.float32) / LONGITUDES
    return (low(inverse), low(inverse * scale[:, None, None]))

def layer_spans(chans, hidden):
    gains = [(0, chans), (chans, hidden), (chans + hidden, hidden)]
    biases = [(0, hidden), (hidden, hidden), (2 * hidden, chans)]
    return list(zip(gains, biases))

def norm_gain(x, gain):
    centre = x - lax.optimization_barrier(jnp.mean(x, axis=-1, keepdims=True))
    return centre * lax.rsqrt(lax.optimization_barrier(jnp.mean(centre * centre, axis=-1, keepdims=True)) + EPS_NORM) * gain

def corrector(x, weights, norm_bias):
    spans = layer_spans(CHANNELS, HIDDEN_SIZE)
    for k in range(3):
        (gstart, gwidth), (bstart, bwidth) = spans[k]
        h_low = low(norm_gain(x, 1.0 + norm_bias[0, gstart:gstart + gwidth]))
        z_val = low_back(jnp.dot(h_low, weights[k], precision=HIGH) + norm_bias[1, bstart:bstart + bwidth])
        x = jax.nn.gelu(z_val, approximate=False) if k < 2 else z_val
    return x

def advance(state, weights, norm_bias, plg, finv, ffw, qrow, colw):
    state_low = low(state)
    sums = low_back(low(jnp.einsum('mnr,mpnc->mprc', plg, state_low, precision=HIGH)))
    grid = low_back(jnp.einsum('mpk,mprc->rkc', finv, sums, precision=HIGH))
    out = corrector(grid.reshape(-1, CHANNELS), weights, norm_bias).reshape(grid.shape)
    pred = grid + STEP_SCALE * out
    num = jnp.einsum('frk,rkfl->f', colw, pred.reshape(LATITUDES, LONGITUDES, FIELDS, LEVELS), precision=HIGH)
    tend = low(out * qrow[:, None, None])
    coeff = low_back(low(jnp.einsum('mpk,rkc->mprc', ffw, tend, precision=HIGH)))
    spec = low_back(jnp.einsum('mnr,mprc->mpnc', plg, coeff, precision=HIGH))
    return (state + STEP_SCALE * spec, num)

def time_loss(params, state_t, avail_t, target_t, plg, finv, ffw, qrow):
    w_first, w_mid, w_last, norm_bias = params
    weights = (low(w_first), low(w_mid), low(w_last))
    colw = qrow[None, :, None] * avail_t.astype(jnp.float32)
    den = lax.optimization_barrier(jnp.sum(colw, axis=(1, 2)))
    stepper = jax.checkpoint(advance)
    state = state_t
    total = jnp.zeros((), jnp.float32)
    for s in range(STEPS):
        state, num = stepper(state, weights, norm_bias, plg, finv, ffw, qrow, colw)
        bias = num / (LEVELS * den) - target_t[s]
        total = total + jnp.sum(bias * bias)
    return total / STEPS

def adamw(weight, mean, square, grad):
    mean_new = BETA_ONE * mean + (1.0 - BETA_ONE) * grad
    square_new = BETA_TWO * square + (1.0 - BETA_TWO) * grad * grad
    weight_new = weight - LEARN_RATE * (mean_new / (jnp.sqrt(square_new) + EPS_ADAM) + DECAY * weight)
    return (weight_new, mean_new, square_new)

def reference(spectral_state, legendre, wave_slots, lat_order, quad_weights, available, targets, w_first, w_mid, w_last, norm_bias, mean_first, mean_mid, mean_last, mean_bias, square_first, square_mid, square_last, square_bias):
    finv, ffw = wave_tables(wave_slots)
    keep = (jnp.arange(DEGREES, dtype=jnp.int32)[None, :] >= wave_slots[:, None]).astype(jnp.float32)
    plg = (legendre.astype(jnp.float32) * keep[:, :, None])[:, :, lat_order]
    qrow = quad_weights[lat_order]
    params = (w_first, w_mid, w_last, norm_bias)

    def per_time(carry, items):
        state_t, avail_t, target_t = items
        value, pull = jax.vjp(lambda p: time_loss(p, state_t, avail_t, target_t, plg, finv, ffw, qrow), params)
        grads = pull(jnp.ones((), jnp.float32))[0]
        return ((carry[0] + value, tuple((a + b for a, b in zip(carry[1], grads)))), None)
    zeros = tuple((jnp.zeros_like(p) for p in params))
    (loss, grads), _ = lax.scan(per_time, (jnp.zeros((), jnp.float32), zeros), (spectral_state, available, targets))
    grad_norm = jnp.sqrt(sum((jnp.sum(g * g) for g in grads)))
    factor = CLIP_NORM / jnp.maximum(grad_norm, CLIP_NORM)
    means = (mean_first, mean_mid, mean_last, mean_bias)
    squares = (square_first, square_mid, square_last, square_bias)
    results = [adamw(w, a, b, g * factor) for w, a, b, g in zip(params, means, squares, grads)]
    masters = tuple((r[0] for r in results))
    new_means = tuple((r[1] for r in results))
    new_squares = tuple((r[2] for r in results))
    halves = tuple((w.astype(jnp.bfloat16) for w in masters))
    return (loss, grad_norm, masters[0], masters[1], masters[2], masters[3], new_means[0], new_means[1], new_means[2], new_means[3], new_squares[0], new_squares[1], new_squares[2], new_squares[3], halves[0], halves[1], halves[2], halves[3])
```

```python
from collections import namedtuple
from functools import partial
import math

import jax
import jax.numpy as jnp
from jax import lax
from jax.experimental import pallas as pl
from jax.experimental.pallas import tpu as pltpu
from jax.sharding import PartitionSpec as P

STEPS = 4


EPS_NORM = 1e-05
STEP_SCALE = 0.5
CLIP_NORM = 1.0
LEARN_RATE = 0.01
BETA_ONE = 0.9
BETA_TWO = 0.95
EPS_ADAM = 1e-08
DECAY = 0.1
HIGH = lax.Precision.HIGHEST


def wave_tables(wave_slots, lon_count):
    product = wave_slots[:, None] * jnp.arange(lon_count, dtype=jnp.int32)[None, :] % lon_count
    phase = product.astype(jnp.float32) * (2.0 * math.pi / lon_count)
    inverse = jnp.stack([jnp.cos(phase), -jnp.sin(phase)], axis=1)
    scale = jnp.where(wave_slots == 0, 1.0, 2.0).astype(jnp.float32) / lon_count
    return (inverse.astype(jnp.bfloat16), (inverse * scale[:, None, None]).astype(jnp.bfloat16))


def layer_spans(chans, hidden):
    gains = [(0, chans), (chans, hidden), (chans + hidden, hidden)]
    biases = [(0, hidden), (hidden, hidden), (2 * hidden, chans)]
    return list(zip(gains, biases))


def norm_gain(x, gain):
    centre = x - jnp.mean(x, axis=-1, keepdims=True)
    return centre * lax.rsqrt(jnp.mean(centre * centre, axis=-1, keepdims=True) + EPS_NORM) * gain


def corrector_forward(x, weights, norm_bias):
    spans = layer_spans(weights[0].shape[0], weights[0].shape[1])
    saved = []
    for k in range(3):
        (gstart, gwidth), (bstart, bwidth) = spans[k]
        h_low = norm_gain(x, 1.0 + norm_bias[0, gstart : gstart + gwidth]).astype(jnp.bfloat16)
        z_val = (
            jnp.dot(h_low, weights[k], preferred_element_type=jnp.float32)
            + norm_bias[1, bstart : bstart + bwidth]
        )
        saved.append((x, h_low, z_val))
        x = jax.nn.gelu(z_val, approximate=False) if k < 2 else z_val
    return (x, saved)


def corrector_backward(grad, saved, weights, norm_bias):
    spans = layer_spans(weights[0].shape[0], weights[0].shape[1])
    weight_grads = [None, None, None]
    gain_parts = [None, None, None]
    bias_parts = [None, None, None]
    for k in (2, 1, 0):
        (gstart, gwidth), (bstart, bwidth) = spans[k]
        x, h_low, z_val = saved[k]
        if k < 2:
            grad = jax.vjp(partial(jax.nn.gelu, approximate=False), z_val)[1](grad)[0]
        grad_low = grad.astype(jnp.bfloat16)
        weight_grads[k] = lax.dot_general(
            h_low, grad_low, (((0,), (0,)), ((), ())), preferred_element_type=jnp.float32
        )
        bias_parts[k] = jnp.sum(grad_low, axis=0, dtype=jnp.float32)
        back_h = lax.dot_general(
            grad_low, weights[k], (((1,), (1,)), ((), ())), preferred_element_type=jnp.float32
        )
        grad, gain_parts[k] = jax.vjp(norm_gain, x, 1.0 + norm_bias[0, gstart : gstart + gwidth])[
            1
        ](back_h)
    vector_grad = jnp.stack([jnp.concatenate(gain_parts), jnp.concatenate(bias_parts)])
    return (grad, (weight_grads[0], weight_grads[1], weight_grads[2], vector_grad))


def adamw(weight, mean, square, grad):
    mean_new = BETA_ONE * mean + (1.0 - BETA_ONE) * grad
    square_new = BETA_TWO * square + (1.0 - BETA_TWO) * grad * grad
    weight_new = weight - LEARN_RATE * (
        mean_new / (jnp.sqrt(square_new) + EPS_ADAM) + DECAY * weight
    )
    return (weight_new, mean_new, square_new)


def spread_device(
    spectral_state,
    legendre,
    wave_slots,
    lat_order,
    quad_weights,
    available,
    targets,
    w_first,
    w_mid,
    w_last,
    norm_bias,
    mean_first,
    mean_mid,
    mean_last,
    mean_bias,
    square_first,
    square_mid,
    square_last,
    square_bias,
):
    tdev, wdev, _, degrees, chans = spectral_state.shape
    fields = available.shape[1]
    rows_dev = available.shape[2]
    lon_count = available.shape[3]
    levels = chans // fields
    lat_index = lax.axis_index("lat")
    slots = lax.dynamic_slice_in_dim(wave_slots, lat_index * wdev, wdev)
    finv, ffw = wave_tables(wave_slots, lon_count)
    keep = (jnp.arange(degrees, dtype=jnp.int32)[None, :] >= slots[:, None]).astype(jnp.bfloat16)
    plg = jnp.take(legendre, lat_order, axis=2) * keep[:, :, None]
    qrow = jnp.take(quad_weights, lat_order)
    qlocal = lax.dynamic_slice_in_dim(qrow, lat_index * rows_dev, rows_dev)
    colw = qlocal[None, None, :, None] * available.astype(jnp.float32)
    den_part = jnp.sum(colw, axis=(2, 3))
    params = (w_first, w_mid, w_last, norm_bias)
    weights = (
        w_first.astype(jnp.bfloat16),
        w_mid.astype(jnp.bfloat16),
        w_last.astype(jnp.bfloat16),
    )

    def legendre_sum(piece):
        return jnp.einsum("mnr,tmprc->tmpnc", plg, piece, preferred_element_type=jnp.float32)

    def fourier_sum(table, piece):
        return jnp.einsum("mpk,tmprc->trkc", table, piece, preferred_element_type=jnp.float32)

    def to_grid(state):
        sums = jnp.einsum(
            "mnr,tmpnc->tmprc", plg, state.astype(jnp.bfloat16), preferred_element_type=jnp.float32
        ).astype(jnp.bfloat16)
        return fourier_sum(
            finv, lax.all_to_all(sums, "lat", split_axis=3, concat_axis=1, tiled=True)
        )

    def column_pass(grid):
        out, saved = corrector_forward(grid.reshape(-1, chans), weights, norm_bias)
        return (out.reshape(grid.shape), saved)

    states = []
    nums = []
    den_total = den_part
    state = spectral_state
    for s in range(STEPS):
        states.append(state)
        grid = to_grid(state)
        out, saved = column_pass(grid)
        pred = grid + STEP_SCALE * out
        num_part = jnp.einsum(
            "tfrk,trkfl->tf",
            colw,
            pred.reshape(tdev, rows_dev, lon_count, fields, levels),
            precision=HIGH,
        )
        num_total, den_total = lax.psum((num_part, den_part), "lat")
        nums.append(num_total)
        tend = (out * qlocal[None, :, None, None]).astype(jnp.bfloat16)
        coeff = jnp.einsum("mpk,trkc->tmprc", ffw, tend, preferred_element_type=jnp.float32).astype(
            jnp.bfloat16
        )
        spec = legendre_sum(lax.all_to_all(coeff, "lat", split_axis=1, concat_axis=3, tiled=True))
        state = state + STEP_SCALE * spec
    num_all = jnp.stack(nums)
    bias = num_all / (levels * den_total[None]) - jnp.moveaxis(targets, 1, 0)
    loss = lax.psum(jnp.sum(bias * bias) / STEPS, "tm")
    grad_bias = 2.0 * bias / (STEPS * levels * den_total[None])
    totals = tuple((jnp.zeros_like(p) for p in params))
    back_state = None
    for s in reversed(range(STEPS)):
        grid = to_grid(states[s])
        out, saved = column_pass(grid)
        scaled = jnp.moveaxis(colw * grad_bias[s][:, :, None, None], 1, 3)
        back_pred = jnp.broadcast_to(scaled[..., None], scaled.shape + (levels,)).reshape(
            grid.shape
        )
        back_out = STEP_SCALE * back_pred
        if back_state is not None:
            back_spec = (STEP_SCALE * back_state).astype(jnp.bfloat16)
            back_coeff = jnp.einsum(
                "mnr,tmpnc->tmprc", plg, back_spec, preferred_element_type=jnp.float32
            ).astype(jnp.bfloat16)
            back_tend = fourier_sum(
                ffw, lax.all_to_all(back_coeff, "lat", split_axis=3, concat_axis=1, tiled=True)
            )
            back_out = back_out + qlocal[None, :, None, None] * back_tend
        back_in, grads = corrector_backward(back_out.reshape(-1, chans), saved, weights, norm_bias)
        totals = tuple((a + b for a, b in zip(totals, grads)))
        if s > 0:
            back_grid = (back_pred + back_in.reshape(grid.shape)).astype(jnp.bfloat16)
            back_sums = jnp.einsum(
                "mpk,trkc->tmprc", finv, back_grid, preferred_element_type=jnp.float32
            ).astype(jnp.bfloat16)
            back_low = legendre_sum(
                lax.all_to_all(back_sums, "lat", split_axis=1, concat_axis=3, tiled=True)
            )
            back_state = back_low if back_state is None else back_state + back_low
    means = (mean_first, mean_mid, mean_last, mean_bias)
    squares = (square_first, square_mid, square_last, square_bias)
    grads = lax.psum(totals, ("tm", "lat"))
    grad_norm = jnp.sqrt(sum((jnp.sum(g * g) for g in grads)))
    factor = CLIP_NORM / jnp.maximum(grad_norm, CLIP_NORM)
    results = [adamw(w, a, b, g * factor) for w, a, b, g in zip(params, means, squares, grads)]
    masters = [r[0] for r in results]
    new_means = [r[1] for r in results]
    new_squares = [r[2] for r in results]
    halves = [w.astype(jnp.bfloat16) for w in masters]
    return (
        loss,
        grad_norm,
        masters[0],
        masters[1],
        masters[2],
        masters[3],
        new_means[0],
        new_means[1],
        new_means[2],
        new_means[3],
        new_squares[0],
        new_squares[1],
        new_squares[2],
        new_squares[3],
        halves[0],
        halves[1],
        halves[2],
        halves[3],
    )


F32 = jnp.float32
BF16 = jnp.bfloat16
VM = pltpu.VMEM
LANES = 128
GROUP = 2
SUB = 256
ROWS_BLOCK = 2
VMEM_LIMIT = 30 << 20
SAVED_LIMIT = 96 << 20


Plan = namedtuple("Plan", ("group", "rows", "waves", "degrees", "steps", "fields", "chans", "hidden", "lons"))


def dot(a, b, dims=((1,), (0,))):
    return lax.dot_general(a, b, (dims, ((), ())), preferred_element_type=F32)


def norm_unit(x, eps):
    centre = x - jnp.mean(x, axis=-1, keepdims=True)
    scale = lax.rsqrt(jnp.mean(centre * centre, axis=-1, keepdims=True) + eps)
    return centre * scale, scale


def gelu_twice(z):
    arg = z * math.sqrt(0.5)
    cdf = 1.0 + lax.erf(arg)
    pdf = jnp.exp2(arg * arg * -math.log2(math.e))
    return z * cdf, cdf + (z * math.sqrt(2.0 / math.pi)) * pdf


def whole(a):
    return pl.BlockSpec(a.shape, lambda *_: (0,) * len(a.shape))


def fold(v):
    return jnp.sum(v.reshape(v.shape[0] // 8, 8, v.shape[1]), axis=0)


def field_mask(fields, chans):
    lane = lax.broadcasted_iota(jnp.int32, (fields, chans), 1)
    row = lax.broadcasted_iota(jnp.int32, (fields, chans), 0) * (chans // fields)
    return (lane >= row) & (lane < row + chans // fields)


def splits(nb, chans, hidden):
    gains = [1.0 + nb[0:1, a:b] for a, b in ((0, chans), (chans, chans + hidden), (chans + hidden, chans + 2 * hidden))]
    biases = [nb[1:2, a:b] for a, b in ((0, hidden), (hidden, 2 * hidden), (2 * hidden, 2 * hidden + chans))]
    return gains, biases


def pair_rows(plan):
    return ROWS_BLOCK if plan.rows % ROWS_BLOCK == 0 else 1


def row_weight(plan, info, order, quad, row):
    return quad[order[(info[1] * 2 + info[0]) * plan.rows + row]]


def prepare_kernel(plan, info, slots, order, quad, got, got_o, inv, ffw, state, links, lt, avail, nums, table, ffw_t):
    group, rows, waves, degrees, steps, fields, chans, _, _ = plan
    members = 2 * group
    core, member = info[0], info[1]
    span = waves * degrees
    mine = rows * waves
    half = fields // 2
    lats = rows * members
    leg = jnp.zeros((waves, chans), F32)
    row_of = lax.broadcasted_iota(jnp.int32, (waves, chans), 0)
    pick = lax.broadcasted_iota(jnp.int32, (8, chans), 0) == half
    for j in range(waves):
        at = pl.ds(j * degrees, degrees)
        for ref, p in ((got, core), (got_o, 1 - core)):
            hi = ref[j, 0:degrees, :].astype(F32)
            state[p, at, :] = hi + ref[j, degrees : 2 * degrees, :].astype(F32)
        tail = got[j, 2 * degrees : 2 * degrees + 8, :].astype(F32)
        line = jnp.sum(jnp.where(pick, tail, 0.0), axis=0, keepdims=True)
        leg = jnp.where(row_of == j, line, leg)
    iota = lambda d, s: lax.broadcasted_iota(jnp.int32, s, d)
    shape = (span, span)
    r0, r1 = iota(0, shape), iota(1, shape)
    expand = (iota(0, (span, waves)) // degrees == iota(1, (span, waves))).astype(F32).astype(BF16)
    rep = dot(expand, leg.astype(BF16))
    rep = jnp.where(r1 // lats == r0 % degrees, rep, 0.0).astype(BF16)
    lat_lane = jnp.zeros((8, span), jnp.int32)
    lane = iota(1, (8, span)) // waves
    for r in range(lats):
        lat_lane = jnp.where(lane == r, order[r], lat_lane)
    wave_row = jnp.zeros(shape, jnp.int32)
    for j in range(waves):
        wave_row = jnp.where(r0 // degrees == j, slots[j], wave_row)
    choose = (r0 % lats == lat_lane[0:1, :]).astype(F32).astype(BF16)
    plg = dot(rep, choose)
    plg = jnp.where((r0 // degrees == r1 % waves) & (r0 % degrees >= wave_row), plg, 0.0)
    flip = plg.T
    spot = member * 2 + core
    for role in range(members):
        other = (member ^ (role & (group - 1))) * 2 + (core ^ (role // group))
        piece = jnp.zeros((span, mine), F32)
        for w in range(members):
            piece = jnp.where(other == w, plg[:, w * mine : (w + 1) * mine], piece)
        links[role] = piece.astype(BF16)
    own = jnp.zeros((mine, span), F32)
    for w in range(members):
        own = jnp.where(spot == w, flip[w * mine : (w + 1) * mine, :], own)
    lt[...] = own.astype(BF16)
    den = jnp.zeros((fields, chans), F32)
    for r in range(rows):
        src = spot * rows + r
        a = got[src, 2 * degrees : 2 * degrees + 8, :].astype(F32)
        b = got_o[src, 2 * degrees : 2 * degrees + 8, :].astype(F32)
        first = jnp.where(core == 0, a, b)[0:half]
        second = jnp.where(core == 0, b, a)[0:half]
        both = jnp.concatenate([first, second], axis=0)
        avail[r] = both.astype(BF16)
        den += quad[order[src]] * both
    nums[...] = jnp.zeros_like(nums)
    nums[steps * fields :, :] = jnp.broadcast_to(jnp.sum(den, axis=1, keepdims=True), (fields, nums.shape[1]))
    table[...] = inv[...].T.astype(BF16)
    ffw_t[...] = ffw[...].T.astype(BF16)


def prepare_call(plan, info, slots, order, quad, got, got_o, inv, ffw):
    group, rows, waves, degrees, steps, fields, chans, _, lons = plan
    span, mine = waves * degrees, rows * waves
    ins = [got, got_o, inv, ffw]
    shapes = [
        jax.ShapeDtypeStruct((2, span, chans), F32),
        jax.ShapeDtypeStruct((2 * group, span, mine), BF16),
        jax.ShapeDtypeStruct((mine, span), BF16),
        jax.ShapeDtypeStruct((rows, fields, lons), BF16),
        jax.ShapeDtypeStruct(((steps + 1) * fields, LANES), F32),
        jax.ShapeDtypeStruct((lons, 2 * waves), BF16),
        jax.ShapeDtypeStruct((lons, 2 * waves), BF16),
    ]
    return pl.pallas_call(
        partial(prepare_kernel, plan),
        out_shape=shapes,
        grid_spec=pltpu.PrefetchScalarGridSpec(
            num_scalar_prefetch=4,
            grid=(1,),
            in_specs=[whole(a) for a in ins],
            out_specs=[whole(a) for a in shapes],
        ),
        compiler_params=kernel_params(),
        name="prepare",
    )(info, slots, order, quad, *ins)


def kernel_params():
    return pltpu.CompilerParams(vmem_limit_bytes=VMEM_LIMIT)


def forward_kernel(plan, step, info, order, quad, *refs):
    group, rows, waves, _, steps, fields, chans, hidden, lons = plan
    first, last = step == 0, step == steps - 1
    rows_blk = pair_rows(plan)
    refs = list(refs)
    take = lambda: refs.pop(0)
    state, avail, nums_in, table, ffw, lt, w1, w2, w3, nb = [take() for _ in range(10)]
    if not first:
        links = take()
        pieces = [take() for _ in range(2 * group)]
    units, slopes, scales, nums = [take() for _ in range(4)]
    if not last:
        y_out = take()
    if not first and not last:
        state_out = take()
    sums, num_acc = take(), take()
    i = pl.program_id(0)

    @pl.when(i == 0)
    def _():
        for p in range(2):
            st = state[p]
            if not first:
                spec = dot(links[0], pieces[0][p])
                for role in range(1, 2 * group):
                    spec = spec + dot(links[role], pieces[role][p])
                st = st + STEP_SCALE * spec
                if not last:
                    state_out[p] = st
            sums[p] = dot(lt[...], st.astype(BF16)).astype(BF16)
        num_acc[...] = jnp.zeros_like(num_acc)

    gains, biases = splits(nb, chans, hidden)
    for rr in range(rows_blk):
        row = i * rows_blk + rr
        at = pl.ds(pl.multiple_of(row * waves, waves), waves)
        rhs = jnp.concatenate([sums[0, at, :], sums[1, at, :]], axis=0)
        q = row_weight(plan, info, order, quad, row)
        highs, lows, tends = [], [], []
        for c0 in range(0, lons, SUB):
            cs = slice(rr * lons + c0, rr * lons + c0 + SUB)
            grid = dot(table[c0 : c0 + SUB, :], rhs)
            u1, s1 = norm_unit(grid, EPS_NORM)
            units[cs, 0:chans] = u1
            scales[cs, :] = jnp.broadcast_to(s1, (SUB, LANES))
            a1, d1 = gelu_twice(dot((u1 * gains[0]).astype(BF16), w1[...]) + biases[0])
            u2, s2 = norm_unit(a1, 4.0 * EPS_NORM)
            units[cs, chans : chans + hidden] = u2
            slopes[cs, 0:hidden] = d1 * s2
            a2, d2 = gelu_twice(dot((u2 * gains[1]).astype(BF16), w2[...]) + biases[1])
            u3, s3 = norm_unit(a2, 4.0 * EPS_NORM)
            units[cs, chans + hidden :] = u3
            slopes[cs, hidden:] = d2 * s3
            out = dot((u3 * gains[2]).astype(BF16), w3[...]) + biases[2]
            pred = grid + STEP_SCALE * out
            hi = pred.astype(BF16)
            highs.append(hi)
            lows.append((pred - hi.astype(F32)).astype(BF16))
            tends.append((out * q).astype(BF16))
        weigh = lambda parts: dot(avail[rr], jnp.concatenate(parts, axis=0))
        num_acc[...] += q * (weigh(highs) + weigh(lows))
        if not last:
            coeff = dot(ffw[...], jnp.concatenate(tends, axis=0)).astype(BF16)
            y_out[0, rr * waves : (rr + 1) * waves, :] = coeff[:waves]
            y_out[1, rr * waves : (rr + 1) * waves, :] = coeff[waves:]

    @pl.when(i == pl.num_programs(0) - 1)
    def _():
        kept = jnp.where(field_mask(fields, chans), num_acc[...], 0.0)
        nums[...] = nums_in[...]
        nums[step * fields : (step + 1) * fields, :] = jnp.broadcast_to(
            jnp.sum(kept, axis=1, keepdims=True), (fields, LANES)
        )


def forward_call(plan, step, scalars, state, avail, nums, table, ffw, lt, weights, nb, links, pieces):
    group, rows, waves, _, steps, fields, chans, hidden, lons = plan
    first, last = step == 0, step == steps - 1
    rows_blk = pair_rows(plan)
    cols, blk = rows * lons, rows_blk * lons
    ins = [state, avail, nums, table, ffw, lt, *weights, nb]
    if not first:
        ins += [links, *pieces]
    specs = [whole(a) for a in ins]
    specs[1] = pl.BlockSpec((rows_blk, fields, lons), lambda i, *_: (i, 0, 0))
    shapes, ospecs = [], []
    for width in (chans + 2 * hidden, 2 * hidden, LANES):
        shapes.append(jax.ShapeDtypeStruct((cols, width), F32))
        ospecs.append(pl.BlockSpec((blk, width), lambda i, *_: (i, 0)))
    shapes.append(jax.ShapeDtypeStruct(nums.shape, F32))
    ospecs.append(whole(nums))
    if not last:
        shapes.append(jax.ShapeDtypeStruct((2, rows * waves, chans), BF16))
        ospecs.append(pl.BlockSpec((2, rows_blk * waves, chans), lambda i, *_: (0, i, 0)))
    if not first and not last:
        shapes.append(jax.ShapeDtypeStruct(state.shape, F32))
        ospecs.append(whole(state))
    return pl.pallas_call(
        partial(forward_kernel, plan, step),
        out_shape=shapes,
        grid_spec=pltpu.PrefetchScalarGridSpec(
            num_scalar_prefetch=3,
            grid=(rows // rows_blk,),
            in_specs=specs,
            out_specs=ospecs,
            scratch_shapes=[VM((2, rows * waves, chans), BF16), VM((fields, chans), F32)],
        ),
        compiler_params=kernel_params(),
        name=f"forward_{step}",
    )(*scalars, *ins)


def packed_parts(plan):
    parts, at = [], 0
    sizes = ((plan.chans, plan.hidden), (plan.hidden, plan.hidden), (plan.hidden, plan.chans))
    for which, (rows, cols) in enumerate(sizes):
        for tile in range(cols // LANES):
            parts.append((which, tile, at, rows))
            at += rows
    return parts, at


def packed_block(plan, chips):
    vectors = 2 * (plan.chans + 2 * plan.hidden) // LANES
    need = packed_parts(plan)[1] + vectors
    return -(-need // (2 * chips * 16)) * 16


def both_halves(at, rows, half):
    out, done = [], 0
    while done < rows:
        h = (at + done) // half
        n = min(rows - done, (h + 1) * half - at - done)
        out.append((h, at + done - h * half, done, n))
        done += n
    return out


def backward_kernel(plan, step, info, order, quad, *refs):
    group, rows, waves, _, steps, fields, chans, hidden, lons = plan
    first, last = step == steps - 1, step == 0
    fresh = step == steps - 2
    rows_blk = pair_rows(plan)
    members = 2 * group
    levels = chans // fields
    refs = list(refs)
    take = lambda: refs.pop(0)
    units, slopes, scales, avail, tgt, w1, w2, w3, nb = [take() for _ in range(9)]
    counts = [take() for _ in range(members)]
    if not first:
        links, lt, ffw_t = [take() for _ in range(3)]
        pieces = [take() for _ in range(members)]
        if not fresh:
            bstate = take()
        before = [take() for _ in range(4)]
    if not last:
        inv = take()
        grads = [take() for _ in range(4)]
        b_out = take()
        if not first:
            bstate_out = take()
    else:
        mine, send = take(), take()
    if first:
        loss = take()
    coef, gmask = take(), take()
    if last:
        grads = [take() for _ in range(4)]
        packed = take()
    d1, d2, d3, dv = grads
    i = pl.program_id(0)

    @pl.when(i == 0)
    def _():
        def total(s):
            acc = [c[s * fields : (s + 1) * fields, :] for c in counts]
            while len(acc) > 1:
                acc = [a + b for a, b in zip(acc[::2], acc[1::2])]
            return acc[0]

        den = total(steps)
        bias_of = lambda s: total(s) / (levels * den) - tgt[s * fields : (s + 1) * fields, :]
        gb = 2.0 * bias_of(step) / (steps * levels * den)
        gb = jnp.concatenate([gb] * (chans // LANES), axis=1)
        gb = jnp.where(field_mask(fields, chans), gb, 0.0)
        hi = gb.astype(BF16).astype(F32)
        gmask[...] = jnp.concatenate([hi, gb - hi], axis=0).astype(BF16)
        if first:
            sq = bias_of(0) * bias_of(0)
            for s in range(1, steps):
                sq = sq + bias_of(s) * bias_of(s)
            loss[...] = jnp.broadcast_to(jnp.sum(sq, axis=0, keepdims=True) / steps, loss.shape)
            for d in grads:
                d[...] = jnp.zeros_like(d)
        else:
            for d, b in zip(grads, before):
                d[...] = b[...]
            for p in range(2):
                st = dot(links[0], pieces[0][p])
                for role in range(1, members):
                    st = st + dot(links[role], pieces[role][p])
                if not fresh:
                    st = bstate[p] + st
                if not last:
                    bstate_out[p] = st
                coef[p] = dot(lt[...], (STEP_SCALE * st).astype(BF16)).astype(BF16)

    gains, _ = splits(nb, chans, hidden)

    def norm_back(back, gain, unit):
        prod = back * unit
        low = back * gain
        m1 = jnp.mean(low, axis=-1, keepdims=True)
        m2 = jnp.mean(prod * gain, axis=-1, keepdims=True)
        return prod, low - m1 - unit * m2

    for rr in range(rows_blk):
        row = i * rows_blk + rr
        q = row_weight(plan, info, order, quad, row)
        av2 = jnp.concatenate([avail[rr].astype(F32)] * 2, axis=0).astype(BF16)
        if not first:
            at = pl.ds(pl.multiple_of(row * waves, waves), waves)
            rhs = jnp.concatenate([coef[0, at, :], coef[1, at, :]], axis=0)
        grids = []
        for c0 in range(0, lons, SUB):
            cs = slice(rr * lons + c0, rr * lons + c0 + SUB)
            dpred = q * dot(av2[:, c0 : c0 + SUB], gmask[...], ((0,), (0,)))
            dout = STEP_SCALE * dpred
            if not first:
                dout = dout + q * dot(ffw_t[c0 : c0 + SUB, :], rhs)
            dz = dout.astype(BF16)
            u = units[cs, chans + hidden :]
            d3[...] += dot((u * gains[2]).astype(BF16), dz, ((0,), (0,)))
            dv[8:16, 2 * hidden :] += fold(dz.astype(F32))
            prod, dx = norm_back(dot(dz, w3[...], ((1,), (1,))), gains[2], u)
            dv[0:8, chans + hidden :] += fold(prod)
            dz = (dx * slopes[cs, hidden:]).astype(BF16)
            u = units[cs, chans : chans + hidden]
            d2[...] += dot((u * gains[1]).astype(BF16), dz, ((0,), (0,)))
            dv[8:16, hidden : 2 * hidden] += fold(dz.astype(F32))
            prod, dx = norm_back(dot(dz, w2[...], ((1,), (1,))), gains[1], u)
            dv[0:8, chans : chans + hidden] += fold(prod)
            dz = (dx * slopes[cs, 0:hidden]).astype(BF16)
            u = units[cs, 0:chans]
            d1[...] += dot((u * gains[0]).astype(BF16), dz, ((0,), (0,)))
            dv[8:16, 0:hidden] += fold(dz.astype(F32))
            back = dot(dz, w1[...], ((1,), (1,)))
            if last:
                dv[0:8, 0:chans] += fold(back * u)
            else:
                prod, dx = norm_back(back, gains[0], u)
                dv[0:8, 0:chans] += fold(prod)
                grids.append((dpred + dx * scales[cs, 0:1]).astype(BF16))
        if not last:
            coeff = dot(inv[...], jnp.concatenate(grids, axis=0)).astype(BF16)
            b_out[0, rr * waves : (rr + 1) * waves, :] = coeff[:waves]
            b_out[1, rr * waves : (rr + 1) * waves, :] = coeff[waves:]

    if last:

        @pl.when(i == pl.num_programs(0) - 1)
        def _():
            half = packed.shape[1]
            parts, at = packed_parts(plan)
            for which, tile, start, count in parts:
                for h, dst, src, n in both_halves(start, count, half):
                    packed[h, dst : dst + n, :] = grads[which][src : src + n, tile * LANES : (tile + 1) * LANES]
            for v in range(2):
                line = jnp.sum(dv[v * 8 : v * 8 + 8, :], axis=0, keepdims=True)
                for tile in range(line.shape[1] // LANES):
                    row = at - half
                    packed[1, row : row + 1, :] = line[:, tile * LANES : (tile + 1) * LANES]
                    at += 1
            tail = at - half
            packed[1, tail:, :] = jnp.zeros((half - tail, LANES), F32)
            mine[...] = packed[info[0]]
            send[...] = packed[1 - info[0]]


def backward_call(plan, step, chips, scalars, saved, avail, tgt, weights, nb, counts, tables, pieces, bstate, before):
    group, rows, waves, degrees, steps, fields, chans, hidden, lons = plan
    first, last = step == steps - 1, step == 0
    rows_blk = pair_rows(plan)
    blk = rows_blk * lons
    links, lt, ffw_t, inv = tables
    ins = [*saved, avail, tgt, *weights, nb, *counts]
    if not first:
        ins += [links, lt, ffw_t, *pieces]
        if step != steps - 2:
            ins.append(bstate)
        ins += before
    if not last:
        ins.append(inv)
    specs = [whole(a) for a in ins]
    for n in range(3):
        specs[n] = pl.BlockSpec((blk, saved[n].shape[1]), lambda i, *_: (i, 0))
    specs[3] = pl.BlockSpec((rows_blk, fields, lons), lambda i, *_: (i, 0, 0))
    sums = [((chans, hidden), F32), ((hidden, hidden), F32), ((hidden, chans), F32), ((16, chans + 2 * hidden), F32)]
    scratch = [VM((2, rows * waves, chans), BF16), VM((2 * fields, chans), BF16)]
    if last:
        half = chips * packed_block(plan, chips)
        scratch += [VM(*s) for s in sums] + [VM((2, half, LANES), F32)]
        shapes = [jax.ShapeDtypeStruct((half, LANES), F32)] * 2
        ospecs = [whole(a) for a in shapes]
    else:
        shapes = [jax.ShapeDtypeStruct(*s) for s in sums]
        ospecs = [whole(a) for a in shapes]
        shapes.append(jax.ShapeDtypeStruct((2, rows * waves, chans), BF16))
        ospecs.append(pl.BlockSpec((2, rows_blk * waves, chans), lambda i, *_: (0, i, 0)))
        if not first:
            shapes.append(jax.ShapeDtypeStruct((2, waves * degrees, chans), F32))
            ospecs.append(whole(shapes[-1]))
    if first:
        shapes.append(jax.ShapeDtypeStruct((8, LANES), F32))
        ospecs.append(whole(shapes[-1]))
    return pl.pallas_call(
        partial(backward_kernel, plan, step),
        out_shape=shapes,
        grid_spec=pltpu.PrefetchScalarGridSpec(
            num_scalar_prefetch=3,
            grid=(rows // rows_blk,),
            in_specs=specs,
            out_specs=ospecs,
            scratch_shapes=scratch,
        ),
        compiler_params=kernel_params(),
        name=f"backward_{step}",
    )(*scalars, *ins)


def pairs_kernel(chips, group, mine, got, loss, out):
    blk = mine.shape[0] // chips
    share = loss[...] * (1.0 / group)
    row = lax.broadcasted_iota(jnp.int32, share.shape, 0)
    high = share.astype(BF16).astype(F32)
    rest = share - high
    mid = rest.astype(BF16).astype(F32)
    lines = jnp.where(row == 0, high, jnp.where(row == 1, mid, jnp.where(row == 2, rest - mid, 0.0)))
    lines = jnp.concatenate([lines, jnp.zeros_like(lines)], axis=0).astype(BF16)
    for c in range(chips):
        at = slice(c * blk, (c + 1) * blk)
        out[c, 0:blk, :] = (mine[at, :] + got[at, :]).astype(BF16)
        out[c, blk:, :] = lines


def chips_kernel(got, out, loss):
    chips, blk = out.shape[0], out.shape[1]
    total = got[0].astype(F32)
    for c in range(1, chips):
        total = total + got[c].astype(F32)
    low = total[0:blk].astype(BF16)
    for c in range(chips):
        out[c] = low
    loss[...] = jnp.broadcast_to(jnp.sum(total[blk:], axis=0, keepdims=True), loss.shape)


def update_kernel(plan, info, part, part_o, *refs):
    params, means, squares = refs[0:4], refs[4:8], refs[8:12]
    norm = refs[12]
    masters, new_means, new_squares, halves = refs[13:17], refs[17:21], refs[21:25], refs[25:29]
    packed = refs[29]
    packed[info[0]] = part[...]
    packed[1 - info[0]] = part_o[...]
    half = packed.shape[1]
    acc = jnp.zeros((16, LANES), F32)
    for h in range(2):
        g = packed[h].astype(F32)
        acc = acc + jnp.sum((g * g).reshape(half // 16, 16, LANES), axis=0)
    total = jnp.sum(jnp.sum(acc, axis=0, keepdims=True), axis=1, keepdims=True)
    root = jnp.sqrt(jnp.broadcast_to(total, (8, LANES)))
    norm[...] = root
    factor = (CLIP_NORM / jnp.maximum(root, CLIP_NORM))[0:1, :]

    def apply(which, rs, cs, g):
        w, a, b = adamw(params[which][rs, cs], means[which][rs, cs], squares[which][rs, cs], g * factor)
        masters[which][rs, cs] = w
        new_means[which][rs, cs] = a
        new_squares[which][rs, cs] = b
        halves[which][rs, cs] = w.astype(BF16)

    parts, at = packed_parts(plan)
    for which, tile, start, count in parts:
        for h, src, dst, n in both_halves(start, count, half):
            apply(which, slice(dst, dst + n), slice(tile * LANES, (tile + 1) * LANES), packed[h, src : src + n, :].astype(F32))
    tiles = (plan.chans + 2 * plan.hidden) // LANES
    rows = packed[1, at - half : at - half + 2 * tiles, :].astype(F32)
    for tile in range(tiles):
        g = jnp.concatenate([rows[tile : tile + 1], rows[tiles + tile : tiles + tile + 1]], axis=0)
        apply(3, slice(0, 2), slice(tile * LANES, (tile + 1) * LANES), g)


def small_call(kernel, name, shapes, ins, scalars=(), scratch=()):
    return pl.pallas_call(
        kernel,
        out_shape=shapes,
        grid_spec=pltpu.PrefetchScalarGridSpec(
            num_scalar_prefetch=len(scalars),
            grid=(1,),
            in_specs=[whole(a) for a in ins],
            out_specs=[whole(a) for a in shapes],
            scratch_shapes=list(scratch),
        ),
        compiler_params=kernel_params(),
        name=name,
    )(*scalars, *ins)


def grouped_device(
    plan,
    chips,
    spectral_state,
    legendre,
    wave_slots,
    lat_order,
    quad_weights,
    available,
    targets,
    *flat,
):
    group, rows, waves, degrees, steps, fields, chans, hidden, lons = plan
    params, means, squares = flat[0:4], flat[4:8], flat[8:12]
    weights = [w.astype(BF16) for w in params[:3]]
    nb = params[3]
    tdev = spectral_state.shape[0]
    copies = waves // chips
    core = lax.axis_index("tm")
    chip = lax.axis_index("lat")
    member = chip % group
    info = jnp.stack([core, member]).astype(jnp.int32)
    swap = [(0, 1), (1, 0)]
    across = lambda a: lax.ppermute(a, "tm", swap)

    def to_members(a):
        out = [a]
        bit = 1
        while bit < group:
            out += [lax.ppermute(v, "lat", [(n, n ^ bit) for n in range(waves)]) for v in out]
            bit *= 2
        return out + [across(v) for v in out]

    half = fields // 2
    pad = -(2 * degrees + half + 1) % 8
    high = spectral_state[:, 0].astype(BF16)
    low = (spectral_state[:, 0] - high.astype(F32)).astype(BF16)
    seen = available[:, :, 0].reshape(tdev, 2, half, lons).astype(BF16)
    leg = jnp.broadcast_to(legendre.reshape(1, 1, 1, chans), (tdev, 2, 1, chans))
    pack = jnp.concatenate([high, low, seen, leg, jnp.zeros((tdev, 2, pad, chans), BF16)], axis=2)
    keep = lax.dynamic_index_in_dim(pack, core, axis=1, keepdims=False)
    other = across(lax.dynamic_index_in_dim(pack, 1 - core, axis=1, keepdims=False))
    times = jnp.concatenate([jnp.where(core == 0, keep, other), jnp.where(core == 0, other, keep)], axis=0)
    spread = jnp.broadcast_to(times[None, :, None], (copies, 2 * tdev, group, *times.shape[1:]))
    got = lax.all_to_all(spread.reshape(waves, *times.shape[1:]), "lat", split_axis=0, concat_axis=0, tiled=True)
    got_o = across(got)

    def table(scaled):
        product = wave_slots[:, None] * jnp.arange(lons, dtype=jnp.int32)[None, :] % lons
        phase = product.astype(F32) * (2.0 * math.pi / lons)
        inverse = jnp.concatenate([jnp.cos(phase), -jnp.sin(phase)], axis=0)
        if not scaled:
            return inverse
        scale = jnp.where(wave_slots == 0, 1.0, 2.0).astype(F32) / lons
        return inverse * jnp.concatenate([scale, scale])[:, None]

    inv32, ffw32 = table(False), table(True)
    inv, ffw = inv32.astype(BF16), ffw32.astype(BF16)
    state, links, lt, avail, nums, inv_t, ffw_t = prepare_call(
        plan, info, wave_slots, lat_order, quad_weights, got, got_o, inv32, ffw32
    )
    theirs = across(targets)
    tgt_all = jnp.concatenate([jnp.where(core == 0, targets, theirs), jnp.where(core == 0, theirs, targets)], axis=0)
    tgt = lax.dynamic_index_in_dim(tgt_all, (chip // group) % (2 * tdev), axis=0, keepdims=False)
    tgt = jnp.broadcast_to(tgt.reshape(steps * fields, 1), (steps * fields, LANES))
    scalars = (info, lat_order, quad_weights)

    saved, pieces = [], None
    for s in range(steps):
        units, slopes, scales, nums, *rest = forward_call(
            plan, s, scalars, state, avail, nums, inv_t, ffw, lt, weights, nb, links, pieces
        )
        saved.append((units, slopes, scales))
        if s < steps - 1:
            pieces = to_members(rest[0])
        if 0 < s < steps - 1:
            state = rest[1]
    counts = to_members(nums)
    before, bstate, loss = None, None, None
    for s in reversed(range(steps)):
        out = backward_call(
            plan, s, chips, scalars, saved[s], avail, tgt, weights, nb, counts, (links, lt, ffw_t, inv), pieces, bstate, before
        )
        if s > 0:
            before = out[:4]
            pieces = to_members(out[4])
            if s == steps - 1:
                loss = out[5]
            else:
                bstate = out[5]
    mine, send = out
    blk = mine.shape[0] // chips
    groups = [[c * chips + n for n in range(chips)] for c in range(copies)]
    exchange = lambda a: lax.all_to_all(a, "lat", split_axis=0, concat_axis=0, tiled=True, axis_index_groups=groups)
    (parts,) = small_call(
        partial(pairs_kernel, chips, group),
        "pairs",
        [jax.ShapeDtypeStruct((chips, blk + 16, LANES), BF16)],
        [mine, across(send), loss],
    )
    reduced, loss = small_call(
        chips_kernel,
        "chips",
        [jax.ShapeDtypeStruct((chips, blk, LANES), BF16), jax.ShapeDtypeStruct((8, LANES), F32)],
        [exchange(parts)],
    )
    part = exchange(reduced).reshape(chips * blk, LANES)
    shapes = [jax.ShapeDtypeStruct((8, LANES), F32)]
    for kind in (F32, F32, F32, BF16):
        shapes += [jax.ShapeDtypeStruct(w.shape, kind) for w in params]
    norm, *results = small_call(
        partial(update_kernel, plan),
        "update",
        shapes,
        [part, across(part), *params, *means, *squares],
        (info,),
        [VM((2, chips * blk, LANES), BF16)],
    )
    return (loss[0, 0], norm[0, 0], *results)


def make_plan(mesh, args):
    state, legendre, _, _, _, available, targets, w_first = args[:8]
    times, waves, _, degrees, chans = state.shape
    _, fields, lats, lons = available.shape
    hidden = w_first.shape[1]
    cores, chips_all = mesh.shape["tm"], mesh.shape["lat"]
    group = GROUP
    chips = group * times
    rows, rest = divmod(lats, 2 * group)
    fits = (
        cores == 2
        and times % cores == 0
        and chips_all == waves == lats
        and waves % chips == 0
        and rest == 0
        and fields == 8
        and lons == chans == degrees * lats
        and waves % 16 == 0
        and degrees % 16 == 0
        and chans % LANES == 0
        and hidden % LANES == 0
        and lons % SUB == 0
    )
    if not fits or legendre.shape != (waves, degrees, lats):
        return None
    steps = targets.shape[1]
    if steps < 3 or steps * rows * lons * (chans + 4 * hidden + LANES) * 4 > SAVED_LIMIT:
        return None
    return Plan(group, rows, waves, degrees, steps, fields, chans, hidden, lons), chips


def solution(mesh):
    in_specs = (
        P("tm", "lat", None, None, None),
        P("lat", None, None),
        P(),
        P(),
        P(),
        P("tm", None, "lat", None),
        P("tm", None, None),
    ) + (P(),) * 12

    def run(*args):
        made = make_plan(mesh, args)
        body = spread_device if made is None else partial(grouped_device, *made)
        return jax.shard_map(body, mesh=mesh, in_specs=in_specs, out_specs=(P(),) * 18, check_vma=False)(*args)

    return run
```

```python
from collections import namedtuple
from functools import partial
import math

import jax
import jax.numpy as jnp
from jax import lax
from jax.experimental import pallas as pl
from jax.experimental.pallas import tpu as pltpu
from jax.sharding import PartitionSpec as P

STEPS = 4


EPS_NORM = 1e-05
STEP_SCALE = 0.5
CLIP_NORM = 1.0
LEARN_RATE = 0.01
BETA_ONE = 0.9
BETA_TWO = 0.95
EPS_ADAM = 1e-08
DECAY = 0.1
HIGH = lax.Precision.HIGHEST


def wave_tables(wave_slots, lon_count):
    product = wave_slots[:, None] * jnp.arange(lon_count, dtype=jnp.int32)[None, :] % lon_count
    phase = product.astype(jnp.float32) * (2.0 * math.pi / lon_count)
    inverse = jnp.stack([jnp.cos(phase), -jnp.sin(phase)], axis=1)
    scale = jnp.where(wave_slots == 0, 1.0, 2.0).astype(jnp.float32) / lon_count
    return (inverse.astype(jnp.bfloat16), (inverse * scale[:, None, None]).astype(jnp.bfloat16))


def layer_spans(chans, hidden):
    gains = [(0, chans), (chans, hidden), (chans + hidden, hidden)]
    biases = [(0, hidden), (hidden, hidden), (2 * hidden, chans)]
    return list(zip(gains, biases))


def norm_gain(x, gain):
    centre = x - jnp.mean(x, axis=-1, keepdims=True)
    return centre * lax.rsqrt(jnp.mean(centre * centre, axis=-1, keepdims=True) + EPS_NORM) * gain


def corrector_forward(x, weights, norm_bias):
    spans = layer_spans(weights[0].shape[0], weights[0].shape[1])
    saved = []
    for k in range(3):
        (gstart, gwidth), (bstart, bwidth) = spans[k]
        h_low = norm_gain(x, 1.0 + norm_bias[0, gstart : gstart + gwidth]).astype(jnp.bfloat16)
        z_val = (
            jnp.dot(h_low, weights[k], preferred_element_type=jnp.float32)
            + norm_bias[1, bstart : bstart + bwidth]
        )
        saved.append((x, h_low, z_val))
        x = jax.nn.gelu(z_val, approximate=False) if k < 2 else z_val
    return (x, saved)


def corrector_backward(grad, saved, weights, norm_bias):
    spans = layer_spans(weights[0].shape[0], weights[0].shape[1])
    weight_grads = [None, None, None]
    gain_parts = [None, None, None]
    bias_parts = [None, None, None]
    for k in (2, 1, 0):
        (gstart, gwidth), (bstart, bwidth) = spans[k]
        x, h_low, z_val = saved[k]
        if k < 2:
            grad = jax.vjp(partial(jax.nn.gelu, approximate=False), z_val)[1](grad)[0]
        grad_low = grad.astype(jnp.bfloat16)
        weight_grads[k] = lax.dot_general(
            h_low, grad_low, (((0,), (0,)), ((), ())), preferred_element_type=jnp.float32
        )
        bias_parts[k] = jnp.sum(grad_low, axis=0, dtype=jnp.float32)
        back_h = lax.dot_general(
            grad_low, weights[k], (((1,), (1,)), ((), ())), preferred_element_type=jnp.float32
        )
        grad, gain_parts[k] = jax.vjp(norm_gain, x, 1.0 + norm_bias[0, gstart : gstart + gwidth])[
            1
        ](back_h)
    vector_grad = jnp.stack([jnp.concatenate(gain_parts), jnp.concatenate(bias_parts)])
    return (grad, (weight_grads[0], weight_grads[1], weight_grads[2], vector_grad))


def adamw(weight, mean, square, grad):
    mean_new = BETA_ONE * mean + (1.0 - BETA_ONE) * grad
    square_new = BETA_TWO * square + (1.0 - BETA_TWO) * grad * grad
    weight_new = weight - LEARN_RATE * (
        mean_new / (jnp.sqrt(square_new) + EPS_ADAM) + DECAY * weight
    )
    return (weight_new, mean_new, square_new)


def spread_device(
    spectral_state,
    legendre,
    wave_slots,
    lat_order,
    quad_weights,
    available,
    targets,
    w_first,
    w_mid,
    w_last,
    norm_bias,
    mean_first,
    mean_mid,
    mean_last,
    mean_bias,
    square_first,
    square_mid,
    square_last,
    square_bias,
):
    tdev, wdev, _, degrees, chans = spectral_state.shape
    fields = available.shape[1]
    rows_dev = available.shape[2]
    lon_count = available.shape[3]
    levels = chans // fields
    lat_index = lax.axis_index("lat")
    slots = lax.dynamic_slice_in_dim(wave_slots, lat_index * wdev, wdev)
    finv, ffw = wave_tables(wave_slots, lon_count)
    keep = (jnp.arange(degrees, dtype=jnp.int32)[None, :] >= slots[:, None]).astype(jnp.bfloat16)
    plg = jnp.take(legendre, lat_order, axis=2) * keep[:, :, None]
    qrow = jnp.take(quad_weights, lat_order)
    qlocal = lax.dynamic_slice_in_dim(qrow, lat_index * rows_dev, rows_dev)
    colw = qlocal[None, None, :, None] * available.astype(jnp.float32)
    den_part = jnp.sum(colw, axis=(2, 3))
    params = (w_first, w_mid, w_last, norm_bias)
    weights = (
        w_first.astype(jnp.bfloat16),
        w_mid.astype(jnp.bfloat16),
        w_last.astype(jnp.bfloat16),
    )

    def legendre_sum(piece):
        return jnp.einsum("mnr,tmprc->tmpnc", plg, piece, preferred_element_type=jnp.float32)

    def fourier_sum(table, piece):
        return jnp.einsum("mpk,tmprc->trkc", table, piece, preferred_element_type=jnp.float32)

    def to_grid(state):
        sums = jnp.einsum(
            "mnr,tmpnc->tmprc", plg, state.astype(jnp.bfloat16), preferred_element_type=jnp.float32
        ).astype(jnp.bfloat16)
        return fourier_sum(
            finv, lax.all_to_all(sums, "lat", split_axis=3, concat_axis=1, tiled=True)
        )

    def column_pass(grid):
        out, saved = corrector_forward(grid.reshape(-1, chans), weights, norm_bias)
        return (out.reshape(grid.shape), saved)

    states = []
    nums = []
    den_total = den_part
    state = spectral_state
    for s in range(STEPS):
        states.append(state)
        grid = to_grid(state)
        out, saved = column_pass(grid)
        pred = grid + STEP_SCALE * out
        num_part = jnp.einsum(
            "tfrk,trkfl->tf",
            colw,
            pred.reshape(tdev, rows_dev, lon_count, fields, levels),
            precision=HIGH,
        )
        num_total, den_total = lax.psum((num_part, den_part), "lat")
        nums.append(num_total)
        tend = (out * qlocal[None, :, None, None]).astype(jnp.bfloat16)
        coeff = jnp.einsum("mpk,trkc->tmprc", ffw, tend, preferred_element_type=jnp.float32).astype(
            jnp.bfloat16
        )
        spec = legendre_sum(lax.all_to_all(coeff, "lat", split_axis=1, concat_axis=3, tiled=True))
        state = state + STEP_SCALE * spec
    num_all = jnp.stack(nums)
    bias = num_all / (levels * den_total[None]) - jnp.moveaxis(targets, 1, 0)
    loss = lax.psum(jnp.sum(bias * bias) / STEPS, "tm")
    grad_bias = 2.0 * bias / (STEPS * levels * den_total[None])
    totals = tuple((jnp.zeros_like(p) for p in params))
    back_state = None
    for s in reversed(range(STEPS)):
        grid = to_grid(states[s])
        out, saved = column_pass(grid)
        scaled = jnp.moveaxis(colw * grad_bias[s][:, :, None, None], 1, 3)
        back_pred = jnp.broadcast_to(scaled[..., None], scaled.shape + (levels,)).reshape(
            grid.shape
        )
        back_out = STEP_SCALE * back_pred
        if back_state is not None:
            back_spec = (STEP_SCALE * back_state).astype(jnp.bfloat16)
            back_coeff = jnp.einsum(
                "mnr,tmpnc->tmprc", plg, back_spec, preferred_element_type=jnp.float32
            ).astype(jnp.bfloat16)
            back_tend = fourier_sum(
                ffw, lax.all_to_all(back_coeff, "lat", split_axis=3, concat_axis=1, tiled=True)
            )
            back_out = back_out + qlocal[None, :, None, None] * back_tend
        back_in, grads = corrector_backward(back_out.reshape(-1, chans), saved, weights, norm_bias)
        totals = tuple((a + b for a, b in zip(totals, grads)))
        if s > 0:
            back_grid = (back_pred + back_in.reshape(grid.shape)).astype(jnp.bfloat16)
            back_sums = jnp.einsum(
                "mpk,trkc->tmprc", finv, back_grid, preferred_element_type=jnp.float32
            ).astype(jnp.bfloat16)
            back_low = legendre_sum(
                lax.all_to_all(back_sums, "lat", split_axis=1, concat_axis=3, tiled=True)
            )
            back_state = back_low if back_state is None else back_state + back_low
    means = (mean_first, mean_mid, mean_last, mean_bias)
    squares = (square_first, square_mid, square_last, square_bias)
    grads = lax.psum(totals, ("tm", "lat"))
    grad_norm = jnp.sqrt(sum((jnp.sum(g * g) for g in grads)))
    factor = CLIP_NORM / jnp.maximum(grad_norm, CLIP_NORM)
    results = [adamw(w, a, b, g * factor) for w, a, b, g in zip(params, means, squares, grads)]
    masters = [r[0] for r in results]
    new_means = [r[1] for r in results]
    new_squares = [r[2] for r in results]
    halves = [w.astype(jnp.bfloat16) for w in masters]
    return (
        loss,
        grad_norm,
        masters[0],
        masters[1],
        masters[2],
        masters[3],
        new_means[0],
        new_means[1],
        new_means[2],
        new_means[3],
        new_squares[0],
        new_squares[1],
        new_squares[2],
        new_squares[3],
        halves[0],
        halves[1],
        halves[2],
        halves[3],
    )


F32 = jnp.float32
BF16 = jnp.bfloat16
VM = pltpu.VMEM
LANES = 128
GROUP = 2
SUB = 256
ROWS_BLOCK = 2
VMEM_LIMIT = 10 << 20
SAVED_LIMIT = 96 << 20


Plan = namedtuple("Plan", ("group", "rows", "waves", "degrees", "steps", "fields", "chans", "hidden", "lons"))


def dot(a, b, dims=((1,), (0,))):
    return lax.dot_general(a, b, (dims, ((), ())), preferred_element_type=F32)


def norm_unit(x, eps):
    centre = x - jnp.mean(x, axis=-1, keepdims=True)
    scale = lax.rsqrt(jnp.mean(centre * centre, axis=-1, keepdims=True) + eps)
    return centre * scale, scale


def gelu_twice(z):
    arg = z * math.sqrt(0.5)
    cdf = 1.0 + lax.erf(arg)
    pdf = jnp.exp2(arg * arg * -math.log2(math.e))
    return z * cdf, cdf + (z * math.sqrt(2.0 / math.pi)) * pdf


def whole(a):
    return pl.BlockSpec(a.shape, lambda *_: (0,) * len(a.shape))


def fold(v):
    return jnp.sum(v.reshape(v.shape[0] // 8, 8, v.shape[1]), axis=0)


def field_mask(fields, chans):
    lane = lax.broadcasted_iota(jnp.int32, (fields, chans), 1)
    row = lax.broadcasted_iota(jnp.int32, (fields, chans), 0) * (chans // fields)
    return (lane >= row) & (lane < row + chans // fields)


def splits(nb, chans, hidden):
    gains = [1.0 + nb[0:1, a:b] for a, b in ((0, chans), (chans, chans + hidden), (chans + hidden, chans + 2 * hidden))]
    biases = [nb[1:2, a:b] for a, b in ((0, hidden), (hidden, 2 * hidden), (2 * hidden, 2 * hidden + chans))]
    return gains, biases


def pair_rows(plan):
    return ROWS_BLOCK if plan.rows % ROWS_BLOCK == 0 else 1


def row_weight(plan, info, order, quad, row):
    return quad[order[(info[1] * 2 + info[0]) * plan.rows + row]]


def prepare_kernel(
    plan, info, slots, order, quad, got, got_o, inv, ffw, wanted, state, links, lt, avail, nums, table, ffw_t, tgt
):
    group, rows, waves, degrees, steps, fields, chans, _, _ = plan
    members = 2 * group
    core, member = info[0], info[1]
    span = waves * degrees
    mine = rows * waves
    half = fields // 2
    lats = rows * members
    leg = jnp.zeros((waves, chans), F32)
    row_of = lax.broadcasted_iota(jnp.int32, (waves, chans), 0)
    pick = lax.broadcasted_iota(jnp.int32, (8, chans), 0) == half
    for j in range(waves):
        at = pl.ds(j * degrees, degrees)
        for ref, p in ((got, core), (got_o, 1 - core)):
            hi = ref[j, 0:degrees, :].astype(F32)
            state[p, at, :] = hi + ref[j, degrees : 2 * degrees, :].astype(F32)
        tail = got[j, 2 * degrees : 2 * degrees + 8, :].astype(F32)
        line = jnp.sum(jnp.where(pick, tail, 0.0), axis=0, keepdims=True)
        leg = jnp.where(row_of == j, line, leg)
    iota = lambda d, s: lax.broadcasted_iota(jnp.int32, s, d)
    shape = (span, span)
    r0, r1 = iota(0, shape), iota(1, shape)
    expand = (iota(0, (span, waves)) // degrees == iota(1, (span, waves))).astype(F32).astype(BF16)
    rep = dot(expand, leg.astype(BF16))
    rep = jnp.where(r1 // lats == r0 % degrees, rep, 0.0).astype(BF16)
    lat_lane = jnp.zeros((8, span), jnp.int32)
    lane = iota(1, (8, span)) // waves
    for r in range(lats):
        lat_lane = jnp.where(lane == r, order[r], lat_lane)
    wave_row = jnp.zeros(shape, jnp.int32)
    for j in range(waves):
        wave_row = jnp.where(r0 // degrees == j, slots[j], wave_row)
    choose = (r0 % lats == lat_lane[0:1, :]).astype(F32).astype(BF16)
    plg = dot(rep, choose)
    plg = jnp.where((r0 // degrees == r1 % waves) & (r0 % degrees >= wave_row), plg, 0.0)
    flip = plg.T
    spot = member * 2 + core
    for role in range(members):
        other = (member ^ (role & (group - 1))) * 2 + (core ^ (role // group))
        piece = jnp.zeros((span, mine), F32)
        for w in range(members):
            piece = jnp.where(other == w, plg[:, w * mine : (w + 1) * mine], piece)
        links[role] = piece.astype(BF16)
    own = jnp.zeros((mine, span), F32)
    for w in range(members):
        own = jnp.where(spot == w, flip[w * mine : (w + 1) * mine, :], own)
    lt[...] = own.astype(BF16)
    den = jnp.zeros((fields, chans), F32)
    for r in range(rows):
        src = spot * rows + r
        a = got[src, 2 * degrees : 2 * degrees + 8, :].astype(F32)
        b = got_o[src, 2 * degrees : 2 * degrees + 8, :].astype(F32)
        first = jnp.where(core == 0, a, b)[0:half]
        second = jnp.where(core == 0, b, a)[0:half]
        both = jnp.concatenate([first, second], axis=0)
        avail[r] = both.astype(BF16)
        den += quad[order[src]] * both
    nums[...] = jnp.zeros_like(nums)
    nums[steps * fields :, :] = jnp.broadcast_to(jnp.sum(den, axis=1, keepdims=True), (fields, nums.shape[1]))
    table[...] = inv[...].T.astype(BF16)
    ffw_t[...] = ffw[...].T.astype(BF16)
    tgt[...] = wanted[...]


def prepare_call(plan, info, slots, order, quad, got, got_o, inv, ffw, wanted):
    group, rows, waves, degrees, steps, fields, chans, _, lons = plan
    span, mine = waves * degrees, rows * waves
    ins = [got, got_o, inv, ffw, wanted]
    shapes = [
        jax.ShapeDtypeStruct((2, span, chans), F32),
        jax.ShapeDtypeStruct((2 * group, span, mine), BF16),
        jax.ShapeDtypeStruct((mine, span), BF16),
        jax.ShapeDtypeStruct((rows, fields, lons), BF16),
        jax.ShapeDtypeStruct(((steps + 1) * fields, LANES), F32),
        jax.ShapeDtypeStruct((lons, 2 * waves), BF16),
        jax.ShapeDtypeStruct((lons, 2 * waves), BF16),
        jax.ShapeDtypeStruct(wanted.shape, F32),
    ]
    return pl.pallas_call(
        partial(prepare_kernel, plan),
        out_shape=shapes,
        grid_spec=pltpu.PrefetchScalarGridSpec(
            num_scalar_prefetch=4,
            grid=(1,),
            in_specs=[whole(a) for a in ins],
            out_specs=[whole(a) for a in shapes],
        ),
        compiler_params=kernel_params(),
        name="prepare",
    )(info, slots, order, quad, *ins)


def kernel_params():
    return pltpu.CompilerParams(vmem_limit_bytes=VMEM_LIMIT)


def forward_kernel(plan, step, info, order, quad, *refs):
    group, rows, waves, _, steps, fields, chans, hidden, lons = plan
    first, last = step == 0, step == steps - 1
    rows_blk = pair_rows(plan)
    refs = list(refs)
    take = lambda: refs.pop(0)
    state, avail, nums_in, table, ffw, lt, w1, w2, w3, nb = [take() for _ in range(10)]
    if not first:
        links = take()
        pieces = [take() for _ in range(2 * group)]
    units, slopes, scales, nums = [take() for _ in range(4)]
    if not last:
        y_out = take()
    if not first and not last:
        state_out = take()
    sums, num_acc = take(), take()
    i = pl.program_id(0)

    @pl.when(i == 0)
    def _():
        for p in range(2):
            st = state[p]
            if not first:
                spec = dot(links[0], pieces[0][p])
                for role in range(1, 2 * group):
                    spec = spec + dot(links[role], pieces[role][p])
                st = st + STEP_SCALE * spec
                if not last:
                    state_out[p] = st
            sums[p] = dot(lt[...], st.astype(BF16)).astype(BF16)
        num_acc[...] = jnp.zeros_like(num_acc)

    gains, biases = splits(nb, chans, hidden)
    for rr in range(rows_blk):
        row = i * rows_blk + rr
        at = pl.ds(pl.multiple_of(row * waves, waves), waves)
        rhs = jnp.concatenate([sums[0, at, :], sums[1, at, :]], axis=0)
        q = row_weight(plan, info, order, quad, row)
        highs, lows, tends = [], [], []
        for c0 in range(0, lons, SUB):
            cs = pl.ds(pl.multiple_of(row * lons + c0, SUB), SUB)
            grid = dot(table[c0 : c0 + SUB, :], rhs)
            u1, s1 = norm_unit(grid, EPS_NORM)
            units[cs, 0:chans] = u1
            scales[cs, :] = jnp.broadcast_to(s1, (SUB, LANES))
            a1, d1 = gelu_twice(dot((u1 * gains[0]).astype(BF16), w1[...]) + biases[0])
            u2, s2 = norm_unit(a1, 4.0 * EPS_NORM)
            units[cs, chans : chans + hidden] = u2
            slopes[cs, 0:hidden] = d1 * s2
            a2, d2 = gelu_twice(dot((u2 * gains[1]).astype(BF16), w2[...]) + biases[1])
            u3, s3 = norm_unit(a2, 4.0 * EPS_NORM)
            units[cs, chans + hidden :] = u3
            slopes[cs, hidden:] = d2 * s3
            out = dot((u3 * gains[2]).astype(BF16), w3[...]) + biases[2]
            pred = grid + STEP_SCALE * out
            hi = pred.astype(BF16)
            highs.append(hi)
            lows.append((pred - hi.astype(F32)).astype(BF16))
            tends.append((out * q).astype(BF16))
        weigh = lambda parts: dot(avail[rr], jnp.concatenate(parts, axis=0))
        num_acc[...] += q * (weigh(highs) + weigh(lows))
        if not last:
            coeff = dot(ffw[...], jnp.concatenate(tends, axis=0)).astype(BF16)
            y_out[0, rr * waves : (rr + 1) * waves, :] = coeff[:waves]
            y_out[1, rr * waves : (rr + 1) * waves, :] = coeff[waves:]

    @pl.when(i == pl.num_programs(0) - 1)
    def _():
        kept = jnp.where(field_mask(fields, chans), num_acc[...], 0.0)
        nums[...] = nums_in[...]
        nums[step * fields : (step + 1) * fields, :] = jnp.broadcast_to(
            jnp.sum(kept, axis=1, keepdims=True), (fields, LANES)
        )


def forward_call(plan, step, scalars, state, avail, nums, table, ffw, lt, weights, nb, links, pieces):
    group, rows, waves, _, steps, fields, chans, hidden, lons = plan
    first, last = step == 0, step == steps - 1
    rows_blk = pair_rows(plan)
    cols, blk = rows * lons, rows_blk * lons
    ins = [state, avail, nums, table, ffw, lt, *weights, nb]
    if not first:
        ins += [links, *pieces]
    specs = [whole(a) for a in ins]
    specs[1] = pl.BlockSpec((rows_blk, fields, lons), lambda i, *_: (i, 0, 0))
    shapes, ospecs = [], []
    for width in (chans + 2 * hidden, 2 * hidden, LANES):
        shapes.append(VM((cols, width), F32))
        ospecs.append(pl.BlockSpec(memory_space=VM))
    shapes.append(jax.ShapeDtypeStruct(nums.shape, F32))
    ospecs.append(whole(nums))
    if not last:
        shapes.append(jax.ShapeDtypeStruct((2, rows * waves, chans), BF16))
        ospecs.append(pl.BlockSpec((2, rows_blk * waves, chans), lambda i, *_: (0, i, 0)))
    if not first and not last:
        shapes.append(jax.ShapeDtypeStruct(state.shape, F32))
        ospecs.append(whole(state))
    return pl.pallas_call(
        partial(forward_kernel, plan, step),
        out_shape=shapes,
        grid_spec=pltpu.PrefetchScalarGridSpec(
            num_scalar_prefetch=3,
            grid=(rows // rows_blk,),
            in_specs=specs,
            out_specs=ospecs,
            scratch_shapes=[VM((2, rows * waves, chans), BF16), VM((fields, chans), F32)],
        ),
        compiler_params=kernel_params(),
        name=f"forward_{step}",
    )(*scalars, *ins)


def packed_parts(plan):
    parts, at = [], 0
    sizes = ((plan.chans, plan.hidden), (plan.hidden, plan.hidden), (plan.hidden, plan.chans))
    for which, (rows, cols) in enumerate(sizes):
        for tile in range(cols // LANES):
            parts.append((which, tile, at, rows))
            at += rows
    return parts, at


def packed_block(plan, chips):
    vectors = 2 * (plan.chans + 2 * plan.hidden) // LANES
    need = packed_parts(plan)[1] + vectors
    return -(-need // (2 * chips * 16)) * 16


def both_halves(at, rows, half):
    out, done = [], 0
    while done < rows:
        h = (at + done) // half
        n = min(rows - done, (h + 1) * half - at - done)
        out.append((h, at + done - h * half, done, n))
        done += n
    return out


def backward_kernel(plan, step, info, order, quad, *refs):
    group, rows, waves, _, steps, fields, chans, hidden, lons = plan
    first, last = step == steps - 1, step == 0
    fresh = step == steps - 2
    rows_blk = pair_rows(plan)
    members = 2 * group
    levels = chans // fields
    refs = list(refs)
    take = lambda: refs.pop(0)
    units, slopes, scales, avail, tgt, w1, w2, w3, nb = [take() for _ in range(9)]
    counts = [take() for _ in range(members)]
    if not first:
        links, lt, ffw_t = [take() for _ in range(3)]
        pieces = [take() for _ in range(members)]
        if not fresh:
            bstate = take()
        before = [take() for _ in range(4)]
    if not last:
        inv = take()
        grads = [take() for _ in range(4)]
        b_out = take()
        if not first:
            bstate_out = take()
    else:
        mine, send = take(), take()
    if first:
        loss = take()
    coef, gmask = take(), take()
    if last:
        grads = [take() for _ in range(4)]
        packed = take()
    d1, d2, d3, dv = grads
    i = pl.program_id(0)

    @pl.when(i == 0)
    def _():
        def total(s):
            acc = [c[s * fields : (s + 1) * fields, :] for c in counts]
            while len(acc) > 1:
                acc = [a + b for a, b in zip(acc[::2], acc[1::2])]
            return acc[0]

        den = total(steps)
        bias_of = lambda s: total(s) / (levels * den) - tgt[s * fields : (s + 1) * fields, :]
        gb = 2.0 * bias_of(step) / (steps * levels * den)
        gb = jnp.concatenate([gb] * (chans // LANES), axis=1)
        gb = jnp.where(field_mask(fields, chans), gb, 0.0)
        hi = gb.astype(BF16).astype(F32)
        gmask[...] = jnp.concatenate([hi, gb - hi], axis=0).astype(BF16)
        if first:
            sq = bias_of(0) * bias_of(0)
            for s in range(1, steps):
                sq = sq + bias_of(s) * bias_of(s)
            loss[...] = jnp.broadcast_to(jnp.sum(sq, axis=0, keepdims=True) / steps, loss.shape)
            for d in grads:
                d[...] = jnp.zeros_like(d)
        else:
            for d, b in zip(grads, before):
                d[...] = b[...]
            for p in range(2):
                st = dot(links[0], pieces[0][p])
                for role in range(1, members):
                    st = st + dot(links[role], pieces[role][p])
                if not fresh:
                    st = bstate[p] + st
                if not last:
                    bstate_out[p] = st
                coef[p] = dot(lt[...], (STEP_SCALE * st).astype(BF16)).astype(BF16)

    gains, _ = splits(nb, chans, hidden)

    def norm_back(back, gain, unit):
        prod = back * unit
        low = back * gain
        m1 = jnp.mean(low, axis=-1, keepdims=True)
        m2 = jnp.mean(prod * gain, axis=-1, keepdims=True)
        return prod, low - m1 - unit * m2

    for rr in range(rows_blk):
        row = i * rows_blk + rr
        q = row_weight(plan, info, order, quad, row)
        av2 = jnp.concatenate([avail[rr].astype(F32)] * 2, axis=0).astype(BF16)
        if not first:
            at = pl.ds(pl.multiple_of(row * waves, waves), waves)
            rhs = jnp.concatenate([coef[0, at, :], coef[1, at, :]], axis=0)
        grids = []
        for c0 in range(0, lons, SUB):
            cs = pl.ds(pl.multiple_of(row * lons + c0, SUB), SUB)
            dpred = q * dot(av2[:, c0 : c0 + SUB], gmask[...], ((0,), (0,)))
            dout = STEP_SCALE * dpred
            if not first:
                dout = dout + q * dot(ffw_t[c0 : c0 + SUB, :], rhs)
            dz = dout.astype(BF16)
            u = units[cs, chans + hidden :]
            d3[...] += dot((u * gains[2]).astype(BF16), dz, ((0,), (0,)))
            dv[8:16, 2 * hidden :] += fold(dz.astype(F32))
            prod, dx = norm_back(dot(dz, w3[...], ((1,), (1,))), gains[2], u)
            dv[0:8, chans + hidden :] += fold(prod)
            dz = (dx * slopes[cs, hidden:]).astype(BF16)
            u = units[cs, chans : chans + hidden]
            d2[...] += dot((u * gains[1]).astype(BF16), dz, ((0,), (0,)))
            dv[8:16, hidden : 2 * hidden] += fold(dz.astype(F32))
            prod, dx = norm_back(dot(dz, w2[...], ((1,), (1,))), gains[1], u)
            dv[0:8, chans : chans + hidden] += fold(prod)
            dz = (dx * slopes[cs, 0:hidden]).astype(BF16)
            u = units[cs, 0:chans]
            d1[...] += dot((u * gains[0]).astype(BF16), dz, ((0,), (0,)))
            dv[8:16, 0:hidden] += fold(dz.astype(F32))
            back = dot(dz, w1[...], ((1,), (1,)))
            if last:
                dv[0:8, 0:chans] += fold(back * u)
            else:
                prod, dx = norm_back(back, gains[0], u)
                dv[0:8, 0:chans] += fold(prod)
                grids.append((dpred + dx * scales[cs, 0:1]).astype(BF16))
        if not last:
            coeff = dot(inv[...], jnp.concatenate(grids, axis=0)).astype(BF16)
            b_out[0, rr * waves : (rr + 1) * waves, :] = coeff[:waves]
            b_out[1, rr * waves : (rr + 1) * waves, :] = coeff[waves:]

    if last:

        @pl.when(i == pl.num_programs(0) - 1)
        def _():
            half = packed.shape[1]
            parts, at = packed_parts(plan)
            for which, tile, start, count in parts:
                for h, dst, src, n in both_halves(start, count, half):
                    packed[h, dst : dst + n, :] = grads[which][src : src + n, tile * LANES : (tile + 1) * LANES]
            for v in range(2):
                line = jnp.sum(dv[v * 8 : v * 8 + 8, :], axis=0, keepdims=True)
                for tile in range(line.shape[1] // LANES):
                    row = at - half
                    packed[1, row : row + 1, :] = line[:, tile * LANES : (tile + 1) * LANES]
                    at += 1
            tail = at - half
            packed[1, tail:, :] = jnp.zeros((half - tail, LANES), F32)
            mine[...] = packed[info[0]]
            send[...] = packed[1 - info[0]]


def backward_call(plan, step, chips, scalars, saved, avail, tgt, weights, nb, counts, tables, pieces, bstate, before):
    group, rows, waves, degrees, steps, fields, chans, hidden, lons = plan
    first, last = step == steps - 1, step == 0
    rows_blk = pair_rows(plan)
    blk = rows_blk * lons
    links, lt, ffw_t, inv = tables
    ins = [*saved, avail, tgt, *weights, nb, *counts]
    if not first:
        ins += [links, lt, ffw_t, *pieces]
        if step != steps - 2:
            ins.append(bstate)
        ins += before
    if not last:
        ins.append(inv)
    specs = [whole(a) for a in ins]
    for n in range(3):
        specs[n] = pl.BlockSpec(memory_space=VM)
    specs[3] = pl.BlockSpec((rows_blk, fields, lons), lambda i, *_: (i, 0, 0))
    sums = [((chans, hidden), F32), ((hidden, hidden), F32), ((hidden, chans), F32), ((16, chans + 2 * hidden), F32)]
    scratch = [VM((2, rows * waves, chans), BF16), VM((2 * fields, chans), BF16)]
    if last:
        half = chips * packed_block(plan, chips)
        scratch += [VM(*s) for s in sums] + [VM((2, half, LANES), F32)]
        shapes = [jax.ShapeDtypeStruct((half, LANES), F32)] * 2
        ospecs = [whole(a) for a in shapes]
    else:
        shapes = [jax.ShapeDtypeStruct(*s) for s in sums]
        ospecs = [whole(a) for a in shapes]
        shapes.append(jax.ShapeDtypeStruct((2, rows * waves, chans), BF16))
        ospecs.append(pl.BlockSpec((2, rows_blk * waves, chans), lambda i, *_: (0, i, 0)))
        if not first:
            shapes.append(jax.ShapeDtypeStruct((2, waves * degrees, chans), F32))
            ospecs.append(whole(shapes[-1]))
    if first:
        shapes.append(jax.ShapeDtypeStruct((8, LANES), F32))
        ospecs.append(whole(shapes[-1]))
    return pl.pallas_call(
        partial(backward_kernel, plan, step),
        out_shape=shapes,
        grid_spec=pltpu.PrefetchScalarGridSpec(
            num_scalar_prefetch=3,
            grid=(rows // rows_blk,),
            in_specs=specs,
            out_specs=ospecs,
            scratch_shapes=scratch,
        ),
        compiler_params=kernel_params(),
        name=f"backward_{step}",
    )(*scalars, *ins)


def pairs_kernel(chips, group, mine, got, loss, out):
    blk = mine.shape[0] // chips
    share = loss[...] * (1.0 / group)
    row = lax.broadcasted_iota(jnp.int32, share.shape, 0)
    high = share.astype(BF16).astype(F32)
    rest = share - high
    mid = rest.astype(BF16).astype(F32)
    lines = jnp.where(row == 0, high, jnp.where(row == 1, mid, jnp.where(row == 2, rest - mid, 0.0)))
    lines = jnp.concatenate([lines, jnp.zeros_like(lines)], axis=0).astype(BF16)
    for c in range(chips):
        at = slice(c * blk, (c + 1) * blk)
        out[c, 0:blk, :] = (mine[at, :] + got[at, :]).astype(BF16)
        out[c, blk:, :] = lines


def chips_kernel(got, out, loss):
    chips, blk = out.shape[0], out.shape[1]
    total = got[0].astype(F32)
    for c in range(1, chips):
        total = total + got[c].astype(F32)
    low = total[0:blk].astype(BF16)
    for c in range(chips):
        out[c] = low
    loss[...] = jnp.broadcast_to(jnp.sum(total[blk:], axis=0, keepdims=True), loss.shape)


def update_kernel(plan, info, part, part_o, *refs):
    params, means, squares = refs[0:4], refs[4:8], refs[8:12]
    norm = refs[12]
    masters, new_means, new_squares, halves = refs[13:17], refs[17:21], refs[21:25], refs[25:29]
    packed = refs[29]
    packed[info[0]] = part[...]
    packed[1 - info[0]] = part_o[...]
    half = packed.shape[1]
    acc = jnp.zeros((16, LANES), F32)
    for h in range(2):
        g = packed[h].astype(F32)
        acc = acc + jnp.sum((g * g).reshape(half // 16, 16, LANES), axis=0)
    total = jnp.sum(jnp.sum(acc, axis=0, keepdims=True), axis=1, keepdims=True)
    root = jnp.sqrt(jnp.broadcast_to(total, (8, LANES)))
    norm[...] = root
    factor = (CLIP_NORM / jnp.maximum(root, CLIP_NORM))[0:1, :]

    def apply(which, rs, cs, g):
        w, a, b = adamw(params[which][rs, cs], means[which][rs, cs], squares[which][rs, cs], g * factor)
        masters[which][rs, cs] = w
        new_means[which][rs, cs] = a
        new_squares[which][rs, cs] = b
        halves[which][rs, cs] = w.astype(BF16)

    parts, at = packed_parts(plan)
    for which, tile, start, count in parts:
        for h, src, dst, n in both_halves(start, count, half):
            apply(which, slice(dst, dst + n), slice(tile * LANES, (tile + 1) * LANES), packed[h, src : src + n, :].astype(F32))
    tiles = (plan.chans + 2 * plan.hidden) // LANES
    rows = packed[1, at - half : at - half + 2 * tiles, :].astype(F32)
    for tile in range(tiles):
        g = jnp.concatenate([rows[tile : tile + 1], rows[tiles + tile : tiles + tile + 1]], axis=0)
        apply(3, slice(0, 2), slice(tile * LANES, (tile + 1) * LANES), g)


def small_call(kernel, name, shapes, ins, scalars=(), scratch=()):
    return pl.pallas_call(
        kernel,
        out_shape=shapes,
        grid_spec=pltpu.PrefetchScalarGridSpec(
            num_scalar_prefetch=len(scalars),
            grid=(1,),
            in_specs=[whole(a) for a in ins],
            out_specs=[whole(a) for a in shapes],
            scratch_shapes=list(scratch),
        ),
        compiler_params=kernel_params(),
        name=name,
    )(*scalars, *ins)


def grouped_device(
    plan,
    chips,
    spectral_state,
    legendre,
    wave_slots,
    lat_order,
    quad_weights,
    available,
    targets,
    *flat,
):
    group, rows, waves, degrees, steps, fields, chans, hidden, lons = plan
    params, means, squares = flat[0:4], flat[4:8], flat[8:12]
    weights = [w.astype(BF16) for w in params[:3]]
    nb = params[3]
    tdev = spectral_state.shape[0]
    copies = waves // chips
    core = lax.axis_index("tm")
    chip = lax.axis_index("lat")
    member = chip % group
    info = jnp.stack([core, member]).astype(jnp.int32)
    swap = [(0, 1), (1, 0)]
    across = lambda a: lax.ppermute(a, "tm", swap)

    def to_members(a):
        out = [a]
        bit = 1
        while bit < group:
            out += [lax.ppermute(v, "lat", [(n, n ^ bit) for n in range(waves)]) for v in out]
            bit *= 2
        return out + [across(v) for v in out]

    half = fields // 2
    pad = -(2 * degrees + half + 1) % 8
    high = spectral_state[:, 0].astype(BF16)
    low = (spectral_state[:, 0] - high.astype(F32)).astype(BF16)
    seen = available[:, :, 0].reshape(tdev, 2, half, lons).astype(BF16)
    leg = jnp.broadcast_to(legendre.reshape(1, 1, 1, chans), (tdev, 2, 1, chans))
    pack = jnp.concatenate([high, low, seen, leg, jnp.zeros((tdev, 2, pad, chans), BF16)], axis=2)
    keep = lax.dynamic_index_in_dim(pack, core, axis=1, keepdims=False)
    other = across(lax.dynamic_index_in_dim(pack, 1 - core, axis=1, keepdims=False))
    times = jnp.concatenate([jnp.where(core == 0, keep, other), jnp.where(core == 0, other, keep)], axis=0)
    spread = jnp.broadcast_to(times[None, :, None], (copies, 2 * tdev, group, *times.shape[1:]))
    got = lax.all_to_all(spread.reshape(waves, *times.shape[1:]), "lat", split_axis=0, concat_axis=0, tiled=True)
    got_o = across(got)

    def table(scaled):
        product = wave_slots[:, None] * jnp.arange(lons, dtype=jnp.int32)[None, :] % lons
        phase = product.astype(F32) * (2.0 * math.pi / lons)
        inverse = jnp.concatenate([jnp.cos(phase), -jnp.sin(phase)], axis=0)
        if not scaled:
            return inverse
        scale = jnp.where(wave_slots == 0, 1.0, 2.0).astype(F32) / lons
        return inverse * jnp.concatenate([scale, scale])[:, None]

    inv32, ffw32 = table(False), table(True)
    inv, ffw = inv32.astype(BF16), ffw32.astype(BF16)
    theirs = across(targets)
    tgt_all = jnp.concatenate([jnp.where(core == 0, targets, theirs), jnp.where(core == 0, theirs, targets)], axis=0)
    tgt = lax.dynamic_index_in_dim(tgt_all, (chip // group) % (2 * tdev), axis=0, keepdims=False)
    tgt = jnp.broadcast_to(tgt.reshape(steps * fields, 1), (steps * fields, LANES))
    state, links, lt, avail, nums, inv_t, ffw_t, tgt = prepare_call(
        plan, info, wave_slots, lat_order, quad_weights, got, got_o, inv32, ffw32, tgt
    )
    scalars = (info, lat_order, quad_weights)

    saved, pieces = [], None
    for s in range(steps):
        units, slopes, scales, nums, *rest = forward_call(
            plan, s, scalars, state, avail, nums, inv_t, ffw, lt, weights, nb, links, pieces
        )
        saved.append((units, slopes, scales))
        if s < steps - 1:
            pieces = to_members(rest[0])
        if 0 < s < steps - 1:
            state = rest[1]
    counts = to_members(nums)
    before, bstate, loss = None, None, None
    for s in reversed(range(steps)):
        out = backward_call(
            plan, s, chips, scalars, saved[s], avail, tgt, weights, nb, counts, (links, lt, ffw_t, inv), pieces, bstate, before
        )
        if s > 0:
            before = out[:4]
            pieces = to_members(out[4])
            if s == steps - 1:
                loss = out[5]
            else:
                bstate = out[5]
    mine, send = out
    blk = mine.shape[0] // chips
    groups = [[c * chips + n for n in range(chips)] for c in range(copies)]
    exchange = lambda a: lax.all_to_all(a, "lat", split_axis=0, concat_axis=0, tiled=True, axis_index_groups=groups)
    (parts,) = small_call(
        partial(pairs_kernel, chips, group),
        "pairs",
        [jax.ShapeDtypeStruct((chips, blk + 16, LANES), BF16)],
        [mine, across(send), loss],
    )
    reduced, loss = small_call(
        chips_kernel,
        "chips",
        [jax.ShapeDtypeStruct((chips, blk, LANES), BF16), jax.ShapeDtypeStruct((8, LANES), F32)],
        [exchange(parts)],
    )
    part = exchange(reduced).reshape(chips * blk, LANES)
    shapes = [jax.ShapeDtypeStruct((8, LANES), F32)]
    for kind in (F32, F32, F32, BF16):
        shapes += [jax.ShapeDtypeStruct(w.shape, kind) for w in params]
    norm, *results = small_call(
        partial(update_kernel, plan),
        "update",
        shapes,
        [part, across(part), *params, *means, *squares],
        (info,),
        [VM((2, chips * blk, LANES), BF16)],
    )
    return (loss[0, 0], norm[0, 0], *results)


def make_plan(mesh, args):
    state, legendre, _, _, _, available, targets, w_first = args[:8]
    times, waves, _, degrees, chans = state.shape
    _, fields, lats, lons = available.shape
    hidden = w_first.shape[1]
    cores, chips_all = mesh.shape["tm"], mesh.shape["lat"]
    group = GROUP
    chips = group * times
    rows, rest = divmod(lats, 2 * group)
    fits = (
        cores == 2
        and times % cores == 0
        and chips_all == waves == lats
        and waves % chips == 0
        and rest == 0
        and fields == 8
        and lons == chans == degrees * lats
        and waves % 16 == 0
        and degrees % 16 == 0
        and chans % LANES == 0
        and hidden % LANES == 0
        and lons % SUB == 0
    )
    if not fits or legendre.shape != (waves, degrees, lats):
        return None
    steps = targets.shape[1]
    if steps < 3 or steps * rows * lons * (chans + 4 * hidden + LANES) * 4 > SAVED_LIMIT:
        return None
    return Plan(group, rows, waves, degrees, steps, fields, chans, hidden, lons), chips


def solution(mesh):
    in_specs = (
        P("tm", "lat", None, None, None),
        P("lat", None, None),
        P(),
        P(),
        P(),
        P("tm", None, "lat", None),
        P("tm", None, None),
    ) + (P(),) * 12

    def run(*args):
        made = make_plan(mesh, args)
        body = spread_device if made is None else partial(grouped_device, *made)
        return jax.shard_map(body, mesh=mesh, in_specs=in_specs, out_specs=(P(),) * 18, check_vma=False)(*args)

    return run
```

```python
from collections import namedtuple
from functools import partial
import math

import jax
import jax.numpy as jnp
from jax import lax
from jax.experimental import pallas as pl
from jax.experimental.pallas import tpu as pltpu
from jax.sharding import PartitionSpec as P

STEPS = 4


EPS_NORM = 1e-05
STEP_SCALE = 0.5
CLIP_NORM = 1.0
LEARN_RATE = 0.01
BETA_ONE = 0.9
BETA_TWO = 0.95
EPS_ADAM = 1e-08
DECAY = 0.1
HIGH = lax.Precision.HIGHEST


def wave_tables(wave_slots, lon_count):
    product = wave_slots[:, None] * jnp.arange(lon_count, dtype=jnp.int32)[None, :] % lon_count
    phase = product.astype(jnp.float32) * (2.0 * math.pi / lon_count)
    inverse = jnp.stack([jnp.cos(phase), -jnp.sin(phase)], axis=1)
    scale = jnp.where(wave_slots == 0, 1.0, 2.0).astype(jnp.float32) / lon_count
    return (inverse.astype(jnp.bfloat16), (inverse * scale[:, None, None]).astype(jnp.bfloat16))


def layer_spans(chans, hidden):
    gains = [(0, chans), (chans, hidden), (chans + hidden, hidden)]
    biases = [(0, hidden), (hidden, hidden), (2 * hidden, chans)]
    return list(zip(gains, biases))


def norm_gain(x, gain):
    centre = x - jnp.mean(x, axis=-1, keepdims=True)
    return centre * lax.rsqrt(jnp.mean(centre * centre, axis=-1, keepdims=True) + EPS_NORM) * gain


def corrector_forward(x, weights, norm_bias):
    spans = layer_spans(weights[0].shape[0], weights[0].shape[1])
    saved = []
    for k in range(3):
        (gstart, gwidth), (bstart, bwidth) = spans[k]
        h_low = norm_gain(x, 1.0 + norm_bias[0, gstart : gstart + gwidth]).astype(jnp.bfloat16)
        z_val = (
            jnp.dot(h_low, weights[k], preferred_element_type=jnp.float32)
            + norm_bias[1, bstart : bstart + bwidth]
        )
        saved.append((x, h_low, z_val))
        x = jax.nn.gelu(z_val, approximate=False) if k < 2 else z_val
    return (x, saved)


def corrector_backward(grad, saved, weights, norm_bias):
    spans = layer_spans(weights[0].shape[0], weights[0].shape[1])
    weight_grads = [None, None, None]
    gain_parts = [None, None, None]
    bias_parts = [None, None, None]
    for k in (2, 1, 0):
        (gstart, gwidth), (bstart, bwidth) = spans[k]
        x, h_low, z_val = saved[k]
        if k < 2:
            grad = jax.vjp(partial(jax.nn.gelu, approximate=False), z_val)[1](grad)[0]
        grad_low = grad.astype(jnp.bfloat16)
        weight_grads[k] = lax.dot_general(
            h_low, grad_low, (((0,), (0,)), ((), ())), preferred_element_type=jnp.float32
        )
        bias_parts[k] = jnp.sum(grad_low, axis=0, dtype=jnp.float32)
        back_h = lax.dot_general(
            grad_low, weights[k], (((1,), (1,)), ((), ())), preferred_element_type=jnp.float32
        )
        grad, gain_parts[k] = jax.vjp(norm_gain, x, 1.0 + norm_bias[0, gstart : gstart + gwidth])[
            1
        ](back_h)
    vector_grad = jnp.stack([jnp.concatenate(gain_parts), jnp.concatenate(bias_parts)])
    return (grad, (weight_grads[0], weight_grads[1], weight_grads[2], vector_grad))


def adamw(weight, mean, square, grad):
    mean_new = BETA_ONE * mean + (1.0 - BETA_ONE) * grad
    square_new = BETA_TWO * square + (1.0 - BETA_TWO) * grad * grad
    weight_new = weight - LEARN_RATE * (
        mean_new / (jnp.sqrt(square_new) + EPS_ADAM) + DECAY * weight
    )
    return (weight_new, mean_new, square_new)


def spread_device(
    spectral_state,
    legendre,
    wave_slots,
    lat_order,
    quad_weights,
    available,
    targets,
    w_first,
    w_mid,
    w_last,
    norm_bias,
    mean_first,
    mean_mid,
    mean_last,
    mean_bias,
    square_first,
    square_mid,
    square_last,
    square_bias,
):
    tdev, wdev, _, degrees, chans = spectral_state.shape
    fields = available.shape[1]
    rows_dev = available.shape[2]
    lon_count = available.shape[3]
    levels = chans // fields
    lat_index = lax.axis_index("lat")
    slots = lax.dynamic_slice_in_dim(wave_slots, lat_index * wdev, wdev)
    finv, ffw = wave_tables(wave_slots, lon_count)
    keep = (jnp.arange(degrees, dtype=jnp.int32)[None, :] >= slots[:, None]).astype(jnp.bfloat16)
    plg = jnp.take(legendre, lat_order, axis=2) * keep[:, :, None]
    qrow = jnp.take(quad_weights, lat_order)
    qlocal = lax.dynamic_slice_in_dim(qrow, lat_index * rows_dev, rows_dev)
    colw = qlocal[None, None, :, None] * available.astype(jnp.float32)
    den_part = jnp.sum(colw, axis=(2, 3))
    params = (w_first, w_mid, w_last, norm_bias)
    weights = (
        w_first.astype(jnp.bfloat16),
        w_mid.astype(jnp.bfloat16),
        w_last.astype(jnp.bfloat16),
    )

    def legendre_sum(piece):
        return jnp.einsum("mnr,tmprc->tmpnc", plg, piece, preferred_element_type=jnp.float32)

    def fourier_sum(table, piece):
        return jnp.einsum("mpk,tmprc->trkc", table, piece, preferred_element_type=jnp.float32)

    def to_grid(state):
        sums = jnp.einsum(
            "mnr,tmpnc->tmprc", plg, state.astype(jnp.bfloat16), preferred_element_type=jnp.float32
        ).astype(jnp.bfloat16)
        return fourier_sum(
            finv, lax.all_to_all(sums, "lat", split_axis=3, concat_axis=1, tiled=True)
        )

    def column_pass(grid):
        out, saved = corrector_forward(grid.reshape(-1, chans), weights, norm_bias)
        return (out.reshape(grid.shape), saved)

    states = []
    nums = []
    den_total = den_part
    state = spectral_state
    for s in range(STEPS):
        states.append(state)
        grid = to_grid(state)
        out, saved = column_pass(grid)
        pred = grid + STEP_SCALE * out
        num_part = jnp.einsum(
            "tfrk,trkfl->tf",
            colw,
            pred.reshape(tdev, rows_dev, lon_count, fields, levels),
            precision=HIGH,
        )
        num_total, den_total = lax.psum((num_part, den_part), "lat")
        nums.append(num_total)
        tend = (out * qlocal[None, :, None, None]).astype(jnp.bfloat16)
        coeff = jnp.einsum("mpk,trkc->tmprc", ffw, tend, preferred_element_type=jnp.float32).astype(
            jnp.bfloat16
        )
        spec = legendre_sum(lax.all_to_all(coeff, "lat", split_axis=1, concat_axis=3, tiled=True))
        state = state + STEP_SCALE * spec
    num_all = jnp.stack(nums)
    bias = num_all / (levels * den_total[None]) - jnp.moveaxis(targets, 1, 0)
    loss = lax.psum(jnp.sum(bias * bias) / STEPS, "tm")
    grad_bias = 2.0 * bias / (STEPS * levels * den_total[None])
    totals = tuple((jnp.zeros_like(p) for p in params))
    back_state = None
    for s in reversed(range(STEPS)):
        grid = to_grid(states[s])
        out, saved = column_pass(grid)
        scaled = jnp.moveaxis(colw * grad_bias[s][:, :, None, None], 1, 3)
        back_pred = jnp.broadcast_to(scaled[..., None], scaled.shape + (levels,)).reshape(
            grid.shape
        )
        back_out = STEP_SCALE * back_pred
        if back_state is not None:
            back_spec = (STEP_SCALE * back_state).astype(jnp.bfloat16)
            back_coeff = jnp.einsum(
                "mnr,tmpnc->tmprc", plg, back_spec, preferred_element_type=jnp.float32
            ).astype(jnp.bfloat16)
            back_tend = fourier_sum(
                ffw, lax.all_to_all(back_coeff, "lat", split_axis=3, concat_axis=1, tiled=True)
            )
            back_out = back_out + qlocal[None, :, None, None] * back_tend
        back_in, grads = corrector_backward(back_out.reshape(-1, chans), saved, weights, norm_bias)
        totals = tuple((a + b for a, b in zip(totals, grads)))
        if s > 0:
            back_grid = (back_pred + back_in.reshape(grid.shape)).astype(jnp.bfloat16)
            back_sums = jnp.einsum(
                "mpk,trkc->tmprc", finv, back_grid, preferred_element_type=jnp.float32
            ).astype(jnp.bfloat16)
            back_low = legendre_sum(
                lax.all_to_all(back_sums, "lat", split_axis=1, concat_axis=3, tiled=True)
            )
            back_state = back_low if back_state is None else back_state + back_low
    means = (mean_first, mean_mid, mean_last, mean_bias)
    squares = (square_first, square_mid, square_last, square_bias)
    grads = lax.psum(totals, ("tm", "lat"))
    grad_norm = jnp.sqrt(sum((jnp.sum(g * g) for g in grads)))
    factor = CLIP_NORM / jnp.maximum(grad_norm, CLIP_NORM)
    results = [adamw(w, a, b, g * factor) for w, a, b, g in zip(params, means, squares, grads)]
    masters = [r[0] for r in results]
    new_means = [r[1] for r in results]
    new_squares = [r[2] for r in results]
    halves = [w.astype(jnp.bfloat16) for w in masters]
    return (
        loss,
        grad_norm,
        masters[0],
        masters[1],
        masters[2],
        masters[3],
        new_means[0],
        new_means[1],
        new_means[2],
        new_means[3],
        new_squares[0],
        new_squares[1],
        new_squares[2],
        new_squares[3],
        halves[0],
        halves[1],
        halves[2],
        halves[3],
    )


F32 = jnp.float32
BF16 = jnp.bfloat16
VM = pltpu.VMEM
LANES = 128
GROUP = 2
SUB = 256
CHUNK = 32
ROWS_BLOCK = 2
VMEM_LIMIT = 10 << 20
SAVED_LIMIT = 96 << 20


Plan = namedtuple("Plan", ("group", "rows", "waves", "degrees", "steps", "fields", "chans", "hidden", "lons"))


def dot(a, b, dims=((1,), (0,))):
    return lax.dot_general(a, b, (dims, ((), ())), preferred_element_type=F32)


def norm_unit(x, eps):
    centre = x - jnp.mean(x, axis=-1, keepdims=True)
    scale = lax.rsqrt(jnp.mean(centre * centre, axis=-1, keepdims=True) + eps)
    return centre * scale, scale


def gelu_parts(z):
    arg = z * math.sqrt(0.5)
    return arg, 1.0 + lax.erf(arg)


def slope_twice(z):
    arg, cdf = gelu_parts(z)
    return cdf + (z * math.sqrt(2.0 / math.pi)) * jnp.exp2(arg * arg * -math.log2(math.e))


def wide(scale, width):
    return jnp.concatenate([scale] * (width // LANES), axis=1)


def whole(a):
    return pl.BlockSpec(a.shape, lambda *_: (0,) * len(a.shape))


def fold(v):
    return jnp.sum(v.reshape(v.shape[0] // 8, 8, v.shape[1]), axis=0)


def field_mask(fields, chans):
    lane = lax.broadcasted_iota(jnp.int32, (fields, chans), 1)
    row = lax.broadcasted_iota(jnp.int32, (fields, chans), 0) * (chans // fields)
    return (lane >= row) & (lane < row + chans // fields)


def splits(nb, chans, hidden):
    gains = [1.0 + nb[0:1, a:b] for a, b in ((0, chans), (chans, chans + hidden), (chans + hidden, chans + 2 * hidden))]
    biases = [nb[1:2, a:b] for a, b in ((0, hidden), (hidden, 2 * hidden), (2 * hidden, 2 * hidden + chans))]
    return gains, biases


def stagger(chains):
    live, waiting = [], list(chains)
    while live or waiting:
        if waiting:
            live.append(waiting.pop(0))
        for chain in list(live):
            if next(chain, live) is live:
                live.remove(chain)


def pair_rows(plan):
    return ROWS_BLOCK if plan.rows % ROWS_BLOCK == 0 else 1


def row_weight(plan, info, order, quad, row):
    return quad[order[(info[1] * 2 + info[0]) * plan.rows + row]]


def prepare_kernel(
    plan, info, slots, order, quad, got, got_o, inv, ffw, wanted, state, links, lt, avail, nums, table, ffw_t, tgt
):
    group, rows, waves, degrees, steps, fields, chans, _, _ = plan
    members = 2 * group
    core, member = info[0], info[1]
    span = waves * degrees
    mine = rows * waves
    half = fields // 2
    lats = rows * members
    leg = jnp.zeros((waves, chans), F32)
    row_of = lax.broadcasted_iota(jnp.int32, (waves, chans), 0)
    pick = lax.broadcasted_iota(jnp.int32, (8, chans), 0) == half
    for j in range(waves):
        at = pl.ds(j * degrees, degrees)
        for ref, p in ((got, core), (got_o, 1 - core)):
            hi = ref[j, 0:degrees, :].astype(F32)
            state[p, at, :] = hi + ref[j, degrees : 2 * degrees, :].astype(F32)
        tail = got[j, 2 * degrees : 2 * degrees + 8, :].astype(F32)
        line = jnp.sum(jnp.where(pick, tail, 0.0), axis=0, keepdims=True)
        leg = jnp.where(row_of == j, line, leg)
    iota = lambda d, s: lax.broadcasted_iota(jnp.int32, s, d)
    shape = (span, span)
    r0, r1 = iota(0, shape), iota(1, shape)
    expand = (iota(0, (span, waves)) // degrees == iota(1, (span, waves))).astype(F32).astype(BF16)
    rep = dot(expand, leg.astype(BF16))
    rep = jnp.where(r1 // lats == r0 % degrees, rep, 0.0).astype(BF16)
    lat_lane = jnp.zeros((8, span), jnp.int32)
    lane = iota(1, (8, span)) // waves
    for role in range(members):
        other = (member ^ (role & (group - 1))) * 2 + (core ^ (role // group))
        for r in range(rows):
            lat_lane = jnp.where(lane == role * rows + r, order[other * rows + r], lat_lane)
    wave_row = jnp.zeros(shape, jnp.int32)
    for j in range(waves):
        wave_row = jnp.where(r0 // degrees == j, slots[j], wave_row)
    choose = (r0 % lats == lat_lane[0:1, :]).astype(F32).astype(BF16)
    plg = dot(rep, choose)
    plg = jnp.where((r0 // degrees == r1 % waves) & (r0 % degrees >= wave_row), plg, 0.0)
    links[...] = plg.astype(BF16)
    lt[...] = plg[:, 0:mine].T.astype(BF16)
    spot = member * 2 + core
    den = jnp.zeros((fields, chans), F32)
    for r in range(rows):
        src = spot * rows + r
        a = got[src, 2 * degrees : 2 * degrees + 8, :].astype(F32)
        b = got_o[src, 2 * degrees : 2 * degrees + 8, :].astype(F32)
        first = jnp.where(core == 0, a, b)[0:half]
        second = jnp.where(core == 0, b, a)[0:half]
        both = jnp.concatenate([first, second], axis=0)
        avail[r] = both.astype(BF16)
        den += quad[order[src]] * both
    nums[...] = jnp.zeros_like(nums)
    nums[steps * fields :, :] = jnp.broadcast_to(jnp.sum(den, axis=1, keepdims=True), (fields, nums.shape[1]))
    table[...] = inv[...].T.astype(BF16)
    ffw_t[...] = ffw[...].T.astype(BF16)
    tgt[...] = wanted[...]


def prepare_call(plan, info, slots, order, quad, got, got_o, inv, ffw, wanted):
    group, rows, waves, degrees, steps, fields, chans, _, lons = plan
    span, mine = waves * degrees, rows * waves
    ins = [got, got_o, inv, ffw, wanted]
    shapes = [
        jax.ShapeDtypeStruct((2, span, chans), F32),
        jax.ShapeDtypeStruct((span, 2 * group * mine), BF16),
        jax.ShapeDtypeStruct((mine, span), BF16),
        jax.ShapeDtypeStruct((rows, fields, lons), BF16),
        jax.ShapeDtypeStruct(((steps + 1) * fields, LANES), F32),
        jax.ShapeDtypeStruct((lons, 2 * waves), BF16),
        jax.ShapeDtypeStruct((lons, 2 * waves), BF16),
        jax.ShapeDtypeStruct(wanted.shape, F32),
    ]
    return pl.pallas_call(
        partial(prepare_kernel, plan),
        out_shape=shapes,
        grid_spec=pltpu.PrefetchScalarGridSpec(
            num_scalar_prefetch=4,
            grid=(1,),
            in_specs=[whole(a) for a in ins],
            out_specs=[whole(a) for a in shapes],
        ),
        compiler_params=kernel_params(),
        name="prepare",
    )(info, slots, order, quad, *ins)


def kernel_params():
    return pltpu.CompilerParams(vmem_limit_bytes=VMEM_LIMIT)


def write_count(plan, step, nums_in, nums, acc):
    fields, chans = plan.fields, plan.chans
    kept = jnp.where(field_mask(fields, chans), acc, 0.0)
    nums[...] = nums_in[...]
    nums[step * fields : (step + 1) * fields, :] = jnp.broadcast_to(
        jnp.sum(kept, axis=1, keepdims=True), (fields, LANES)
    )


def weighted_sum(weights, values):
    hi = values.astype(BF16)
    lo = (values - hi.astype(F32)).astype(BF16)
    return dot(weights, hi) + dot(weights, lo)


def forward_kernel(plan, step, info, order, quad, *refs):
    group, rows, waves, _, steps, fields, chans, hidden, lons = plan
    first, last = step == 0, step == steps - 1
    rows_blk = pair_rows(plan)
    refs = list(refs)
    take = lambda: refs.pop(0)
    state, table, ffw, lt, w1, w2, w3, nb = [take() for _ in range(8)]
    if last:
        avail, nums_in = take(), take()
    if not first:
        links = take()
        pieces = [take() for _ in range(2 * group)]
    units, inners, scales = [take() for _ in range(3)]
    if last:
        nums = take()
    else:
        sums, outs, y_out = [take() for _ in range(3)]
        if not first:
            state_out = take()
    if last:
        sums, num_acc = take(), take()
    i = pl.program_id(0)

    @pl.when(i == 0)
    def _():
        for p in range(2):
            st = state[p]
            if not first:
                spec = dot(links[...], jnp.concatenate([piece[p] for piece in pieces], axis=0))
                st = st + STEP_SCALE * spec
                if not last:
                    state_out[p] = st
            sums[p] = dot(lt[...], st.astype(BF16)).astype(BF16)
        if last:
            num_acc[...] = jnp.zeros_like(num_acc)

    gains, biases = splits(nb, chans, hidden)
    spans = ((0, chans), (chans, hidden), (chans + hidden, hidden))
    weights = (w1, w2, w3)

    def row_chain(rr):
        row = i * rows_blk + rr
        at = pl.ds(pl.multiple_of(row * waves, waves), waves)
        rhs = jnp.concatenate([sums[0, at, :], sums[1, at, :]], axis=0)
        q = row_weight(plan, info, order, quad, row)
        grid = dot(table[...], rhs)
        yield
        x = [grid[c : c + CHUNK] for c in range(0, lons, CHUNK)]
        for k in range(3):
            low = []
            for n, part in enumerate(x):
                cs = pl.ds(pl.multiple_of(row * lons + n * CHUNK, CHUNK), CHUNK)
                if k:
                    part = part + biases[k - 1]
                    inners[cs, (k - 1) * hidden : k * hidden] = part
                    part = part * gelu_parts(part)[1]
                unit, scale = norm_unit(part, 4.0 * EPS_NORM if k else EPS_NORM)
                units[cs, spans[k][0] : spans[k][0] + spans[k][1]] = unit
                scales[cs, k * LANES : (k + 1) * LANES] = jnp.broadcast_to(scale, (CHUNK, LANES))
                low.append((unit * gains[k]).astype(BF16))
            yield
            z = dot(jnp.concatenate(low, axis=0), weights[k][...])
            x = [z[c : c + CHUNK] for c in range(0, lons, CHUNK)]
            yield
        if last:
            pred = grid + STEP_SCALE * (z + biases[2])
            yield
            num_acc[...] += q * weighted_sum(avail[row], pred)
        else:
            tends = []
            for n, part in enumerate(x):
                cs = pl.ds(pl.multiple_of(row * lons + n * CHUNK, CHUNK), CHUNK)
                out = part + biases[2]
                outs[cs, :] = out
                tends.append((out * q).astype(BF16))
            yield
            coeff = dot(ffw[...], jnp.concatenate(tends, axis=0)).astype(BF16)
            y_out[0, at, :] = coeff[:waves]
            y_out[1, at, :] = coeff[waves:]
        yield

    stagger([row_chain(rr) for rr in range(rows_blk)])

    if last:

        @pl.when(i == pl.num_programs(0) - 1)
        def _():
            write_count(plan, step, nums_in, nums, num_acc[...])


def step_call(kernel, name, grid, shapes, ins, scalars, work, scratch=(), aliases=None):
    cols, flops = work
    return pl.pallas_call(
        kernel,
        out_shape=shapes,
        grid_spec=pltpu.PrefetchScalarGridSpec(
            num_scalar_prefetch=len(scalars),
            grid=(grid,),
            in_specs=[pl.BlockSpec(memory_space=VM)] * len(ins),
            out_specs=[pl.BlockSpec(memory_space=VM)] * len(shapes),
            scratch_shapes=list(scratch),
        ),
        input_output_aliases=aliases or {},
        compiler_params=kernel_params(),
        cost_estimate=pl.CostEstimate(flops=cols * flops, bytes_accessed=cols * 8192, transcendentals=cols * 1024),
        name=name,
    )(*scalars, *ins)


def forward_call(plan, step, scalars, state, avail, nums, table, ffw, lt, weights, nb, links, pieces):
    group, rows, waves, _, steps, fields, chans, hidden, lons = plan
    first, last = step == 0, step == steps - 1
    rows_blk = pair_rows(plan)
    cols = rows * lons
    ins = [state, table, ffw, lt, *weights, nb]
    if last:
        ins += [avail, nums]
    if not first:
        ins += [links, *pieces]
    shapes = [VM((cols, width), F32) for width in (chans + 2 * hidden, 2 * hidden, 3 * LANES)]
    sums = (2, rows * waves, chans)
    scratch = []
    if last:
        shapes.append(VM(nums.shape, F32))
        scratch = [VM(sums, BF16), VM((fields, chans), F32)]
    else:
        shapes += [VM(sums, BF16), VM((cols, chans), F32), VM(sums, BF16)]
        if not first:
            shapes.append(VM(state.shape, F32))
    flops = 2 * hidden * (2 * chans + hidden)
    return step_call(
        partial(forward_kernel, plan, step), f"forward_{step}", rows // rows_blk, shapes, ins, scalars, (cols, flops), scratch
    )


def slopes_kernel(plan, inners, scales, slopes):
    rows, hidden, lons = plan.rows, plan.hidden, plan.lons
    i = pl.program_id(0)
    for n in range(lons // CHUNK):
        cs = pl.ds(pl.multiple_of(i * lons + n * CHUNK, CHUNK), CHUNK)
        for k in range(2):
            at = slice(k * hidden, (k + 1) * hidden)
            scale = wide(scales[cs, (k + 1) * LANES : (k + 2) * LANES], hidden)
            slopes[cs, at] = slope_twice(inners[cs, at]) * scale


def slopes_call(plan, step, inners, scales):
    work = (plan.rows * plan.lons, 16 * plan.hidden)
    return step_call(
        partial(slopes_kernel, plan), f"slopes_{step}", plan.rows, [VM(inners.shape, F32)], [inners, scales], (), work, (), {0: 0}
    )[0]


def counts_kernel(plan, step, info, order, quad, sums, outs, avail, nums_in, table, nums):
    rows, waves, fields, chans, lons = plan.rows, plan.waves, plan.fields, plan.chans, plan.lons
    acc = jnp.zeros((fields, chans), F32)
    for row in range(rows):
        at = slice(row * waves, (row + 1) * waves)
        grid = dot(table[...], jnp.concatenate([sums[0, at, :], sums[1, at, :]], axis=0))
        pred = grid + STEP_SCALE * outs[row * lons : (row + 1) * lons, :]
        acc = acc + row_weight(plan, info, order, quad, row) * weighted_sum(avail[row], pred)
    write_count(plan, step, nums_in, nums, acc)


def counts_call(plan, step, scalars, ins):
    work = (plan.rows * plan.lons, 8 * plan.chans)
    return step_call(partial(counts_kernel, plan, step), f"counts_{step}", 1, [VM(ins[3].shape, F32)], ins, scalars, work)[0]


def packed_parts(plan):
    parts, at = [], 0
    sizes = ((plan.chans, plan.hidden), (plan.hidden, plan.hidden), (plan.hidden, plan.chans))
    for which, (rows, cols) in enumerate(sizes):
        for tile in range(cols // LANES):
            parts.append((which, tile, at, rows))
            at += rows
    return parts, at


def packed_block(plan, chips):
    vectors = 2 * (plan.chans + 2 * plan.hidden) // LANES
    need = packed_parts(plan)[1] + vectors
    return -(-need // (2 * chips * 16)) * 16


def both_halves(at, rows, half):
    out, done = [], 0
    while done < rows:
        h = (at + done) // half
        n = min(rows - done, (h + 1) * half - at - done)
        out.append((h, at + done - h * half, done, n))
        done += n
    return out


def backward_kernel(plan, step, info, order, quad, *refs):
    group, rows, waves, _, steps, fields, chans, hidden, lons = plan
    first, last = step == steps - 1, step == 0
    fresh = step == steps - 2
    rows_blk = pair_rows(plan)
    members = 2 * group
    levels = chans // fields
    refs = list(refs)
    take = lambda: refs.pop(0)
    units, slopes, scales, avail, tgt, w2, w3, nb = [take() for _ in range(8)]
    counts = [take() for _ in range(members)]
    if not first:
        links, lt, ffw_t = [take() for _ in range(3)]
        pieces = [take() for _ in range(members)]
        if not fresh:
            bstate = take()
    if not last:
        w1, inv = take(), take()
    dzs = take()
    if not last:
        b_out = take()
        if not first:
            bstate_out = take()
    if first:
        loss = take()
    coef, gmask = take(), take()
    i = pl.program_id(0)

    @pl.when(i == 0)
    def _():
        def total(s):
            acc = [c[s * fields : (s + 1) * fields, :] for c in counts]
            while len(acc) > 1:
                acc = [a + b for a, b in zip(acc[::2], acc[1::2])]
            return acc[0]

        den = total(steps)
        bias_of = lambda s: total(s) / (levels * den) - tgt[s * fields : (s + 1) * fields, :]
        gb = 2.0 * bias_of(step) / (steps * levels * den)
        gb = jnp.where(field_mask(fields, chans), wide(gb, chans), 0.0)
        hi = gb.astype(BF16).astype(F32)
        gmask[...] = jnp.concatenate([hi, gb - hi], axis=0).astype(BF16)
        if first:
            sq = bias_of(0) * bias_of(0)
            for s in range(1, steps):
                sq = sq + bias_of(s) * bias_of(s)
            loss[...] = jnp.broadcast_to(jnp.sum(sq, axis=0, keepdims=True) / steps, loss.shape)
        else:
            for p in range(2):
                st = dot(links[...], jnp.concatenate([piece[p] for piece in pieces], axis=0))
                if not fresh:
                    st = bstate[p] + st
                if not last:
                    bstate_out[p] = st
                coef[p] = dot(lt[...], (STEP_SCALE * st).astype(BF16)).astype(BF16)

    gains, _ = splits(nb, chans, hidden)

    def norm_back(back, gain, unit):
        low = back * gain
        m1 = jnp.mean(low, axis=-1, keepdims=True)
        m2 = jnp.mean(low * unit, axis=-1, keepdims=True)
        return low - m1 - unit * m2

    def row_chain(rr):
        row = i * rows_blk + rr
        at = pl.ds(pl.multiple_of(row * waves, waves), waves)
        q = row_weight(plan, info, order, quad, row)
        chunks = [pl.ds(pl.multiple_of(row * lons + c, CHUNK), CHUNK) for c in range(0, lons, CHUNK)]
        cut = lambda v: [v[c : c + CHUNK] for c in range(0, lons, CHUNK)]
        av2 = jnp.concatenate([avail[row].astype(F32)] * 2, axis=0).astype(BF16)
        mask = dot(av2, gmask[...], ((0,), (0,)))
        if not first:
            tend = dot(ffw_t[...], jnp.concatenate([coef[0, at, :], coef[1, at, :]], axis=0))
        yield
        dpreds, low = [], []
        for n, (cs, part) in enumerate(zip(chunks, cut(mask))):
            dpred = q * part
            dout = STEP_SCALE * dpred
            if not first:
                dout = dout + q * cut(tend)[n]
            dpreds.append(dpred)
            low.append(dout.astype(BF16))
            dzs[cs, 2 * hidden :] = low[-1]
        yield
        for k, weight in ((2, w3), (1, w2)):
            back = dot(jnp.concatenate(low, axis=0), weight[...], ((1,), (1,)))
            yield
            low = []
            span = slice(chans + (k - 1) * hidden, chans + k * hidden)
            inner = slice((k - 1) * hidden, k * hidden)
            for cs, part in zip(chunks, cut(back)):
                dx = norm_back(part, gains[k], units[cs, span])
                low.append((dx * slopes[cs, inner]).astype(BF16))
                dzs[cs, inner] = low[-1]
            yield
        if not last:
            back = dot(jnp.concatenate(low, axis=0), w1[...], ((1,), (1,)))
            yield
            grids = []
            for n, (cs, part) in enumerate(zip(chunks, cut(back))):
                dx = norm_back(part, gains[0], units[cs, 0:chans])
                grids.append((dpreds[n] + dx * wide(scales[cs, 0:LANES], chans)).astype(BF16))
            yield
            coeff = dot(inv[...], jnp.concatenate(grids, axis=0)).astype(BF16)
            b_out[0, at, :] = coeff[:waves]
            b_out[1, at, :] = coeff[waves:]
            yield

    stagger([row_chain(rr) for rr in range(rows_blk)])


def backward_call(plan, step, scalars, saved, avail, tgt, weights, nb, counts, tables, pieces, bstate):
    group, rows, waves, degrees, steps, fields, chans, hidden, lons = plan
    first, last = step == steps - 1, step == 0
    rows_blk = pair_rows(plan)
    links, lt, ffw_t, inv = tables
    ins = [*saved, avail, tgt, *weights[1:], nb, *counts]
    if not first:
        ins += [links, lt, ffw_t, *pieces]
        if step != steps - 2:
            ins.append(bstate)
    if not last:
        ins += [weights[0], inv]
    sums = (2, rows * waves, chans)
    shapes = [VM((rows * lons, 2 * hidden + chans), BF16)]
    if not last:
        shapes.append(VM(sums, BF16))
        if not first:
            shapes.append(VM((2, waves * degrees, chans), F32))
    if first:
        shapes.append(VM((8, LANES), F32))
    flops = 2 * hidden * (2 * chans + hidden)
    return step_call(
        partial(backward_kernel, plan, step),
        f"backward_{step}",
        rows // rows_blk,
        shapes,
        ins,
        scalars,
        (rows * lons, flops),
        [VM(sums, BF16), VM((2 * fields, chans), BF16)],
    )


def grads_kernel(plan, step, info, *refs):
    _, rows, _, _, steps, _, chans, hidden, lons = plan
    first, last = step == steps - 1, step == 0
    refs = list(refs)
    take = lambda: refs.pop(0)
    units, dzs, nb = [take() for _ in range(3)]
    before = None if first else [take() for _ in range(4)]
    if last:
        weights = [take() for _ in range(3)]
        mine, send = take(), take()
    grads = [take() for _ in range(4)]
    gains, _ = splits(nb, chans, hidden)
    ins = ((0, chans), (chans, hidden), (chans + hidden, hidden))
    outs = ((0, hidden), (hidden, hidden), (2 * hidden, chans))
    for k in range(3):
        a, b = ins[k][0], outs[k][0]
        unit = slice(a, a + ins[k][1])
        slot = slice(b, b + outs[k][1])
        low = [(units[c : c + CHUNK, unit] * gains[k]).astype(BF16) for c in range(0, rows * lons, CHUNK)]
        new = dot(jnp.concatenate(low, axis=0), dzs[:, slot], ((0,), (0,)))
        bias = fold(dzs[0:CHUNK, slot].astype(F32))
        for c in range(CHUNK, rows * lons, CHUNK):
            bias = bias + fold(dzs[c : c + CHUNK, slot].astype(F32))
        if not first:
            new = before[k][...] + new
            bias = before[3][:, slot] + bias
        grads[k][...] = new
        grads[3][:, slot] = bias
    if not last:
        return
    packed = refs.pop(0)
    half = packed.shape[1]
    parts, at = packed_parts(plan)
    for which, tile, start, count in parts:
        for h, dst, src, n in both_halves(start, count, half):
            packed[h, dst : dst + n, :] = grads[which][src : src + n, tile * LANES : (tile + 1) * LANES]
    lines = []
    for k in range(3):
        prod = grads[k][...] * weights[k][...].astype(F32)
        thin = prod[:, 0:LANES]
        for tile in range(1, prod.shape[1] // LANES):
            thin = thin + prod[:, tile * LANES : (tile + 1) * LANES]
        lines.append(jnp.sum(thin.T, axis=0, keepdims=True) / gains[k])
    for line in (jnp.concatenate(lines, axis=1), jnp.sum(grads[3][...], axis=0, keepdims=True)):
        for tile in range(line.shape[1] // LANES):
            packed[1, at - half : at - half + 1, :] = line[:, tile * LANES : (tile + 1) * LANES]
            at += 1
    packed[1, at - half :, :] = jnp.zeros((2 * half - at, LANES), F32)
    mine[...] = packed[info[0]]
    send[...] = packed[1 - info[0]]


def grads_call(plan, step, chips, info, units, dzs, nb, before, weights):
    _, rows, _, _, steps, _, chans, hidden, lons = plan
    first, last = step == steps - 1, step == 0
    ins = [units, dzs, nb]
    aliases = {}
    if not first:
        ins += before
    sums = [VM(s, F32) for s in ((chans, hidden), (hidden, hidden), (hidden, chans), (8, 2 * hidden + chans))]
    if last:
        ins += weights
        half = chips * packed_block(plan, chips)
        shapes, scratch = [VM((half, LANES), F32)] * 2, [*sums, VM((2, half, LANES), F32)]
    else:
        shapes, scratch = sums, []
        if not first:
            aliases = {4 + n: n for n in range(4)}
    flops = 2 * hidden * (2 * chans + hidden)
    return step_call(
        partial(grads_kernel, plan, step), f"grads_{step}", 1, shapes, ins, (info,), (rows * lons, flops), scratch, aliases
    )


def pairs_kernel(chips, group, mine, got, loss, out):
    blk = mine.shape[0] // chips
    share = loss[...] * (1.0 / group)
    row = lax.broadcasted_iota(jnp.int32, share.shape, 0)
    high = share.astype(BF16).astype(F32)
    rest = share - high
    mid = rest.astype(BF16).astype(F32)
    lines = jnp.where(row == 0, high, jnp.where(row == 1, mid, jnp.where(row == 2, rest - mid, 0.0)))
    lines = jnp.concatenate([lines, jnp.zeros_like(lines)], axis=0).astype(BF16)
    for c in range(chips):
        at = slice(c * blk, (c + 1) * blk)
        out[c, 0:blk, :] = (mine[at, :] + got[at, :]).astype(BF16)
        out[c, blk:, :] = lines


def chips_kernel(got, out, loss):
    chips, blk = out.shape[0], out.shape[1]
    total = got[0].astype(F32)
    for c in range(1, chips):
        total = total + got[c].astype(F32)
    low = total[0:blk].astype(BF16)
    for c in range(chips):
        out[c] = low
    loss[...] = jnp.broadcast_to(jnp.sum(total[blk:], axis=0, keepdims=True), loss.shape)


def update_kernel(plan, info, part, part_o, *refs):
    params, means, squares = refs[0:4], refs[4:8], refs[8:12]
    norm = refs[12]
    masters, new_means, new_squares, halves = refs[13:17], refs[17:21], refs[21:25], refs[25:29]
    packed = refs[29]
    packed[info[0]] = part[...]
    packed[1 - info[0]] = part_o[...]
    half = packed.shape[1]
    acc = jnp.zeros((16, LANES), F32)
    for h in range(2):
        g = packed[h].astype(F32)
        acc = acc + jnp.sum((g * g).reshape(half // 16, 16, LANES), axis=0)
    total = jnp.sum(jnp.sum(acc, axis=0, keepdims=True), axis=1, keepdims=True)
    root = jnp.sqrt(jnp.broadcast_to(total, (8, LANES)))
    norm[...] = root
    factor = (CLIP_NORM / jnp.maximum(root, CLIP_NORM))[0:1, :]

    def apply(which, rs, cs, g):
        w, a, b = adamw(params[which][rs, cs], means[which][rs, cs], squares[which][rs, cs], g * factor)
        masters[which][rs, cs] = w
        new_means[which][rs, cs] = a
        new_squares[which][rs, cs] = b
        halves[which][rs, cs] = w.astype(BF16)

    parts, at = packed_parts(plan)
    for which, tile, start, count in parts:
        for h, src, dst, n in both_halves(start, count, half):
            apply(which, slice(dst, dst + n), slice(tile * LANES, (tile + 1) * LANES), packed[h, src : src + n, :].astype(F32))
    tiles = (plan.chans + 2 * plan.hidden) // LANES
    rows = packed[1, at - half : at - half + 2 * tiles, :].astype(F32)
    for tile in range(tiles):
        g = jnp.concatenate([rows[tile : tile + 1], rows[tiles + tile : tiles + tile + 1]], axis=0)
        apply(3, slice(0, 2), slice(tile * LANES, (tile + 1) * LANES), g)


def small_call(kernel, name, shapes, ins, scalars=(), scratch=()):
    return pl.pallas_call(
        kernel,
        out_shape=shapes,
        grid_spec=pltpu.PrefetchScalarGridSpec(
            num_scalar_prefetch=len(scalars),
            grid=(1,),
            in_specs=[whole(a) for a in ins],
            out_specs=[whole(a) for a in shapes],
            scratch_shapes=list(scratch),
        ),
        compiler_params=kernel_params(),
        name=name,
    )(*scalars, *ins)


def grouped_device(
    plan,
    chips,
    spectral_state,
    legendre,
    wave_slots,
    lat_order,
    quad_weights,
    available,
    targets,
    *flat,
):
    group, rows, waves, degrees, steps, fields, chans, hidden, lons = plan
    params, means, squares = flat[0:4], flat[4:8], flat[8:12]
    weights = [w.astype(BF16) for w in params[:3]]
    nb = params[3]
    tdev = spectral_state.shape[0]
    copies = waves // chips
    core = lax.axis_index("tm")
    chip = lax.axis_index("lat")
    member = chip % group
    info = jnp.stack([core, member]).astype(jnp.int32)
    swap = [(0, 1), (1, 0)]
    across = lambda a: lax.ppermute(a, "tm", swap)

    def to_members(a, fill):
        out = [a]
        bit = 1
        while bit < group:
            out += [lax.ppermute(v, "lat", [(n, n ^ bit) for n in range(waves)]) for v in out]
            bit *= 2
        away, filled = lax.optimization_barrier((out[1:], fill()))
        out = [a, *away]
        return out + [across(v) for v in out], filled

    half = fields // 2
    pad = -(2 * degrees + half + 1) % 8
    high = spectral_state[:, 0].astype(BF16)
    low = (spectral_state[:, 0] - high.astype(F32)).astype(BF16)
    seen = available[:, :, 0].reshape(tdev, 2, half, lons).astype(BF16)
    leg = jnp.broadcast_to(legendre.reshape(1, 1, 1, chans), (tdev, 2, 1, chans))
    pack = jnp.concatenate([high, low, seen, leg, jnp.zeros((tdev, 2, pad, chans), BF16)], axis=2)
    keep = lax.dynamic_index_in_dim(pack, core, axis=1, keepdims=False)
    other = across(lax.dynamic_index_in_dim(pack, 1 - core, axis=1, keepdims=False))
    times = jnp.concatenate([jnp.where(core == 0, keep, other), jnp.where(core == 0, other, keep)], axis=0)
    spread = jnp.broadcast_to(times[None, :, None], (copies, 2 * tdev, group, *times.shape[1:]))
    got = lax.all_to_all(spread.reshape(waves, *times.shape[1:]), "lat", split_axis=0, concat_axis=0, tiled=True)
    got_o = across(got)

    def table(scaled):
        product = wave_slots[:, None] * jnp.arange(lons, dtype=jnp.int32)[None, :] % lons
        phase = product.astype(F32) * (2.0 * math.pi / lons)
        inverse = jnp.concatenate([jnp.cos(phase), -jnp.sin(phase)], axis=0)
        if not scaled:
            return inverse
        scale = jnp.where(wave_slots == 0, 1.0, 2.0).astype(F32) / lons
        return inverse * jnp.concatenate([scale, scale])[:, None]

    inv32, ffw32 = table(False), table(True)
    inv, ffw = inv32.astype(BF16), ffw32.astype(BF16)
    theirs = across(targets)
    tgt_all = jnp.concatenate([jnp.where(core == 0, targets, theirs), jnp.where(core == 0, theirs, targets)], axis=0)
    tgt = lax.dynamic_index_in_dim(tgt_all, (chip // group) % (2 * tdev), axis=0, keepdims=False)
    tgt = jnp.broadcast_to(tgt.reshape(steps * fields, 1), (steps * fields, LANES))
    state, links, lt, avail, nums, inv_t, ffw_t, tgt = prepare_call(
        plan, info, wave_slots, lat_order, quad_weights, got, got_o, inv32, ffw32, tgt
    )
    scalars = (info, lat_order, quad_weights)

    saved, pieces = [], None
    for s in range(steps):
        units, inners, scales, *rest = forward_call(
            plan, s, scalars, state, avail, nums, inv_t, ffw, lt, weights, nb, links, pieces
        )
        fill = lambda: slopes_call(plan, s, inners, scales)
        if s < steps - 1:
            pieces, slopes = to_members(rest[2], fill)
            nums = counts_call(plan, s, scalars, [rest[0], rest[1], avail, nums, inv_t])
            pieces, nums = lax.optimization_barrier((pieces, nums))
            if s:
                state = rest[3]
        else:
            counts, slopes = to_members(rest[0], fill)
        saved.append((units, slopes, scales))
    before, bstate = None, None
    for s in reversed(range(steps)):
        dzs, *rest = backward_call(
            plan, s, scalars, saved[s], avail, tgt, weights, nb, counts, (links, lt, ffw_t, inv), pieces, bstate
        )
        fill = lambda: grads_call(plan, s, chips, info, saved[s][0], dzs, nb, before, weights)
        if s == 0:
            before = fill()
        else:
            pieces, before = to_members(rest[0], fill)
            if s == steps - 1:
                loss = rest[1]
            else:
                bstate = rest[1]
    mine, send = before
    blk = mine.shape[0] // chips
    groups = [[c * chips + n for n in range(chips)] for c in range(copies)]
    exchange = lambda a: lax.all_to_all(a, "lat", split_axis=0, concat_axis=0, tiled=True, axis_index_groups=groups)
    (parts,) = small_call(
        partial(pairs_kernel, chips, group),
        "pairs",
        [jax.ShapeDtypeStruct((chips, blk + 16, LANES), BF16)],
        [mine, across(send), loss],
    )
    reduced, loss = small_call(
        chips_kernel,
        "chips",
        [jax.ShapeDtypeStruct((chips, blk, LANES), BF16), jax.ShapeDtypeStruct((8, LANES), F32)],
        [exchange(parts)],
    )
    part = exchange(reduced).reshape(chips * blk, LANES)
    shapes = [jax.ShapeDtypeStruct((8, LANES), F32)]
    for kind in (F32, F32, F32, BF16):
        shapes += [jax.ShapeDtypeStruct(w.shape, kind) for w in params]
    norm, *results = small_call(
        partial(update_kernel, plan),
        "update",
        shapes,
        [part, across(part), *params, *means, *squares],
        (info,),
        [VM((2, chips * blk, LANES), BF16)],
    )
    return (loss[0, 0], norm[0, 0], *results)


def make_plan(mesh, args):
    state, legendre, _, _, _, available, targets, w_first = args[:8]
    times, waves, _, degrees, chans = state.shape
    _, fields, lats, lons = available.shape
    hidden = w_first.shape[1]
    cores, chips_all = mesh.shape["tm"], mesh.shape["lat"]
    group = GROUP
    chips = group * times
    rows, rest = divmod(lats, 2 * group)
    fits = (
        cores == 2
        and times % cores == 0
        and chips_all == waves == lats
        and waves % chips == 0
        and rest == 0
        and fields == 8
        and lons == chans == degrees * lats
        and waves % 16 == 0
        and degrees % 16 == 0
        and chans % LANES == 0
        and hidden % LANES == 0
        and lons % SUB == 0
    )
    if not fits or legendre.shape != (waves, degrees, lats):
        return None
    steps = targets.shape[1]
    if steps < 3 or steps * rows * lons * (chans + 4 * hidden + LANES) * 4 > SAVED_LIMIT:
        return None
    return Plan(group, rows, waves, degrees, steps, fields, chans, hidden, lons), chips


def solution(mesh):
    in_specs = (
        P("tm", "lat", None, None, None),
        P("lat", None, None),
        P(),
        P(),
        P(),
        P("tm", None, "lat", None),
        P("tm", None, None),
    ) + (P(),) * 12

    def run(*args):
        made = make_plan(mesh, args)
        body = spread_device if made is None else partial(grouped_device, *made)
        return jax.shard_map(body, mesh=mesh, in_specs=in_specs, out_specs=(P(),) * 18, check_vma=False)(*args)

    return run
```

```python
from collections import namedtuple
from functools import partial
import math

import jax
import jax.numpy as jnp
from jax import lax
from jax.experimental import pallas as pl
from jax.experimental.pallas import tpu as pltpu
from jax.sharding import PartitionSpec as P

STEPS = 4


EPS_NORM = 1e-05
STEP_SCALE = 0.5
CLIP_NORM = 1.0
LEARN_RATE = 0.01
BETA_ONE = 0.9
BETA_TWO = 0.95
EPS_ADAM = 1e-08
DECAY = 0.1
HIGH = lax.Precision.HIGHEST


def wave_tables(wave_slots, lon_count):
    product = wave_slots[:, None] * jnp.arange(lon_count, dtype=jnp.int32)[None, :] % lon_count
    phase = product.astype(jnp.float32) * (2.0 * math.pi / lon_count)
    inverse = jnp.stack([jnp.cos(phase), -jnp.sin(phase)], axis=1)
    scale = jnp.where(wave_slots == 0, 1.0, 2.0).astype(jnp.float32) / lon_count
    return (inverse.astype(jnp.bfloat16), (inverse * scale[:, None, None]).astype(jnp.bfloat16))


def layer_spans(chans, hidden):
    gains = [(0, chans), (chans, hidden), (chans + hidden, hidden)]
    biases = [(0, hidden), (hidden, hidden), (2 * hidden, chans)]
    return list(zip(gains, biases))


def norm_gain(x, gain):
    centre = x - jnp.mean(x, axis=-1, keepdims=True)
    return centre * lax.rsqrt(jnp.mean(centre * centre, axis=-1, keepdims=True) + EPS_NORM) * gain


def corrector_forward(x, weights, norm_bias):
    spans = layer_spans(weights[0].shape[0], weights[0].shape[1])
    saved = []
    for k in range(3):
        (gstart, gwidth), (bstart, bwidth) = spans[k]
        h_low = norm_gain(x, 1.0 + norm_bias[0, gstart : gstart + gwidth]).astype(jnp.bfloat16)
        z_val = (
            jnp.dot(h_low, weights[k], preferred_element_type=jnp.float32)
            + norm_bias[1, bstart : bstart + bwidth]
        )
        saved.append((x, h_low, z_val))
        x = jax.nn.gelu(z_val, approximate=False) if k < 2 else z_val
    return (x, saved)


def corrector_backward(grad, saved, weights, norm_bias):
    spans = layer_spans(weights[0].shape[0], weights[0].shape[1])
    weight_grads = [None, None, None]
    gain_parts = [None, None, None]
    bias_parts = [None, None, None]
    for k in (2, 1, 0):
        (gstart, gwidth), (bstart, bwidth) = spans[k]
        x, h_low, z_val = saved[k]
        if k < 2:
            grad = jax.vjp(partial(jax.nn.gelu, approximate=False), z_val)[1](grad)[0]
        grad_low = grad.astype(jnp.bfloat16)
        weight_grads[k] = lax.dot_general(
            h_low, grad_low, (((0,), (0,)), ((), ())), preferred_element_type=jnp.float32
        )
        bias_parts[k] = jnp.sum(grad_low, axis=0, dtype=jnp.float32)
        back_h = lax.dot_general(
            grad_low, weights[k], (((1,), (1,)), ((), ())), preferred_element_type=jnp.float32
        )
        grad, gain_parts[k] = jax.vjp(norm_gain, x, 1.0 + norm_bias[0, gstart : gstart + gwidth])[
            1
        ](back_h)
    vector_grad = jnp.stack([jnp.concatenate(gain_parts), jnp.concatenate(bias_parts)])
    return (grad, (weight_grads[0], weight_grads[1], weight_grads[2], vector_grad))


def adamw(weight, mean, square, grad):
    mean_new = BETA_ONE * mean + (1.0 - BETA_ONE) * grad
    square_new = BETA_TWO * square + (1.0 - BETA_TWO) * grad * grad
    weight_new = weight - LEARN_RATE * (
        mean_new / (jnp.sqrt(square_new) + EPS_ADAM) + DECAY * weight
    )
    return (weight_new, mean_new, square_new)


def spread_device(
    spectral_state,
    legendre,
    wave_slots,
    lat_order,
    quad_weights,
    available,
    targets,
    w_first,
    w_mid,
    w_last,
    norm_bias,
    mean_first,
    mean_mid,
    mean_last,
    mean_bias,
    square_first,
    square_mid,
    square_last,
    square_bias,
):
    tdev, wdev, _, degrees, chans = spectral_state.shape
    fields = available.shape[1]
    rows_dev = available.shape[2]
    lon_count = available.shape[3]
    levels = chans // fields
    lat_index = lax.axis_index("lat")
    slots = lax.dynamic_slice_in_dim(wave_slots, lat_index * wdev, wdev)
    finv, ffw = wave_tables(wave_slots, lon_count)
    keep = (jnp.arange(degrees, dtype=jnp.int32)[None, :] >= slots[:, None]).astype(jnp.bfloat16)
    plg = jnp.take(legendre, lat_order, axis=2) * keep[:, :, None]
    qrow = jnp.take(quad_weights, lat_order)
    qlocal = lax.dynamic_slice_in_dim(qrow, lat_index * rows_dev, rows_dev)
    colw = qlocal[None, None, :, None] * available.astype(jnp.float32)
    den_part = jnp.sum(colw, axis=(2, 3))
    params = (w_first, w_mid, w_last, norm_bias)
    weights = (
        w_first.astype(jnp.bfloat16),
        w_mid.astype(jnp.bfloat16),
        w_last.astype(jnp.bfloat16),
    )

    def legendre_sum(piece):
        return jnp.einsum("mnr,tmprc->tmpnc", plg, piece, preferred_element_type=jnp.float32)

    def fourier_sum(table, piece):
        return jnp.einsum("mpk,tmprc->trkc", table, piece, preferred_element_type=jnp.float32)

    def to_grid(state):
        sums = jnp.einsum(
            "mnr,tmpnc->tmprc", plg, state.astype(jnp.bfloat16), preferred_element_type=jnp.float32
        ).astype(jnp.bfloat16)
        return fourier_sum(
            finv, lax.all_to_all(sums, "lat", split_axis=3, concat_axis=1, tiled=True)
        )

    def column_pass(grid):
        out, saved = corrector_forward(grid.reshape(-1, chans), weights, norm_bias)
        return (out.reshape(grid.shape), saved)

    states = []
    nums = []
    den_total = den_part
    state = spectral_state
    for s in range(STEPS):
        states.append(state)
        grid = to_grid(state)
        out, saved = column_pass(grid)
        pred = grid + STEP_SCALE * out
        num_part = jnp.einsum(
            "tfrk,trkfl->tf",
            colw,
            pred.reshape(tdev, rows_dev, lon_count, fields, levels),
            precision=HIGH,
        )
        num_total, den_total = lax.psum((num_part, den_part), "lat")
        nums.append(num_total)
        tend = (out * qlocal[None, :, None, None]).astype(jnp.bfloat16)
        coeff = jnp.einsum("mpk,trkc->tmprc", ffw, tend, preferred_element_type=jnp.float32).astype(
            jnp.bfloat16
        )
        spec = legendre_sum(lax.all_to_all(coeff, "lat", split_axis=1, concat_axis=3, tiled=True))
        state = state + STEP_SCALE * spec
    num_all = jnp.stack(nums)
    bias = num_all / (levels * den_total[None]) - jnp.moveaxis(targets, 1, 0)
    loss = lax.psum(jnp.sum(bias * bias) / STEPS, "tm")
    grad_bias = 2.0 * bias / (STEPS * levels * den_total[None])
    totals = tuple((jnp.zeros_like(p) for p in params))
    back_state = None
    for s in reversed(range(STEPS)):
        grid = to_grid(states[s])
        out, saved = column_pass(grid)
        scaled = jnp.moveaxis(colw * grad_bias[s][:, :, None, None], 1, 3)
        back_pred = jnp.broadcast_to(scaled[..., None], scaled.shape + (levels,)).reshape(
            grid.shape
        )
        back_out = STEP_SCALE * back_pred
        if back_state is not None:
            back_spec = (STEP_SCALE * back_state).astype(jnp.bfloat16)
            back_coeff = jnp.einsum(
                "mnr,tmpnc->tmprc", plg, back_spec, preferred_element_type=jnp.float32
            ).astype(jnp.bfloat16)
            back_tend = fourier_sum(
                ffw, lax.all_to_all(back_coeff, "lat", split_axis=3, concat_axis=1, tiled=True)
            )
            back_out = back_out + qlocal[None, :, None, None] * back_tend
        back_in, grads = corrector_backward(back_out.reshape(-1, chans), saved, weights, norm_bias)
        totals = tuple((a + b for a, b in zip(totals, grads)))
        if s > 0:
            back_grid = (back_pred + back_in.reshape(grid.shape)).astype(jnp.bfloat16)
            back_sums = jnp.einsum(
                "mpk,trkc->tmprc", finv, back_grid, preferred_element_type=jnp.float32
            ).astype(jnp.bfloat16)
            back_low = legendre_sum(
                lax.all_to_all(back_sums, "lat", split_axis=1, concat_axis=3, tiled=True)
            )
            back_state = back_low if back_state is None else back_state + back_low
    means = (mean_first, mean_mid, mean_last, mean_bias)
    squares = (square_first, square_mid, square_last, square_bias)
    grads = lax.psum(totals, ("tm", "lat"))
    grad_norm = jnp.sqrt(sum((jnp.sum(g * g) for g in grads)))
    factor = CLIP_NORM / jnp.maximum(grad_norm, CLIP_NORM)
    results = [adamw(w, a, b, g * factor) for w, a, b, g in zip(params, means, squares, grads)]
    masters = [r[0] for r in results]
    new_means = [r[1] for r in results]
    new_squares = [r[2] for r in results]
    halves = [w.astype(jnp.bfloat16) for w in masters]
    return (
        loss,
        grad_norm,
        masters[0],
        masters[1],
        masters[2],
        masters[3],
        new_means[0],
        new_means[1],
        new_means[2],
        new_means[3],
        new_squares[0],
        new_squares[1],
        new_squares[2],
        new_squares[3],
        halves[0],
        halves[1],
        halves[2],
        halves[3],
    )


F32 = jnp.float32
BF16 = jnp.bfloat16
VM = pltpu.VMEM
LANES = 128
GROUP = 2
SUB = 256
CHUNK = 32
ROWS_BLOCK = 4
VMEM_LIMIT = 10 << 20
SAVED_LIMIT = 96 << 20


Plan = namedtuple("Plan", ("group", "rows", "waves", "degrees", "steps", "fields", "chans", "hidden", "lons"))


def dot(a, b, dims=((1,), (0,))):
    return lax.dot_general(a, b, (dims, ((), ())), preferred_element_type=F32)


def norm_unit(x, eps):
    centre = x - jnp.mean(x, axis=-1, keepdims=True)
    scale = lax.rsqrt(jnp.mean(centre * centre, axis=-1, keepdims=True) + eps)
    return centre * scale, scale


def gelu_parts(z):
    arg = z * math.sqrt(0.5)
    return arg, 1.0 + lax.erf(arg)


def slope_twice(z):
    arg, cdf = gelu_parts(z)
    return cdf + (z * math.sqrt(2.0 / math.pi)) * jnp.exp2(arg * arg * -math.log2(math.e))


def wide(scale, width):
    return jnp.concatenate([scale] * (width // LANES), axis=1)


def whole(a):
    return pl.BlockSpec(a.shape, lambda *_: (0,) * len(a.shape))


def fold(v):
    return jnp.sum(v.reshape(v.shape[0] // 8, 8, v.shape[1]), axis=0)


def field_mask(fields, chans):
    lane = lax.broadcasted_iota(jnp.int32, (fields, chans), 1)
    row = lax.broadcasted_iota(jnp.int32, (fields, chans), 0) * (chans // fields)
    return (lane >= row) & (lane < row + chans // fields)


def splits(nb, chans, hidden):
    gains = [1.0 + nb[0:1, a:b] for a, b in ((0, chans), (chans, chans + hidden), (chans + hidden, chans + 2 * hidden))]
    biases = [nb[1:2, a:b] for a, b in ((0, hidden), (hidden, 2 * hidden), (2 * hidden, 2 * hidden + chans))]
    return gains, biases


def stagger(chains):
    live, waiting = [], list(chains)
    while live or waiting:
        if waiting:
            live.append(waiting.pop(0))
        for chain in list(live):
            if next(chain, live) is live:
                live.remove(chain)


def pair_rows(plan):
    return ROWS_BLOCK if plan.rows % ROWS_BLOCK == 0 else 1


def row_weight(plan, info, order, quad, row):
    return quad[order[(info[1] * 2 + info[0]) * plan.rows + row]]


def prepare_kernel(
    plan, info, slots, order, quad, got, got_o, inv, ffw, wanted, state, links, lt, avail, nums, table, ffw_t, tgt
):
    group, rows, waves, degrees, steps, fields, chans, _, _ = plan
    members = 2 * group
    core, member = info[0], info[1]
    span = waves * degrees
    mine = rows * waves
    half = fields // 2
    lats = rows * members
    leg = jnp.zeros((waves, chans), F32)
    row_of = lax.broadcasted_iota(jnp.int32, (waves, chans), 0)
    pick = lax.broadcasted_iota(jnp.int32, (8, chans), 0) == half
    for j in range(waves):
        at = pl.ds(j * degrees, degrees)
        for ref, p in ((got, core), (got_o, 1 - core)):
            hi = ref[j, 0:degrees, :].astype(F32)
            state[p, at, :] = hi + ref[j, degrees : 2 * degrees, :].astype(F32)
        tail = got[j, 2 * degrees : 2 * degrees + 8, :].astype(F32)
        line = jnp.sum(jnp.where(pick, tail, 0.0), axis=0, keepdims=True)
        leg = jnp.where(row_of == j, line, leg)
    iota = lambda d, s: lax.broadcasted_iota(jnp.int32, s, d)
    shape = (span, span)
    r0, r1 = iota(0, shape), iota(1, shape)
    expand = (iota(0, (span, waves)) // degrees == iota(1, (span, waves))).astype(F32).astype(BF16)
    rep = dot(expand, leg.astype(BF16))
    rep = jnp.where(r1 // lats == r0 % degrees, rep, 0.0).astype(BF16)
    lat_lane = jnp.zeros((8, span), jnp.int32)
    lane = iota(1, (8, span)) // waves
    for role in range(members):
        other = (member ^ (role & (group - 1))) * 2 + (core ^ (role // group))
        for r in range(rows):
            lat_lane = jnp.where(lane == role * rows + r, order[other * rows + r], lat_lane)
    wave_row = jnp.zeros(shape, jnp.int32)
    for j in range(waves):
        wave_row = jnp.where(r0 // degrees == j, slots[j], wave_row)
    choose = (r0 % lats == lat_lane[0:1, :]).astype(F32).astype(BF16)
    plg = dot(rep, choose)
    plg = jnp.where((r0 // degrees == r1 % waves) & (r0 % degrees >= wave_row), plg, 0.0)
    links[...] = plg.astype(BF16)
    lt[...] = plg[:, 0:mine].T.astype(BF16)
    spot = member * 2 + core
    den = jnp.zeros((fields, chans), F32)
    for r in range(rows):
        src = spot * rows + r
        a = got[src, 2 * degrees : 2 * degrees + 8, :].astype(F32)
        b = got_o[src, 2 * degrees : 2 * degrees + 8, :].astype(F32)
        first = jnp.where(core == 0, a, b)[0:half]
        second = jnp.where(core == 0, b, a)[0:half]
        both = jnp.concatenate([first, second], axis=0)
        avail[r] = both.astype(BF16)
        den += quad[order[src]] * both
    nums[...] = jnp.zeros_like(nums)
    nums[steps * fields :, :] = jnp.broadcast_to(jnp.sum(den, axis=1, keepdims=True), (fields, nums.shape[1]))
    table[...] = inv[...].T.astype(BF16)
    ffw_t[...] = ffw[...].T.astype(BF16)
    tgt[...] = wanted[...]


def prepare_call(plan, info, slots, order, quad, got, got_o, inv, ffw, wanted):
    group, rows, waves, degrees, steps, fields, chans, _, lons = plan
    span, mine = waves * degrees, rows * waves
    ins = [got, got_o, inv, ffw, wanted]
    shapes = [
        jax.ShapeDtypeStruct((2, span, chans), F32),
        jax.ShapeDtypeStruct((span, 2 * group * mine), BF16),
        jax.ShapeDtypeStruct((mine, span), BF16),
        jax.ShapeDtypeStruct((rows, fields, lons), BF16),
        jax.ShapeDtypeStruct(((steps + 1) * fields, LANES), F32),
        jax.ShapeDtypeStruct((lons, 2 * waves), BF16),
        jax.ShapeDtypeStruct((lons, 2 * waves), BF16),
        jax.ShapeDtypeStruct(wanted.shape, F32),
    ]
    return pl.pallas_call(
        partial(prepare_kernel, plan),
        out_shape=shapes,
        grid_spec=pltpu.PrefetchScalarGridSpec(
            num_scalar_prefetch=4,
            grid=(1,),
            in_specs=[whole(a) for a in ins],
            out_specs=[whole(a) for a in shapes],
        ),
        compiler_params=kernel_params(),
        name="prepare",
    )(info, slots, order, quad, *ins)


def kernel_params():
    return pltpu.CompilerParams(vmem_limit_bytes=VMEM_LIMIT)


def write_count(plan, step, nums_in, nums, acc):
    fields, chans = plan.fields, plan.chans
    kept = jnp.where(field_mask(fields, chans), acc, 0.0)
    nums[...] = nums_in[...]
    nums[step * fields : (step + 1) * fields, :] = jnp.broadcast_to(
        jnp.sum(kept, axis=1, keepdims=True), (fields, LANES)
    )


def weighted_sum(weights, values):
    hi = values.astype(BF16)
    lo = (values - hi.astype(F32)).astype(BF16)
    return dot(weights, hi) + dot(weights, lo)


def forward_kernel(plan, step, info, order, quad, *refs):
    group, rows, waves, _, steps, fields, chans, hidden, lons = plan
    first, last = step == 0, step == steps - 1
    rows_blk = pair_rows(plan)
    refs = list(refs)
    take = lambda: refs.pop(0)
    state, table, ffw, lt, w1, w2, w3, nb = [take() for _ in range(8)]
    if last:
        avail, nums_in = take(), take()
    if not first:
        links = take()
        pieces = [take() for _ in range(2 * group)]
    units, inners, scales = [take() for _ in range(3)]
    if last:
        nums = take()
    else:
        sums, outs, y_out = [take() for _ in range(3)]
        if not first:
            state_out = take()
    if last:
        sums, num_acc = take(), take()
    i = pl.program_id(0)

    @pl.when(i == 0)
    def _():
        for p in range(2):
            st = state[p]
            if not first:
                spec = dot(links[...], jnp.concatenate([piece[p] for piece in pieces], axis=0))
                st = st + STEP_SCALE * spec
                if not last:
                    state_out[p] = st
            sums[p] = dot(lt[...], st.astype(BF16)).astype(BF16)
        if last:
            num_acc[...] = jnp.zeros_like(num_acc)

    gains, biases = splits(nb, chans, hidden)
    spans = ((0, chans), (chans, hidden), (chans + hidden, hidden))
    weights = (w1, w2, w3)

    def row_chain(rr):
        row = i * rows_blk + rr
        at = pl.ds(pl.multiple_of(row * waves, waves), waves)
        rhs = jnp.concatenate([sums[0, at, :], sums[1, at, :]], axis=0)
        q = row_weight(plan, info, order, quad, row)
        grid = dot(table[...], rhs)
        yield
        x = [grid[c : c + CHUNK] for c in range(0, lons, CHUNK)]
        for k in range(3):
            low = []
            for n, part in enumerate(x):
                cs = pl.ds(pl.multiple_of(row * lons + n * CHUNK, CHUNK), CHUNK)
                if k:
                    part = part + biases[k - 1]
                    inners[cs, (k - 1) * hidden : k * hidden] = part
                    part = part * gelu_parts(part)[1]
                unit, scale = norm_unit(part, 4.0 * EPS_NORM if k else EPS_NORM)
                units[cs, spans[k][0] : spans[k][0] + spans[k][1]] = unit
                scales[cs, k * LANES : (k + 1) * LANES] = jnp.broadcast_to(scale, (CHUNK, LANES))
                low.append((unit * gains[k]).astype(BF16))
            yield
            z = dot(jnp.concatenate(low, axis=0), weights[k][...])
            x = [z[c : c + CHUNK] for c in range(0, lons, CHUNK)]
            yield
        if last:
            pred = grid + STEP_SCALE * (z + biases[2])
            yield
            num_acc[...] += q * weighted_sum(avail[row], pred)
        else:
            tends = []
            for n, part in enumerate(x):
                cs = pl.ds(pl.multiple_of(row * lons + n * CHUNK, CHUNK), CHUNK)
                out = part + biases[2]
                outs[cs, :] = out
                tends.append((out * q).astype(BF16))
            yield
            coeff = dot(ffw[...], jnp.concatenate(tends, axis=0)).astype(BF16)
            y_out[0, at, :] = coeff[:waves]
            y_out[1, at, :] = coeff[waves:]
        yield

    stagger([row_chain(rr) for rr in range(rows_blk)])

    if last:

        @pl.when(i == pl.num_programs(0) - 1)
        def _():
            write_count(plan, step, nums_in, nums, num_acc[...])


def step_call(kernel, name, grid, shapes, ins, scalars, work, scratch=(), aliases=None):
    cols, flops = work
    return pl.pallas_call(
        kernel,
        out_shape=shapes,
        grid_spec=pltpu.PrefetchScalarGridSpec(
            num_scalar_prefetch=len(scalars),
            grid=(grid,),
            in_specs=[pl.BlockSpec(memory_space=VM)] * len(ins),
            out_specs=[pl.BlockSpec(memory_space=VM)] * len(shapes),
            scratch_shapes=list(scratch),
        ),
        input_output_aliases=aliases or {},
        compiler_params=kernel_params(),
        cost_estimate=pl.CostEstimate(flops=cols * flops, bytes_accessed=cols * 8192, transcendentals=cols * 1024),
        name=name,
    )(*scalars, *ins)


def forward_call(plan, step, scalars, state, avail, nums, table, ffw, lt, weights, nb, links, pieces):
    group, rows, waves, _, steps, fields, chans, hidden, lons = plan
    first, last = step == 0, step == steps - 1
    rows_blk = pair_rows(plan)
    cols = rows * lons
    ins = [state, table, ffw, lt, *weights, nb]
    if last:
        ins += [avail, nums]
    if not first:
        ins += [links, *pieces]
    shapes = [VM((cols, width), F32) for width in (chans + 2 * hidden, 2 * hidden, 3 * LANES)]
    sums = (2, rows * waves, chans)
    scratch = []
    if last:
        shapes.append(VM(nums.shape, F32))
        scratch = [VM(sums, BF16), VM((fields, chans), F32)]
    else:
        shapes += [VM(sums, BF16), VM((cols, chans), F32), VM(sums, BF16)]
        if not first:
            shapes.append(VM(state.shape, F32))
    flops = 2 * hidden * (2 * chans + hidden)
    return step_call(
        partial(forward_kernel, plan, step), f"forward_{step}", rows // rows_blk, shapes, ins, scalars, (cols, flops), scratch
    )


def slopes_kernel(plan, inners, scales, slopes):
    rows, hidden, lons = plan.rows, plan.hidden, plan.lons
    i = pl.program_id(0)
    for n in range(lons // CHUNK):
        cs = pl.ds(pl.multiple_of(i * lons + n * CHUNK, CHUNK), CHUNK)
        for k in range(2):
            at = slice(k * hidden, (k + 1) * hidden)
            scale = wide(scales[cs, (k + 1) * LANES : (k + 2) * LANES], hidden)
            slopes[cs, at] = slope_twice(inners[cs, at]) * scale


def slopes_call(plan, step, inners, scales):
    work = (plan.rows * plan.lons, 16 * plan.hidden)
    return step_call(
        partial(slopes_kernel, plan), f"slopes_{step}", plan.rows, [VM(inners.shape, F32)], [inners, scales], (), work, (), {0: 0}
    )[0]


def counts_kernel(plan, step, info, order, quad, sums, outs, avail, nums_in, table, nums):
    rows, waves, fields, chans, lons = plan.rows, plan.waves, plan.fields, plan.chans, plan.lons
    acc = jnp.zeros((fields, chans), F32)
    for row in range(rows):
        at = slice(row * waves, (row + 1) * waves)
        grid = dot(table[...], jnp.concatenate([sums[0, at, :], sums[1, at, :]], axis=0))
        pred = grid + STEP_SCALE * outs[row * lons : (row + 1) * lons, :]
        acc = acc + row_weight(plan, info, order, quad, row) * weighted_sum(avail[row], pred)
    write_count(plan, step, nums_in, nums, acc)


def counts_call(plan, step, scalars, ins):
    work = (plan.rows * plan.lons, 8 * plan.chans)
    return step_call(partial(counts_kernel, plan, step), f"counts_{step}", 1, [VM(ins[3].shape, F32)], ins, scalars, work)[0]


def packed_parts(plan):
    parts, at = [], 0
    sizes = ((plan.chans, plan.hidden), (plan.hidden, plan.hidden), (plan.hidden, plan.chans))
    for which, (rows, cols) in enumerate(sizes):
        for tile in range(cols // LANES):
            parts.append((which, tile, at, rows))
            at += rows
    return parts, at


def packed_block(plan, chips):
    vectors = 2 * (plan.chans + 2 * plan.hidden) // LANES
    need = packed_parts(plan)[1] + vectors
    return -(-need // (2 * chips * 16)) * 16


def both_halves(at, rows, half):
    out, done = [], 0
    while done < rows:
        h = (at + done) // half
        n = min(rows - done, (h + 1) * half - at - done)
        out.append((h, at + done - h * half, done, n))
        done += n
    return out


def backward_kernel(plan, step, info, order, quad, *refs):
    group, rows, waves, _, steps, fields, chans, hidden, lons = plan
    first, last = step == steps - 1, step == 0
    fresh = step == steps - 2
    rows_blk = pair_rows(plan)
    members = 2 * group
    levels = chans // fields
    refs = list(refs)
    take = lambda: refs.pop(0)
    units, slopes, scales, avail, tgt, w2, w3, nb = [take() for _ in range(8)]
    counts = [take() for _ in range(members)]
    if not first:
        links, lt, ffw_t = [take() for _ in range(3)]
        pieces = [take() for _ in range(members)]
        if not fresh:
            bstate = take()
    if not last:
        w1, inv = take(), take()
    dzs = take()
    if not last:
        b_out = take()
        if not first:
            bstate_out = take()
    if first:
        loss = take()
    coef, gmask = take(), take()
    i = pl.program_id(0)

    @pl.when(i == 0)
    def _():
        def total(s):
            acc = [c[s * fields : (s + 1) * fields, :] for c in counts]
            while len(acc) > 1:
                acc = [a + b for a, b in zip(acc[::2], acc[1::2])]
            return acc[0]

        den = total(steps)
        bias_of = lambda s: total(s) / (levels * den) - tgt[s * fields : (s + 1) * fields, :]
        gb = 2.0 * bias_of(step) / (steps * levels * den)
        gb = jnp.where(field_mask(fields, chans), wide(gb, chans), 0.0)
        hi = gb.astype(BF16).astype(F32)
        gmask[...] = jnp.concatenate([hi, gb - hi], axis=0).astype(BF16)
        if first:
            sq = bias_of(0) * bias_of(0)
            for s in range(1, steps):
                sq = sq + bias_of(s) * bias_of(s)
            loss[...] = jnp.broadcast_to(jnp.sum(sq, axis=0, keepdims=True) / steps, loss.shape)
        else:
            for p in range(2):
                st = dot(links[...], jnp.concatenate([piece[p] for piece in pieces], axis=0))
                if not fresh:
                    st = bstate[p] + st
                if not last:
                    bstate_out[p] = st
                coef[p] = dot(lt[...], (STEP_SCALE * st).astype(BF16)).astype(BF16)

    gains, _ = splits(nb, chans, hidden)

    def norm_back(back, gain, unit):
        low = back * gain
        m1 = jnp.mean(low, axis=-1, keepdims=True)
        m2 = jnp.mean(low * unit, axis=-1, keepdims=True)
        return low - m1 - unit * m2

    def row_chain(rr):
        row = i * rows_blk + rr
        at = pl.ds(pl.multiple_of(row * waves, waves), waves)
        q = row_weight(plan, info, order, quad, row)
        chunks = [pl.ds(pl.multiple_of(row * lons + c, CHUNK), CHUNK) for c in range(0, lons, CHUNK)]
        cut = lambda v: [v[c : c + CHUNK] for c in range(0, lons, CHUNK)]
        av2 = jnp.concatenate([avail[row].astype(F32)] * 2, axis=0).astype(BF16)
        mask = dot(av2, gmask[...], ((0,), (0,)))
        if not first:
            tend = dot(ffw_t[...], jnp.concatenate([coef[0, at, :], coef[1, at, :]], axis=0))
        yield
        dpreds, low = [], []
        for n, (cs, part) in enumerate(zip(chunks, cut(mask))):
            dpred = q * part
            dout = STEP_SCALE * dpred
            if not first:
                dout = dout + q * cut(tend)[n]
            dpreds.append(dpred)
            low.append(dout.astype(BF16))
            dzs[cs, 2 * hidden :] = low[-1]
        yield
        for k, weight in ((2, w3), (1, w2)):
            back = dot(jnp.concatenate(low, axis=0), weight[...], ((1,), (1,)))
            yield
            low = []
            span = slice(chans + (k - 1) * hidden, chans + k * hidden)
            inner = slice((k - 1) * hidden, k * hidden)
            for cs, part in zip(chunks, cut(back)):
                dx = norm_back(part, gains[k], units[cs, span])
                low.append((dx * slopes[cs, inner]).astype(BF16))
                dzs[cs, inner] = low[-1]
            yield
        if not last:
            back = dot(jnp.concatenate(low, axis=0), w1[...], ((1,), (1,)))
            yield
            grids = []
            for n, (cs, part) in enumerate(zip(chunks, cut(back))):
                dx = norm_back(part, gains[0], units[cs, 0:chans])
                grids.append((dpreds[n] + dx * wide(scales[cs, 0:LANES], chans)).astype(BF16))
            yield
            coeff = dot(inv[...], jnp.concatenate(grids, axis=0)).astype(BF16)
            b_out[0, at, :] = coeff[:waves]
            b_out[1, at, :] = coeff[waves:]
            yield

    stagger([row_chain(rr) for rr in range(rows_blk)])


def backward_call(plan, step, scalars, saved, avail, tgt, weights, nb, counts, tables, pieces, bstate):
    group, rows, waves, degrees, steps, fields, chans, hidden, lons = plan
    first, last = step == steps - 1, step == 0
    rows_blk = pair_rows(plan)
    links, lt, ffw_t, inv = tables
    ins = [*saved, avail, tgt, *weights[1:], nb, *counts]
    if not first:
        ins += [links, lt, ffw_t, *pieces]
        if step != steps - 2:
            ins.append(bstate)
    if not last:
        ins += [weights[0], inv]
    sums = (2, rows * waves, chans)
    shapes = [VM((rows * lons, 2 * hidden + chans), BF16)]
    if not last:
        shapes.append(VM(sums, BF16))
        if not first:
            shapes.append(VM((2, waves * degrees, chans), F32))
    if first:
        shapes.append(VM((8, LANES), F32))
    flops = 2 * hidden * (2 * chans + hidden)
    return step_call(
        partial(backward_kernel, plan, step),
        f"backward_{step}",
        rows // rows_blk,
        shapes,
        ins,
        scalars,
        (rows * lons, flops),
        [VM(sums, BF16), VM((2 * fields, chans), BF16)],
    )


def grads_kernel(plan, step, info, *refs):
    _, rows, _, _, steps, _, chans, hidden, lons = plan
    first, last = step == steps - 1, step == 0
    refs = list(refs)
    take = lambda: refs.pop(0)
    units, dzs, nb = [take() for _ in range(3)]
    before = None if first else [take() for _ in range(4)]
    if last:
        weights = [take() for _ in range(3)]
        mine, send = take(), take()
    grads = [take() for _ in range(4)]
    gains, _ = splits(nb, chans, hidden)
    ins = ((0, chans), (chans, hidden), (chans + hidden, hidden))
    outs = ((0, hidden), (hidden, hidden), (2 * hidden, chans))
    for k in range(3):
        a, b = ins[k][0], outs[k][0]
        unit = slice(a, a + ins[k][1])
        slot = slice(b, b + outs[k][1])
        low = [(units[c : c + CHUNK, unit] * gains[k]).astype(BF16) for c in range(0, rows * lons, CHUNK)]
        new = dot(jnp.concatenate(low, axis=0), dzs[:, slot], ((0,), (0,)))
        bias = fold(dzs[0:CHUNK, slot].astype(F32))
        for c in range(CHUNK, rows * lons, CHUNK):
            bias = bias + fold(dzs[c : c + CHUNK, slot].astype(F32))
        if not first:
            new = before[k][...] + new
            bias = before[3][:, slot] + bias
        grads[k][...] = new
        grads[3][:, slot] = bias
    if not last:
        return
    packed = refs.pop(0)
    half = packed.shape[1]
    parts, at = packed_parts(plan)
    for which, tile, start, count in parts:
        for h, dst, src, n in both_halves(start, count, half):
            packed[h, dst : dst + n, :] = grads[which][src : src + n, tile * LANES : (tile + 1) * LANES]
    lines = []
    for k in range(3):
        prod = grads[k][...] * weights[k][...].astype(F32)
        thin = prod[:, 0:LANES]
        for tile in range(1, prod.shape[1] // LANES):
            thin = thin + prod[:, tile * LANES : (tile + 1) * LANES]
        lines.append(jnp.sum(thin.T, axis=0, keepdims=True) / gains[k])
    for line in (jnp.concatenate(lines, axis=1), jnp.sum(grads[3][...], axis=0, keepdims=True)):
        for tile in range(line.shape[1] // LANES):
            packed[1, at - half : at - half + 1, :] = line[:, tile * LANES : (tile + 1) * LANES]
            at += 1
    packed[1, at - half :, :] = jnp.zeros((2 * half - at, LANES), F32)
    mine[...] = packed[info[0]]
    send[...] = packed[1 - info[0]]


def grads_call(plan, step, chips, info, units, dzs, nb, before, weights):
    _, rows, _, _, steps, _, chans, hidden, lons = plan
    first, last = step == steps - 1, step == 0
    ins = [units, dzs, nb]
    aliases = {}
    if not first:
        ins += before
    sums = [VM(s, F32) for s in ((chans, hidden), (hidden, hidden), (hidden, chans), (8, 2 * hidden + chans))]
    if last:
        ins += weights
        half = chips * packed_block(plan, chips)
        shapes, scratch = [VM((half, LANES), F32)] * 2, [*sums, VM((2, half, LANES), F32)]
    else:
        shapes, scratch = sums, []
        if not first:
            aliases = {4 + n: n for n in range(4)}
    flops = 2 * hidden * (2 * chans + hidden)
    return step_call(
        partial(grads_kernel, plan, step), f"grads_{step}", 1, shapes, ins, (info,), (rows * lons, flops), scratch, aliases
    )


def pairs_kernel(chips, group, mine, got, loss, out):
    blk = mine.shape[0] // chips
    share = loss[...] * (1.0 / group)
    row = lax.broadcasted_iota(jnp.int32, share.shape, 0)
    high = share.astype(BF16).astype(F32)
    rest = share - high
    mid = rest.astype(BF16).astype(F32)
    lines = jnp.where(row == 0, high, jnp.where(row == 1, mid, jnp.where(row == 2, rest - mid, 0.0)))
    lines = jnp.concatenate([lines, jnp.zeros_like(lines)], axis=0).astype(BF16)
    for c in range(chips):
        at = slice(c * blk, (c + 1) * blk)
        out[c, 0:blk, :] = (mine[at, :] + got[at, :]).astype(BF16)
        out[c, blk:, :] = lines


def chips_kernel(got, out, loss):
    chips, blk = out.shape[0], out.shape[1]
    total = got[0].astype(F32)
    for c in range(1, chips):
        total = total + got[c].astype(F32)
    low = total[0:blk].astype(BF16)
    for c in range(chips):
        out[c] = low
    loss[...] = jnp.broadcast_to(jnp.sum(total[blk:], axis=0, keepdims=True), loss.shape)


def update_kernel(plan, info, part, part_o, *refs):
    params, means, squares = refs[0:4], refs[4:8], refs[8:12]
    norm = refs[12]
    masters, new_means, new_squares, halves = refs[13:17], refs[17:21], refs[21:25], refs[25:29]
    packed = refs[29]
    packed[info[0]] = part[...]
    packed[1 - info[0]] = part_o[...]
    half = packed.shape[1]
    acc = jnp.zeros((16, LANES), F32)
    for h in range(2):
        g = packed[h].astype(F32)
        acc = acc + jnp.sum((g * g).reshape(half // 16, 16, LANES), axis=0)
    total = jnp.sum(jnp.sum(acc, axis=0, keepdims=True), axis=1, keepdims=True)
    root = jnp.sqrt(jnp.broadcast_to(total, (8, LANES)))
    norm[...] = root
    factor = (CLIP_NORM / jnp.maximum(root, CLIP_NORM))[0:1, :]

    def apply(which, rs, cs, g):
        w, a, b = adamw(params[which][rs, cs], means[which][rs, cs], squares[which][rs, cs], g * factor)
        masters[which][rs, cs] = w
        new_means[which][rs, cs] = a
        new_squares[which][rs, cs] = b
        halves[which][rs, cs] = w.astype(BF16)

    parts, at = packed_parts(plan)
    for which, tile, start, count in parts:
        for h, src, dst, n in both_halves(start, count, half):
            apply(which, slice(dst, dst + n), slice(tile * LANES, (tile + 1) * LANES), packed[h, src : src + n, :].astype(F32))
    tiles = (plan.chans + 2 * plan.hidden) // LANES
    rows = packed[1, at - half : at - half + 2 * tiles, :].astype(F32)
    for tile in range(tiles):
        g = jnp.concatenate([rows[tile : tile + 1], rows[tiles + tile : tiles + tile + 1]], axis=0)
        apply(3, slice(0, 2), slice(tile * LANES, (tile + 1) * LANES), g)


def small_call(kernel, name, shapes, ins, scalars=(), scratch=()):
    return pl.pallas_call(
        kernel,
        out_shape=shapes,
        grid_spec=pltpu.PrefetchScalarGridSpec(
            num_scalar_prefetch=len(scalars),
            grid=(1,),
            in_specs=[whole(a) for a in ins],
            out_specs=[whole(a) for a in shapes],
            scratch_shapes=list(scratch),
        ),
        compiler_params=kernel_params(),
        name=name,
    )(*scalars, *ins)


def grouped_device(
    plan,
    chips,
    spectral_state,
    legendre,
    wave_slots,
    lat_order,
    quad_weights,
    available,
    targets,
    *flat,
):
    group, rows, waves, degrees, steps, fields, chans, hidden, lons = plan
    params, means, squares = flat[0:4], flat[4:8], flat[8:12]
    weights = [w.astype(BF16) for w in params[:3]]
    nb = params[3]
    tdev = spectral_state.shape[0]
    copies = waves // chips
    core = lax.axis_index("tm")
    chip = lax.axis_index("lat")
    member = chip % group
    info = jnp.stack([core, member]).astype(jnp.int32)
    swap = [(0, 1), (1, 0)]
    across = lambda a: lax.ppermute(a, "tm", swap)

    def to_members(a, fill):
        out = [a]
        bit = 1
        while bit < group:
            out += [lax.ppermute(v, "lat", [(n, n ^ bit) for n in range(waves)]) for v in out]
            bit *= 2
        away, filled = lax.optimization_barrier((out[1:], fill()))
        out = [a, *away]
        return out + [across(v) for v in out], filled

    half = fields // 2
    pad = -(2 * degrees + half + 1) % 8
    high = spectral_state[:, 0].astype(BF16)
    low = (spectral_state[:, 0] - high.astype(F32)).astype(BF16)
    seen = available[:, :, 0].reshape(tdev, 2, half, lons).astype(BF16)
    leg = jnp.broadcast_to(legendre.reshape(1, 1, 1, chans), (tdev, 2, 1, chans))
    pack = jnp.concatenate([high, low, seen, leg, jnp.zeros((tdev, 2, pad, chans), BF16)], axis=2)
    keep = lax.dynamic_index_in_dim(pack, core, axis=1, keepdims=False)
    other = across(lax.dynamic_index_in_dim(pack, 1 - core, axis=1, keepdims=False))
    times = jnp.concatenate([jnp.where(core == 0, keep, other), jnp.where(core == 0, other, keep)], axis=0)
    spread = jnp.broadcast_to(times[None, :, None], (copies, 2 * tdev, group, *times.shape[1:]))
    got = lax.all_to_all(spread.reshape(waves, *times.shape[1:]), "lat", split_axis=0, concat_axis=0, tiled=True)
    got_o = across(got)

    def table(scaled):
        product = wave_slots[:, None] * jnp.arange(lons, dtype=jnp.int32)[None, :] % lons
        phase = product.astype(F32) * (2.0 * math.pi / lons)
        inverse = jnp.concatenate([jnp.cos(phase), -jnp.sin(phase)], axis=0)
        if not scaled:
            return inverse
        scale = jnp.where(wave_slots == 0, 1.0, 2.0).astype(F32) / lons
        return inverse * jnp.concatenate([scale, scale])[:, None]

    inv32, ffw32 = table(False), table(True)
    inv, ffw = inv32.astype(BF16), ffw32.astype(BF16)
    theirs = across(targets)
    tgt_all = jnp.concatenate([jnp.where(core == 0, targets, theirs), jnp.where(core == 0, theirs, targets)], axis=0)
    tgt = lax.dynamic_index_in_dim(tgt_all, (chip // group) % (2 * tdev), axis=0, keepdims=False)
    tgt = jnp.broadcast_to(tgt.reshape(steps * fields, 1), (steps * fields, LANES))
    state, links, lt, avail, nums, inv_t, ffw_t, tgt = prepare_call(
        plan, info, wave_slots, lat_order, quad_weights, got, got_o, inv32, ffw32, tgt
    )
    scalars = (info, lat_order, quad_weights)

    saved, pieces = [], None
    for s in range(steps):
        units, inners, scales, *rest = forward_call(
            plan, s, scalars, state, avail, nums, inv_t, ffw, lt, weights, nb, links, pieces
        )
        fill = lambda: slopes_call(plan, s, inners, scales)
        if s < steps - 1:
            pieces, slopes = to_members(rest[2], fill)
            nums = counts_call(plan, s, scalars, [rest[0], rest[1], avail, nums, inv_t])
            pieces, nums = lax.optimization_barrier((pieces, nums))
            if s:
                state = rest[3]
        else:
            counts, slopes = to_members(rest[0], fill)
        saved.append((units, slopes, scales))
    before, bstate = None, None
    for s in reversed(range(steps)):
        dzs, *rest = backward_call(
            plan, s, scalars, saved[s], avail, tgt, weights, nb, counts, (links, lt, ffw_t, inv), pieces, bstate
        )
        fill = lambda: grads_call(plan, s, chips, info, saved[s][0], dzs, nb, before, weights)
        if s == 0:
            before = fill()
        else:
            pieces, before = to_members(rest[0], fill)
            if s == steps - 1:
                loss = rest[1]
            else:
                bstate = rest[1]
    mine, send = before
    blk = mine.shape[0] // chips
    groups = [[c * chips + n for n in range(chips)] for c in range(copies)]
    exchange = lambda a: lax.all_to_all(a, "lat", split_axis=0, concat_axis=0, tiled=True, axis_index_groups=groups)
    (parts,) = small_call(
        partial(pairs_kernel, chips, group),
        "pairs",
        [jax.ShapeDtypeStruct((chips, blk + 16, LANES), BF16)],
        [mine, across(send), loss],
    )
    reduced, loss = small_call(
        chips_kernel,
        "chips",
        [jax.ShapeDtypeStruct((chips, blk, LANES), BF16), jax.ShapeDtypeStruct((8, LANES), F32)],
        [exchange(parts)],
    )
    part = exchange(reduced).reshape(chips * blk, LANES)
    shapes = [jax.ShapeDtypeStruct((8, LANES), F32)]
    for kind in (F32, F32, F32, BF16):
        shapes += [jax.ShapeDtypeStruct(w.shape, kind) for w in params]
    norm, *results = small_call(
        partial(update_kernel, plan),
        "update",
        shapes,
        [part, across(part), *params, *means, *squares],
        (info,),
        [VM((2, chips * blk, LANES), BF16)],
    )
    return (loss[0, 0], norm[0, 0], *results)


def make_plan(mesh, args):
    state, legendre, _, _, _, available, targets, w_first = args[:8]
    times, waves, _, degrees, chans = state.shape
    _, fields, lats, lons = available.shape
    hidden = w_first.shape[1]
    cores, chips_all = mesh.shape["tm"], mesh.shape["lat"]
    group = GROUP
    chips = group * times
    rows, rest = divmod(lats, 2 * group)
    fits = (
        cores == 2
        and times % cores == 0
        and chips_all == waves == lats
        and waves % chips == 0
        and rest == 0
        and fields == 8
        and lons == chans == degrees * lats
        and waves % 16 == 0
        and degrees % 16 == 0
        and chans % LANES == 0
        and hidden % LANES == 0
        and lons % SUB == 0
    )
    if not fits or legendre.shape != (waves, degrees, lats):
        return None
    steps = targets.shape[1]
    if steps < 3 or steps * rows * lons * (chans + 4 * hidden + LANES) * 4 > SAVED_LIMIT:
        return None
    return Plan(group, rows, waves, degrees, steps, fields, chans, hidden, lons), chips


def solution(mesh):
    in_specs = (
        P("tm", "lat", None, None, None),
        P("lat", None, None),
        P(),
        P(),
        P(),
        P("tm", None, "lat", None),
        P("tm", None, None),
    ) + (P(),) * 12

    def run(*args):
        made = make_plan(mesh, args)
        body = spread_device if made is None else partial(grouped_device, *made)
        return jax.shard_map(body, mesh=mesh, in_specs=in_specs, out_specs=(P(),) * 18, check_vma=False)(*args)

    return run
```

```python
from collections import namedtuple
from functools import partial
import math

import jax
import jax.numpy as jnp
from jax import lax
from jax.experimental import pallas as pl
from jax.experimental.pallas import tpu as pltpu
from jax.sharding import PartitionSpec as P

STEPS = 4


EPS_NORM = 1e-05
STEP_SCALE = 0.5
CLIP_NORM = 1.0
LEARN_RATE = 0.01
BETA_ONE = 0.9
BETA_TWO = 0.95
EPS_ADAM = 1e-08
DECAY = 0.1
HIGH = lax.Precision.HIGHEST


def wave_tables(wave_slots, lon_count):
    product = wave_slots[:, None] * jnp.arange(lon_count, dtype=jnp.int32)[None, :] % lon_count
    phase = product.astype(jnp.float32) * (2.0 * math.pi / lon_count)
    inverse = jnp.stack([jnp.cos(phase), -jnp.sin(phase)], axis=1)
    scale = jnp.where(wave_slots == 0, 1.0, 2.0).astype(jnp.float32) / lon_count
    return (inverse.astype(jnp.bfloat16), (inverse * scale[:, None, None]).astype(jnp.bfloat16))


def layer_spans(chans, hidden):
    gains = [(0, chans), (chans, hidden), (chans + hidden, hidden)]
    biases = [(0, hidden), (hidden, hidden), (2 * hidden, chans)]
    return list(zip(gains, biases))


def norm_gain(x, gain):
    centre = x - jnp.mean(x, axis=-1, keepdims=True)
    return centre * lax.rsqrt(jnp.mean(centre * centre, axis=-1, keepdims=True) + EPS_NORM) * gain


def corrector_forward(x, weights, norm_bias):
    spans = layer_spans(weights[0].shape[0], weights[0].shape[1])
    saved = []
    for k in range(3):
        (gstart, gwidth), (bstart, bwidth) = spans[k]
        h_low = norm_gain(x, 1.0 + norm_bias[0, gstart : gstart + gwidth]).astype(jnp.bfloat16)
        z_val = (
            jnp.dot(h_low, weights[k], preferred_element_type=jnp.float32)
            + norm_bias[1, bstart : bstart + bwidth]
        )
        saved.append((x, h_low, z_val))
        x = jax.nn.gelu(z_val, approximate=False) if k < 2 else z_val
    return (x, saved)


def corrector_backward(grad, saved, weights, norm_bias):
    spans = layer_spans(weights[0].shape[0], weights[0].shape[1])
    weight_grads = [None, None, None]
    gain_parts = [None, None, None]
    bias_parts = [None, None, None]
    for k in (2, 1, 0):
        (gstart, gwidth), (bstart, bwidth) = spans[k]
        x, h_low, z_val = saved[k]
        if k < 2:
            grad = jax.vjp(partial(jax.nn.gelu, approximate=False), z_val)[1](grad)[0]
        grad_low = grad.astype(jnp.bfloat16)
        weight_grads[k] = lax.dot_general(
            h_low, grad_low, (((0,), (0,)), ((), ())), preferred_element_type=jnp.float32
        )
        bias_parts[k] = jnp.sum(grad_low, axis=0, dtype=jnp.float32)
        back_h = lax.dot_general(
            grad_low, weights[k], (((1,), (1,)), ((), ())), preferred_element_type=jnp.float32
        )
        grad, gain_parts[k] = jax.vjp(norm_gain, x, 1.0 + norm_bias[0, gstart : gstart + gwidth])[
            1
        ](back_h)
    vector_grad = jnp.stack([jnp.concatenate(gain_parts), jnp.concatenate(bias_parts)])
    return (grad, (weight_grads[0], weight_grads[1], weight_grads[2], vector_grad))


def adamw(weight, mean, square, grad):
    mean_new = BETA_ONE * mean + (1.0 - BETA_ONE) * grad
    square_new = BETA_TWO * square + (1.0 - BETA_TWO) * grad * grad
    weight_new = weight - LEARN_RATE * (
        mean_new / (jnp.sqrt(square_new) + EPS_ADAM) + DECAY * weight
    )
    return (weight_new, mean_new, square_new)


def spread_device(
    spectral_state,
    legendre,
    wave_slots,
    lat_order,
    quad_weights,
    available,
    targets,
    w_first,
    w_mid,
    w_last,
    norm_bias,
    mean_first,
    mean_mid,
    mean_last,
    mean_bias,
    square_first,
    square_mid,
    square_last,
    square_bias,
):
    tdev, wdev, _, degrees, chans = spectral_state.shape
    fields = available.shape[1]
    rows_dev = available.shape[2]
    lon_count = available.shape[3]
    levels = chans // fields
    lat_index = lax.axis_index("lat")
    slots = lax.dynamic_slice_in_dim(wave_slots, lat_index * wdev, wdev)
    finv, ffw = wave_tables(wave_slots, lon_count)
    keep = (jnp.arange(degrees, dtype=jnp.int32)[None, :] >= slots[:, None]).astype(jnp.bfloat16)
    plg = jnp.take(legendre, lat_order, axis=2) * keep[:, :, None]
    qrow = jnp.take(quad_weights, lat_order)
    qlocal = lax.dynamic_slice_in_dim(qrow, lat_index * rows_dev, rows_dev)
    colw = qlocal[None, None, :, None] * available.astype(jnp.float32)
    den_part = jnp.sum(colw, axis=(2, 3))
    params = (w_first, w_mid, w_last, norm_bias)
    weights = (
        w_first.astype(jnp.bfloat16),
        w_mid.astype(jnp.bfloat16),
        w_last.astype(jnp.bfloat16),
    )

    def legendre_sum(piece):
        return jnp.einsum("mnr,tmprc->tmpnc", plg, piece, preferred_element_type=jnp.float32)

    def fourier_sum(table, piece):
        return jnp.einsum("mpk,tmprc->trkc", table, piece, preferred_element_type=jnp.float32)

    def to_grid(state):
        sums = jnp.einsum(
            "mnr,tmpnc->tmprc", plg, state.astype(jnp.bfloat16), preferred_element_type=jnp.float32
        ).astype(jnp.bfloat16)
        return fourier_sum(
            finv, lax.all_to_all(sums, "lat", split_axis=3, concat_axis=1, tiled=True)
        )

    def column_pass(grid):
        out, saved = corrector_forward(grid.reshape(-1, chans), weights, norm_bias)
        return (out.reshape(grid.shape), saved)

    states = []
    nums = []
    den_total = den_part
    state = spectral_state
    for s in range(STEPS):
        states.append(state)
        grid = to_grid(state)
        out, saved = column_pass(grid)
        pred = grid + STEP_SCALE * out
        num_part = jnp.einsum(
            "tfrk,trkfl->tf",
            colw,
            pred.reshape(tdev, rows_dev, lon_count, fields, levels),
            precision=HIGH,
        )
        num_total, den_total = lax.psum((num_part, den_part), "lat")
        nums.append(num_total)
        tend = (out * qlocal[None, :, None, None]).astype(jnp.bfloat16)
        coeff = jnp.einsum("mpk,trkc->tmprc", ffw, tend, preferred_element_type=jnp.float32).astype(
            jnp.bfloat16
        )
        spec = legendre_sum(lax.all_to_all(coeff, "lat", split_axis=1, concat_axis=3, tiled=True))
        state = state + STEP_SCALE * spec
    num_all = jnp.stack(nums)
    bias = num_all / (levels * den_total[None]) - jnp.moveaxis(targets, 1, 0)
    loss = lax.psum(jnp.sum(bias * bias) / STEPS, "tm")
    grad_bias = 2.0 * bias / (STEPS * levels * den_total[None])
    totals = tuple((jnp.zeros_like(p) for p in params))
    back_state = None
    for s in reversed(range(STEPS)):
        grid = to_grid(states[s])
        out, saved = column_pass(grid)
        scaled = jnp.moveaxis(colw * grad_bias[s][:, :, None, None], 1, 3)
        back_pred = jnp.broadcast_to(scaled[..., None], scaled.shape + (levels,)).reshape(
            grid.shape
        )
        back_out = STEP_SCALE * back_pred
        if back_state is not None:
            back_spec = (STEP_SCALE * back_state).astype(jnp.bfloat16)
            back_coeff = jnp.einsum(
                "mnr,tmpnc->tmprc", plg, back_spec, preferred_element_type=jnp.float32
            ).astype(jnp.bfloat16)
            back_tend = fourier_sum(
                ffw, lax.all_to_all(back_coeff, "lat", split_axis=3, concat_axis=1, tiled=True)
            )
            back_out = back_out + qlocal[None, :, None, None] * back_tend
        back_in, grads = corrector_backward(back_out.reshape(-1, chans), saved, weights, norm_bias)
        totals = tuple((a + b for a, b in zip(totals, grads)))
        if s > 0:
            back_grid = (back_pred + back_in.reshape(grid.shape)).astype(jnp.bfloat16)
            back_sums = jnp.einsum(
                "mpk,trkc->tmprc", finv, back_grid, preferred_element_type=jnp.float32
            ).astype(jnp.bfloat16)
            back_low = legendre_sum(
                lax.all_to_all(back_sums, "lat", split_axis=1, concat_axis=3, tiled=True)
            )
            back_state = back_low if back_state is None else back_state + back_low
    means = (mean_first, mean_mid, mean_last, mean_bias)
    squares = (square_first, square_mid, square_last, square_bias)
    grads = lax.psum(totals, ("tm", "lat"))
    grad_norm = jnp.sqrt(sum((jnp.sum(g * g) for g in grads)))
    factor = CLIP_NORM / jnp.maximum(grad_norm, CLIP_NORM)
    results = [adamw(w, a, b, g * factor) for w, a, b, g in zip(params, means, squares, grads)]
    masters = [r[0] for r in results]
    new_means = [r[1] for r in results]
    new_squares = [r[2] for r in results]
    halves = [w.astype(jnp.bfloat16) for w in masters]
    return (
        loss,
        grad_norm,
        masters[0],
        masters[1],
        masters[2],
        masters[3],
        new_means[0],
        new_means[1],
        new_means[2],
        new_means[3],
        new_squares[0],
        new_squares[1],
        new_squares[2],
        new_squares[3],
        halves[0],
        halves[1],
        halves[2],
        halves[3],
    )


F32 = jnp.float32
BF16 = jnp.bfloat16
VM = pltpu.VMEM
LANES = 128
GROUP = 2
SUB = 256
CHUNK = 32
ROWS_BLOCK = 4
UPDATE_ROWS = 32
VMEM_LIMIT = 10 << 20
SAVED_LIMIT = 96 << 20


Plan = namedtuple("Plan", ("group", "rows", "waves", "degrees", "steps", "fields", "chans", "hidden", "lons"))


def dot(a, b, dims=((1,), (0,))):
    return lax.dot_general(a, b, (dims, ((), ())), preferred_element_type=F32)


def norm_unit(x, eps):
    centre = x - jnp.mean(x, axis=-1, keepdims=True)
    scale = lax.rsqrt(jnp.mean(centre * centre, axis=-1, keepdims=True) + eps)
    return centre * scale, scale


def gelu_parts(z):
    arg = z * math.sqrt(0.5)
    return arg, 1.0 + lax.erf(arg)


def slope_twice(z):
    arg, cdf = gelu_parts(z)
    return cdf + (z * math.sqrt(2.0 / math.pi)) * jnp.exp2(arg * arg * -math.log2(math.e))


def wide(scale, width):
    return jnp.concatenate([scale] * (width // LANES), axis=1)


def whole(a):
    return pl.BlockSpec(a.shape, lambda *_: (0,) * len(a.shape))


def fold(v):
    return jnp.sum(v.reshape(v.shape[0] // 8, 8, v.shape[1]), axis=0)


def field_mask(fields, chans):
    lane = lax.broadcasted_iota(jnp.int32, (fields, chans), 1)
    row = lax.broadcasted_iota(jnp.int32, (fields, chans), 0) * (chans // fields)
    return (lane >= row) & (lane < row + chans // fields)


def splits(nb, chans, hidden):
    gains = [1.0 + nb[0:1, a:b] for a, b in ((0, chans), (chans, chans + hidden), (chans + hidden, chans + 2 * hidden))]
    biases = [nb[1:2, a:b] for a, b in ((0, hidden), (hidden, 2 * hidden), (2 * hidden, 2 * hidden + chans))]
    return gains, biases


def stagger(chains):
    live, waiting = [], list(chains)
    while live or waiting:
        if waiting:
            live.append(waiting.pop(0))
        for chain in list(live):
            if next(chain, live) is live:
                live.remove(chain)


def pair_rows(plan):
    return ROWS_BLOCK if plan.rows % ROWS_BLOCK == 0 else 1


def row_weight(plan, info, order, quad, row):
    return quad[order[(info[1] * 2 + info[0]) * plan.rows + row]]


def pack_kernel(info, state_in, seen_in, legendre_in, keep, send, state, seen, legendre, sems):
    pairs = ((state_in, state), (seen_in, seen), (legendre_in, legendre))
    loads = [pltpu.make_async_copy(a, b, sems.at[n]) for n, (a, b) in enumerate(pairs)]
    for load in loads:
        load.start()
    for load in loads:
        load.wait()
    times, _, parts, degrees, chans = state.shape
    fields = seen.shape[1]
    lats = legendre.shape[2]
    iota = lambda d, s: lax.broadcasted_iota(jnp.int32, s, d)
    repeat = (iota(1, (lats, chans)) % lats == iota(0, (lats, chans))).astype(F32).astype(BF16)
    line = dot(legendre[0], repeat)
    line = jnp.where(iota(1, (degrees, chans)) // lats == iota(0, (degrees, chans)), line, 0.0)
    line = jnp.sum(line, axis=0, keepdims=True)
    half = fields // parts
    blank = jnp.zeros((keep.shape[1] - 2 * degrees - half - 1, chans), F32)
    mine = info[0] == 0
    for t in range(times):
        rows = []
        for p in range(parts):
            x = state[t, 0, p]
            hi = x.astype(BF16).astype(F32)
            there = [seen[t, f].astype(F32) for f in range(p * half, (p + 1) * half)]
            rows.append(jnp.concatenate([hi, x - hi, *there, line, blank], axis=0))
        keep[t] = jnp.where(mine, rows[0], rows[1]).astype(BF16)
        send[t] = jnp.where(mine, rows[1], rows[0]).astype(BF16)


def pack_call(info, state, seen, legendre, deep):
    times, _, _, _, chans = state.shape
    ins = [pltpu.with_memory_space_constraint(a, pltpu.HBM) for a in (state, seen, legendre)]
    return pl.pallas_call(
        pack_kernel,
        out_shape=[VM((times, deep, chans), BF16)] * 2,
        grid_spec=pltpu.PrefetchScalarGridSpec(
            num_scalar_prefetch=1,
            grid=(1,),
            in_specs=[pl.BlockSpec(memory_space=pltpu.HBM)] * 3,
            out_specs=[pl.BlockSpec(memory_space=VM)] * 2,
            scratch_shapes=[VM(a.shape, a.dtype) for a in ins] + [pltpu.SemaphoreType.DMA((3,))],
        ),
        compiler_params=kernel_params(),
        name="pack",
    )(info, *ins)


def prepare_kernel(
    plan, info, slots, order, quad, got, got_o, inv, ffw, wanted, state, links, lt, avail, nums, table, ffw_t, tgt
):
    group, rows, waves, degrees, steps, fields, chans, _, _ = plan
    members = 2 * group
    core, member = info[0], info[1]
    span = waves * degrees
    mine = rows * waves
    half = fields // 2
    lats = rows * members
    leg = jnp.zeros((waves, chans), F32)
    row_of = lax.broadcasted_iota(jnp.int32, (waves, chans), 0)
    pick = lax.broadcasted_iota(jnp.int32, (8, chans), 0) == half
    for j in range(waves):
        at = pl.ds(j * degrees, degrees)
        for ref, p in ((got, core), (got_o, 1 - core)):
            hi = ref[j, 0:degrees, :].astype(F32)
            state[p, at, :] = hi + ref[j, degrees : 2 * degrees, :].astype(F32)
        tail = got[j, 2 * degrees : 2 * degrees + 8, :].astype(F32)
        line = jnp.sum(jnp.where(pick, tail, 0.0), axis=0, keepdims=True)
        leg = jnp.where(row_of == j, line, leg)
    iota = lambda d, s: lax.broadcasted_iota(jnp.int32, s, d)
    shape = (span, span)
    r0, r1 = iota(0, shape), iota(1, shape)
    expand = (iota(0, (span, waves)) // degrees == iota(1, (span, waves))).astype(F32).astype(BF16)
    rep = dot(expand, leg.astype(BF16))
    rep = jnp.where(r1 // lats == r0 % degrees, rep, 0.0).astype(BF16)
    lat_lane = jnp.zeros((8, span), jnp.int32)
    lane = iota(1, (8, span)) // waves
    for role in range(members):
        other = (member ^ (role & (group - 1))) * 2 + (core ^ (role // group))
        for r in range(rows):
            lat_lane = jnp.where(lane == role * rows + r, order[other * rows + r], lat_lane)
    wave_row = jnp.zeros(shape, jnp.int32)
    for j in range(waves):
        wave_row = jnp.where(r0 // degrees == j, slots[j], wave_row)
    choose = (r0 % lats == lat_lane[0:1, :]).astype(F32).astype(BF16)
    plg = dot(rep, choose)
    plg = jnp.where((r0 // degrees == r1 % waves) & (r0 % degrees >= wave_row), plg, 0.0)
    links[...] = plg.astype(BF16)
    lt[...] = plg[:, 0:mine].T.astype(BF16)
    spot = member * 2 + core
    den = jnp.zeros((fields, chans), F32)
    for r in range(rows):
        src = spot * rows + r
        a = got[src, 2 * degrees : 2 * degrees + 8, :].astype(F32)
        b = got_o[src, 2 * degrees : 2 * degrees + 8, :].astype(F32)
        first = jnp.where(core == 0, a, b)[0:half]
        second = jnp.where(core == 0, b, a)[0:half]
        both = jnp.concatenate([first, second], axis=0)
        avail[r] = both.astype(BF16)
        den += quad[order[src]] * both
    nums[...] = jnp.zeros_like(nums)
    nums[steps * fields :, :] = jnp.broadcast_to(jnp.sum(den, axis=1, keepdims=True), (fields, nums.shape[1]))
    table[...] = inv[...].T.astype(BF16)
    ffw_t[...] = ffw[...].T.astype(BF16)
    tgt[...] = wanted[...]


def prepare_call(plan, info, slots, order, quad, got, got_o, inv, ffw, wanted):
    group, rows, waves, degrees, steps, fields, chans, _, lons = plan
    span, mine = waves * degrees, rows * waves
    shapes = [
        VM((2, span, chans), F32),
        VM((span, 2 * group * mine), BF16),
        VM((mine, span), BF16),
        VM((rows, fields, lons), BF16),
        VM(((steps + 1) * fields, LANES), F32),
        VM((lons, 2 * waves), BF16),
        VM((lons, 2 * waves), BF16),
        VM(wanted.shape, F32),
    ]
    ins = [got, got_o, inv, ffw, wanted]
    return step_call(partial(prepare_kernel, plan), "prepare", 1, shapes, ins, (info, slots, order, quad), (span, 2 * span))


def kernel_params():
    return pltpu.CompilerParams(vmem_limit_bytes=VMEM_LIMIT)


def write_count(plan, step, nums_in, nums, acc):
    fields, chans = plan.fields, plan.chans
    kept = jnp.where(field_mask(fields, chans), acc, 0.0)
    nums[...] = nums_in[...]
    nums[step * fields : (step + 1) * fields, :] = jnp.broadcast_to(
        jnp.sum(kept, axis=1, keepdims=True), (fields, LANES)
    )


def weighted_sum(weights, values):
    hi = values.astype(BF16)
    lo = (values - hi.astype(F32)).astype(BF16)
    return dot(weights, hi) + dot(weights, lo)


def forward_kernel(plan, step, info, order, quad, *refs):
    group, rows, waves, _, steps, fields, chans, hidden, lons = plan
    first, last = step == 0, step == steps - 1
    rows_blk = pair_rows(plan)
    refs = list(refs)
    take = lambda: refs.pop(0)
    state, table, ffw, lt, w1, w2, w3, nb = [take() for _ in range(8)]
    if last:
        avail, nums_in = take(), take()
    if not first:
        links = take()
        pieces = [take() for _ in range(2 * group)]
    units, inners, scales = [take() for _ in range(3)]
    if last:
        nums = take()
    else:
        sums, outs, y_out = [take() for _ in range(3)]
        if not first:
            state_out = take()
    if last:
        sums, num_acc = take(), take()
    i = pl.program_id(0)

    @pl.when(i == 0)
    def _():
        for p in range(2):
            st = state[p]
            if not first:
                spec = dot(links[...], jnp.concatenate([piece[p] for piece in pieces], axis=0))
                st = st + STEP_SCALE * spec
                if not last:
                    state_out[p] = st
            sums[p] = dot(lt[...], st.astype(BF16)).astype(BF16)
        if last:
            num_acc[...] = jnp.zeros_like(num_acc)

    gains, biases = splits(nb, chans, hidden)
    spans = ((0, chans), (chans, hidden), (chans + hidden, hidden))
    weights = (w1, w2, w3)

    def row_chain(rr):
        row = i * rows_blk + rr
        at = pl.ds(pl.multiple_of(row * waves, waves), waves)
        rhs = jnp.concatenate([sums[0, at, :], sums[1, at, :]], axis=0)
        q = row_weight(plan, info, order, quad, row)
        grid = dot(table[...], rhs)
        yield
        x = [grid[c : c + CHUNK] for c in range(0, lons, CHUNK)]
        for k in range(3):
            low = []
            for n, part in enumerate(x):
                cs = pl.ds(pl.multiple_of(row * lons + n * CHUNK, CHUNK), CHUNK)
                if k:
                    part = part + biases[k - 1]
                    inners[cs, (k - 1) * hidden : k * hidden] = part
                    part = part * gelu_parts(part)[1]
                unit, scale = norm_unit(part, 4.0 * EPS_NORM if k else EPS_NORM)
                units[cs, spans[k][0] : spans[k][0] + spans[k][1]] = unit
                scales[cs, k * LANES : (k + 1) * LANES] = jnp.broadcast_to(scale, (CHUNK, LANES))
                low.append((unit * gains[k]).astype(BF16))
            yield
            z = dot(jnp.concatenate(low, axis=0), weights[k][...])
            x = [z[c : c + CHUNK] for c in range(0, lons, CHUNK)]
            yield
        if last:
            pred = grid + STEP_SCALE * (z + biases[2])
            yield
            num_acc[...] += q * weighted_sum(avail[row], pred)
        else:
            tends = []
            for n, part in enumerate(x):
                cs = pl.ds(pl.multiple_of(row * lons + n * CHUNK, CHUNK), CHUNK)
                out = part + biases[2]
                outs[cs, :] = out
                tends.append((out * q).astype(BF16))
            yield
            coeff = dot(ffw[...], jnp.concatenate(tends, axis=0)).astype(BF16)
            y_out[0, at, :] = coeff[:waves]
            y_out[1, at, :] = coeff[waves:]
        yield

    stagger([row_chain(rr) for rr in range(rows_blk)])

    if last:

        @pl.when(i == pl.num_programs(0) - 1)
        def _():
            write_count(plan, step, nums_in, nums, num_acc[...])


def step_call(kernel, name, grid, shapes, ins, scalars, work, scratch=(), aliases=None):
    cols, flops = work
    return pl.pallas_call(
        kernel,
        out_shape=shapes,
        grid_spec=pltpu.PrefetchScalarGridSpec(
            num_scalar_prefetch=len(scalars),
            grid=(grid,),
            in_specs=[pl.BlockSpec(memory_space=VM)] * len(ins),
            out_specs=[pl.BlockSpec(memory_space=VM)] * len(shapes),
            scratch_shapes=list(scratch),
        ),
        input_output_aliases=aliases or {},
        compiler_params=kernel_params(),
        cost_estimate=pl.CostEstimate(flops=cols * flops, bytes_accessed=cols * 8192, transcendentals=cols * 1024),
        name=name,
    )(*scalars, *ins)


def forward_call(plan, step, scalars, state, avail, nums, table, ffw, lt, weights, nb, links, pieces):
    group, rows, waves, _, steps, fields, chans, hidden, lons = plan
    first, last = step == 0, step == steps - 1
    rows_blk = pair_rows(plan)
    cols = rows * lons
    ins = [state, table, ffw, lt, *weights, nb]
    if last:
        ins += [avail, nums]
    if not first:
        ins += [links, *pieces]
    shapes = [VM((cols, width), F32) for width in (chans + 2 * hidden, 2 * hidden, 3 * LANES)]
    sums = (2, rows * waves, chans)
    scratch = []
    if last:
        shapes.append(VM(nums.shape, F32))
        scratch = [VM(sums, BF16), VM((fields, chans), F32)]
    else:
        shapes += [VM(sums, BF16), VM((cols, chans), F32), VM(sums, BF16)]
        if not first:
            shapes.append(VM(state.shape, F32))
    flops = 2 * hidden * (2 * chans + hidden)
    return step_call(
        partial(forward_kernel, plan, step), f"forward_{step}", rows // rows_blk, shapes, ins, scalars, (cols, flops), scratch
    )


def slopes_kernel(plan, inners, scales, slopes):
    rows, hidden, lons = plan.rows, plan.hidden, plan.lons
    i = pl.program_id(0)
    for n in range(lons // CHUNK):
        cs = pl.ds(pl.multiple_of(i * lons + n * CHUNK, CHUNK), CHUNK)
        for k in range(2):
            at = slice(k * hidden, (k + 1) * hidden)
            scale = wide(scales[cs, (k + 1) * LANES : (k + 2) * LANES], hidden)
            slopes[cs, at] = slope_twice(inners[cs, at]) * scale


def slopes_call(plan, step, inners, scales):
    work = (plan.rows * plan.lons, 16 * plan.hidden)
    return step_call(
        partial(slopes_kernel, plan), f"slopes_{step}", plan.rows, [VM(inners.shape, F32)], [inners, scales], (), work, (), {0: 0}
    )[0]


def counts_kernel(plan, step, info, order, quad, sums, outs, avail, nums_in, table, nums):
    rows, waves, fields, chans, lons = plan.rows, plan.waves, plan.fields, plan.chans, plan.lons
    acc = jnp.zeros((fields, chans), F32)
    for row in range(rows):
        at = slice(row * waves, (row + 1) * waves)
        grid = dot(table[...], jnp.concatenate([sums[0, at, :], sums[1, at, :]], axis=0))
        pred = grid + STEP_SCALE * outs[row * lons : (row + 1) * lons, :]
        acc = acc + row_weight(plan, info, order, quad, row) * weighted_sum(avail[row], pred)
    write_count(plan, step, nums_in, nums, acc)


def counts_call(plan, step, scalars, ins):
    work = (plan.rows * plan.lons, 8 * plan.chans)
    return step_call(partial(counts_kernel, plan, step), f"counts_{step}", 1, [VM(ins[3].shape, F32)], ins, scalars, work)[0]


def packed_parts(plan):
    parts, at = [], 0
    sizes = ((plan.chans, plan.hidden), (plan.hidden, plan.hidden), (plan.hidden, plan.chans))
    for which, (rows, cols) in enumerate(sizes):
        for tile in range(cols // LANES):
            parts.append((which, tile, at, rows))
            at += rows
    return parts, at


def packed_block(plan, chips):
    vectors = 2 * (plan.chans + 2 * plan.hidden) // LANES
    need = packed_parts(plan)[1] + vectors
    return -(-need // (2 * chips * 16)) * 16


def both_halves(at, rows, half):
    out, done = [], 0
    while done < rows:
        h = (at + done) // half
        n = min(rows - done, (h + 1) * half - at - done)
        out.append((h, at + done - h * half, done, n))
        done += n
    return out


def shares(plan, step, counts, tgt):
    steps, fields, chans = plan.steps, plan.fields, plan.chans
    levels = chans // fields

    def total(s):
        acc = [c[s * fields : (s + 1) * fields, :] for c in counts]
        while len(acc) > 1:
            acc = [a + b for a, b in zip(acc[::2], acc[1::2])]
        return acc[0]

    den = total(steps)
    bias_of = lambda s: total(s) / (levels * den) - tgt[s * fields : (s + 1) * fields, :]
    gb = 2.0 * bias_of(step) / (steps * levels * den)
    gb = jnp.where(field_mask(fields, chans), wide(gb, chans), 0.0)
    hi = gb.astype(BF16).astype(F32)
    return jnp.concatenate([hi, gb - hi], axis=0).astype(BF16), bias_of


def spread_share(avail, gmask, row):
    av2 = jnp.concatenate([avail[row].astype(F32)] * 2, axis=0).astype(BF16)
    return dot(av2, gmask, ((0,), (0,)))


def masks_kernel(plan, step, info, order, quad, avail, tgt, *refs):
    rows, lons = plan.rows, plan.lons
    counts, out = refs[:-1], refs[-1]
    gmask, _ = shares(plan, step, counts, tgt)
    for row in range(rows):
        out[row * lons : (row + 1) * lons, :] = row_weight(plan, info, order, quad, row) * spread_share(avail, gmask, row)


def masks_call(plan, step, scalars, avail, tgt, counts):
    cols = plan.rows * plan.lons
    shapes = [VM((cols, plan.chans), F32)]
    work = (cols, 32 * plan.chans)
    return step_call(partial(masks_kernel, plan, step), f"masks_{step}", 1, shapes, [avail, tgt, *counts], scalars, work)[0]


def backward_kernel(plan, step, info, order, quad, *refs):
    group, rows, waves, _, steps, fields, chans, hidden, lons = plan
    first, last = step == steps - 1, step == 0
    fresh = step == steps - 2
    rows_blk = pair_rows(plan)
    members = 2 * group
    levels = chans // fields
    refs = list(refs)
    take = lambda: refs.pop(0)
    units, slopes, scales, w2, w3, nb = [take() for _ in range(6)]
    if first:
        avail, tgt = take(), take()
        counts = [take() for _ in range(members)]
    else:
        masks = take()
        links, lt, ffw_t = [take() for _ in range(3)]
        pieces = [take() for _ in range(members)]
        if not fresh:
            bstate = take()
    if not last:
        w1, inv = take(), take()
    dzs = take()
    if not last:
        b_out = take()
        if not first:
            bstate_out = take()
    if first:
        loss, gmask = take(), take()
    else:
        coef = take()
    i = pl.program_id(0)

    @pl.when(i == 0)
    def _():
        if first:
            gmask[...], bias_of = shares(plan, step, counts, tgt)
            sq = bias_of(0) * bias_of(0)
            for s in range(1, steps):
                sq = sq + bias_of(s) * bias_of(s)
            loss[...] = jnp.broadcast_to(jnp.sum(sq, axis=0, keepdims=True) / steps, loss.shape)
        else:
            for p in range(2):
                st = dot(links[...], jnp.concatenate([piece[p] for piece in pieces], axis=0))
                if not fresh:
                    st = bstate[p] + st
                if not last:
                    bstate_out[p] = st
                coef[p] = dot(lt[...], (STEP_SCALE * st).astype(BF16)).astype(BF16)

    gains, _ = splits(nb, chans, hidden)

    def norm_back(back, gain, unit):
        low = back * gain
        m1 = jnp.mean(low, axis=-1, keepdims=True)
        m2 = jnp.mean(low * unit, axis=-1, keepdims=True)
        return low - m1 - unit * m2

    def row_chain(rr):
        row = i * rows_blk + rr
        at = pl.ds(pl.multiple_of(row * waves, waves), waves)
        q = row_weight(plan, info, order, quad, row)
        chunks = [pl.ds(pl.multiple_of(row * lons + c, CHUNK), CHUNK) for c in range(0, lons, CHUNK)]
        cut = lambda v: [v[c : c + CHUNK] for c in range(0, lons, CHUNK)]
        if first:
            mask = cut(spread_share(avail, gmask[...], row))
        else:
            tend = dot(ffw_t[...], jnp.concatenate([coef[0, at, :], coef[1, at, :]], axis=0))
        yield
        dpreds, low = [], []
        for n, cs in enumerate(chunks):
            dpred = q * mask[n] if first else masks[cs, :]
            dout = STEP_SCALE * dpred
            if first:
                dpreds.append(dpred)
            else:
                dout = dout + q * cut(tend)[n]
            low.append(dout.astype(BF16))
            dzs[cs, 2 * hidden :] = low[-1]
        yield
        for k, weight in ((2, w3), (1, w2)):
            back = dot(jnp.concatenate(low, axis=0), weight[...], ((1,), (1,)))
            yield
            low = []
            span = slice(chans + (k - 1) * hidden, chans + k * hidden)
            inner = slice((k - 1) * hidden, k * hidden)
            for cs, part in zip(chunks, cut(back)):
                dx = norm_back(part, gains[k], units[cs, span])
                low.append((dx * slopes[cs, inner]).astype(BF16))
                dzs[cs, inner] = low[-1]
            yield
        if not last:
            back = dot(jnp.concatenate(low, axis=0), w1[...], ((1,), (1,)))
            yield
            grids = []
            for n, (cs, part) in enumerate(zip(chunks, cut(back))):
                dx = norm_back(part, gains[0], units[cs, 0:chans])
                dpred = dpreds[n] if first else masks[cs, :]
                grids.append((dpred + dx * wide(scales[cs, 0:LANES], chans)).astype(BF16))
            yield
            coeff = dot(inv[...], jnp.concatenate(grids, axis=0)).astype(BF16)
            b_out[0, at, :] = coeff[:waves]
            b_out[1, at, :] = coeff[waves:]
            yield

    stagger([row_chain(rr) for rr in range(rows_blk)])


def backward_call(plan, step, scalars, saved, wanted, weights, nb, tables, pieces, bstate):
    group, rows, waves, degrees, steps, fields, chans, hidden, lons = plan
    first, last = step == steps - 1, step == 0
    rows_blk = pair_rows(plan)
    links, lt, ffw_t, inv = tables
    ins = [*saved, *weights[1:], nb, *wanted]
    if not first:
        ins += [links, lt, ffw_t, *pieces]
        if step != steps - 2:
            ins.append(bstate)
    if not last:
        ins += [weights[0], inv]
    sums = (2, rows * waves, chans)
    shapes = [VM((rows * lons, 2 * hidden + chans), BF16)]
    if not last:
        shapes.append(VM(sums, BF16))
        if not first:
            shapes.append(VM((2, waves * degrees, chans), F32))
    if first:
        shapes.append(VM((8, LANES), F32))
    flops = 2 * hidden * (2 * chans + hidden)
    return step_call(
        partial(backward_kernel, plan, step),
        f"backward_{step}",
        rows // rows_blk,
        shapes,
        ins,
        scalars,
        (rows * lons, flops),
        [VM((2 * fields, chans), BF16) if first else VM(sums, BF16)],
    )


def grads_kernel(plan, step, info, *refs):
    _, rows, _, _, steps, _, chans, hidden, lons = plan
    first, last = step == steps - 1, step == 0
    refs = list(refs)
    take = lambda: refs.pop(0)
    units, dzs, nb = [take() for _ in range(3)]
    before = None if first else [take() for _ in range(4)]
    if last:
        weights = [take() for _ in range(3)]
        mine, send = take(), take()
    grads = [take() for _ in range(4)]
    gains, _ = splits(nb, chans, hidden)
    ins = ((0, chans), (chans, hidden), (chans + hidden, hidden))
    outs = ((0, hidden), (hidden, hidden), (2 * hidden, chans))
    for k in range(3):
        a, b = ins[k][0], outs[k][0]
        unit = slice(a, a + ins[k][1])
        slot = slice(b, b + outs[k][1])
        low = [(units[c : c + CHUNK, unit] * gains[k]).astype(BF16) for c in range(0, rows * lons, CHUNK)]
        new = dot(jnp.concatenate(low, axis=0), dzs[:, slot], ((0,), (0,)))
        bias = fold(dzs[0:CHUNK, slot].astype(F32))
        for c in range(CHUNK, rows * lons, CHUNK):
            bias = bias + fold(dzs[c : c + CHUNK, slot].astype(F32))
        if not first:
            new = before[k][...] + new
            bias = before[3][:, slot] + bias
        grads[k][...] = new
        grads[3][:, slot] = bias
    if not last:
        return
    packed = refs.pop(0)
    half = packed.shape[1]
    parts, at = packed_parts(plan)
    for which, tile, start, count in parts:
        for h, dst, src, n in both_halves(start, count, half):
            packed[h, dst : dst + n, :] = grads[which][src : src + n, tile * LANES : (tile + 1) * LANES]
    lines = []
    for k in range(3):
        prod = grads[k][...] * weights[k][...].astype(F32)
        thin = prod[:, 0:LANES]
        for tile in range(1, prod.shape[1] // LANES):
            thin = thin + prod[:, tile * LANES : (tile + 1) * LANES]
        lines.append(jnp.sum(thin.T, axis=0, keepdims=True) / gains[k])
    for line in (jnp.concatenate(lines, axis=1), jnp.sum(grads[3][...], axis=0, keepdims=True)):
        for tile in range(line.shape[1] // LANES):
            packed[1, at - half : at - half + 1, :] = line[:, tile * LANES : (tile + 1) * LANES]
            at += 1
    packed[1, at - half :, :] = jnp.zeros((2 * half - at, LANES), F32)
    mine[...] = packed[info[0]]
    send[...] = packed[1 - info[0]]


def grads_call(plan, step, chips, info, units, dzs, nb, before, weights):
    _, rows, _, _, steps, _, chans, hidden, lons = plan
    first, last = step == steps - 1, step == 0
    ins = [units, dzs, nb]
    aliases = {}
    if not first:
        ins += before
    sums = [VM(s, F32) for s in ((chans, hidden), (hidden, hidden), (hidden, chans), (8, 2 * hidden + chans))]
    if last:
        ins += weights
        half = chips * packed_block(plan, chips)
        shapes, scratch = [VM((half, LANES), F32)] * 2, [*sums, VM((2, half, LANES), F32)]
    else:
        shapes, scratch = sums, []
        if not first:
            aliases = {4 + n: n for n in range(4)}
    flops = 2 * hidden * (2 * chans + hidden)
    return step_call(
        partial(grads_kernel, plan, step), f"grads_{step}", 1, shapes, ins, (info,), (rows * lons, flops), scratch, aliases
    )


def pairs_kernel(chips, group, mine, got, loss, out):
    blk = mine.shape[0] // chips
    share = loss[...] * (1.0 / group)
    row = lax.broadcasted_iota(jnp.int32, share.shape, 0)
    high = share.astype(BF16).astype(F32)
    rest = share - high
    mid = rest.astype(BF16).astype(F32)
    lines = jnp.where(row == 0, high, jnp.where(row == 1, mid, jnp.where(row == 2, rest - mid, 0.0)))
    lines = jnp.concatenate([lines, jnp.zeros_like(lines)], axis=0).astype(BF16)
    for c in range(chips):
        at = slice(c * blk, (c + 1) * blk)
        out[c, 0:blk, :] = (mine[at, :] + got[at, :]).astype(BF16)
        out[c, blk:, :] = lines


def chips_kernel(got, out, loss):
    chips, blk = out.shape[0], out.shape[1]
    total = got[0].astype(F32)
    for c in range(1, chips):
        total = total + got[c].astype(F32)
    low = total[0:blk].astype(BF16)
    for c in range(chips):
        out[c] = low
    loss[...] = jnp.broadcast_to(jnp.sum(total[blk:], axis=0, keepdims=True), loss.shape)


def update_kernel(plan, info, part, part_o, loss, *refs):
    params, means, squares = refs[0:4], refs[4:8], refs[8:12]
    scalars = refs[12:14]
    outs = [refs[14 + 4 * k : 18 + 4 * k] for k in range(4)]
    packed, sems = refs[30], refs[31]
    stage = [refs[32 + 4 * k : 36 + 4 * k] for k in range(4)]
    ones = refs[48:50]
    packed[info[0]] = part[...]
    packed[1 - info[0]] = part_o[...]
    half = packed.shape[1]
    acc = jnp.zeros((16, LANES), F32)
    for h in range(2):
        g = packed[h].astype(F32)
        acc = acc + jnp.sum((g * g).reshape(half // 16, 16, LANES), axis=0)
    total = jnp.sum(jnp.sum(acc, axis=0, keepdims=True), axis=1, keepdims=True)
    root = jnp.sqrt(total)
    ones[0][...] = loss[0:1, 0:1]
    ones[1][...] = root
    singles = [pltpu.make_async_copy(ones[n], scalars[n], sems.at[16 + n]) for n in range(2)]
    for copy in singles:
        copy.start()
    factor = jnp.broadcast_to(CLIP_NORM / jnp.maximum(root, CLIP_NORM), (1, LANES))

    def apply(which, rs, cs, g):
        g = g * factor
        w = params[which][rs, cs]
        a = BETA_ONE * means[which][rs, cs] + (1.0 - BETA_ONE) * g
        b = BETA_TWO * squares[which][rs, cs] + (1.0 - BETA_TWO) * g * g
        w = w - LEARN_RATE * (a / (b * lax.rsqrt(b) + EPS_ADAM) + DECAY * w)
        for k, value in enumerate((w, a, b, w.astype(BF16))):
            stage[k][which][rs, cs] = value

    def copies(which):
        return [
            pltpu.make_async_copy(stage[k][which], outs[k][which], sems.at[4 * which + k]) for k in range(4)
        ]

    parts, at = packed_parts(plan)
    for n, (which, tile, start, count) in enumerate(parts):
        cs = slice(tile * LANES, (tile + 1) * LANES)
        for h, src, dst, size in both_halves(start, count, half):
            for c in range(0, size, UPDATE_ROWS):
                n_rows = min(UPDATE_ROWS, size - c)
                g = packed[h, src + c : src + c + n_rows, :].astype(F32)
                apply(which, slice(dst + c, dst + c + n_rows), cs, g)
        if n + 1 == len(parts) or parts[n + 1][0] != which:
            for copy in copies(which):
                copy.start()
    tiles = (plan.chans + 2 * plan.hidden) // LANES
    rows = packed[1, at - half : at - half + 2 * tiles, :].astype(F32)
    for tile in range(tiles):
        g = jnp.concatenate([rows[tile : tile + 1], rows[tiles + tile : tiles + tile + 1]], axis=0)
        apply(3, slice(0, 2), slice(tile * LANES, (tile + 1) * LANES), g)
    for copy in copies(3):
        copy.start()
    for copy in singles:
        copy.wait()
    for which in range(4):
        for copy in copies(which):
            copy.wait()


def update_call(plan, info, part, part_o, loss, params, means, squares):
    kinds = (F32, F32, F32, BF16)
    hbm = pl.BlockSpec(memory_space=pl.ANY)
    vmem = pl.BlockSpec(memory_space=VM)
    return pl.pallas_call(
        partial(update_kernel, plan),
        out_shape=[jax.ShapeDtypeStruct((1, 1), F32)] * 2 + [jax.ShapeDtypeStruct(w.shape, kind) for kind in kinds for w in params],
        grid_spec=pltpu.PrefetchScalarGridSpec(
            num_scalar_prefetch=1,
            grid=(1,),
            in_specs=[vmem] * 15,
            out_specs=[hbm] * 18,
            scratch_shapes=[VM((2, *part.shape), BF16), pltpu.SemaphoreType.DMA((18,))]
            + [VM(w.shape, kind) for kind in kinds for w in params]
            + [VM((1, 1), F32)] * 2,
        ),
        compiler_params=kernel_params(),
        name="update",
    )(info, part, part_o, loss, *params, *means, *squares)


def small_call(kernel, name, shapes, ins, scalars=(), scratch=()):
    return pl.pallas_call(
        kernel,
        out_shape=shapes,
        grid_spec=pltpu.PrefetchScalarGridSpec(
            num_scalar_prefetch=len(scalars),
            grid=(1,),
            in_specs=[whole(a) for a in ins],
            out_specs=[whole(a) for a in shapes],
            scratch_shapes=list(scratch),
        ),
        compiler_params=kernel_params(),
        name=name,
    )(*scalars, *ins)


def grouped_device(
    plan,
    chips,
    spectral_state,
    legendre,
    wave_slots,
    lat_order,
    quad_weights,
    available,
    targets,
    *flat,
):
    group, rows, waves, degrees, steps, fields, chans, hidden, lons = plan
    params, means, squares = flat[0:4], flat[4:8], flat[8:12]
    weights = [w.astype(BF16) for w in params[:3]]
    nb = params[3]
    tdev = spectral_state.shape[0]
    copies = waves // chips
    core = lax.axis_index("tm")
    chip = lax.axis_index("lat")
    member = chip % group
    info = jnp.stack([core, member]).astype(jnp.int32)
    swap = [(0, 1), (1, 0)]
    across = lambda a: lax.ppermute(a, "tm", swap)

    def to_members(a, fill):
        out = [a]
        bit = 1
        while bit < group:
            out += [lax.ppermute(v, "lat", [(n, n ^ bit) for n in range(waves)]) for v in out]
            bit *= 2
        away, filled = lax.optimization_barrier((out[1:], fill()))
        out = [a, *away]
        return out + [across(v) for v in out], filled

    def to_each(a, fill):
        places = [(c, n) for c in range(2) for n in range(waves)]
        out = []
        for other, m in [(c, n) for c in range(2) for n in range(group)][1:]:
            if other and not m:
                out.append(across(a))
            else:
                pairs = [(c * waves + n, (c ^ other) * waves + (n ^ m)) for c, n in places]
                out.append(lax.ppermute(a, ("tm", "lat"), pairs))
        out, filled = lax.optimization_barrier((out, fill()))
        return [a, *out], filled

    deep = -(-(2 * degrees + fields // 2 + 1) // 8) * 8
    keep, send = pack_call(info, spectral_state, available, legendre, deep)
    other = across(send)
    times = jnp.concatenate([jnp.where(core == 0, keep, other), jnp.where(core == 0, other, keep)], axis=0)
    spread = jnp.broadcast_to(times[None, :, None], (copies, 2 * tdev, group, *times.shape[1:]))
    got = lax.all_to_all(spread.reshape(waves, *times.shape[1:]), "lat", split_axis=0, concat_axis=0, tiled=True)
    got_o = across(got)

    def table(scaled):
        product = wave_slots[:, None] * jnp.arange(lons, dtype=jnp.int32)[None, :] % lons
        phase = product.astype(F32) * (2.0 * math.pi / lons)
        inverse = jnp.concatenate([jnp.cos(phase), -jnp.sin(phase)], axis=0)
        if not scaled:
            return inverse
        scale = jnp.where(wave_slots == 0, 1.0, 2.0).astype(F32) / lons
        return inverse * jnp.concatenate([scale, scale])[:, None]

    inv32, ffw32 = table(False), table(True)
    inv, ffw = inv32.astype(BF16), ffw32.astype(BF16)
    theirs = across(targets)
    tgt_all = jnp.concatenate([jnp.where(core == 0, targets, theirs), jnp.where(core == 0, theirs, targets)], axis=0)
    tgt = lax.dynamic_index_in_dim(tgt_all, (chip // group) % (2 * tdev), axis=0, keepdims=False)
    tgt = jnp.broadcast_to(tgt.reshape(steps * fields, 1), (steps * fields, LANES))
    state, links, lt, avail, nums, inv_t, ffw_t, tgt = prepare_call(
        plan, info, wave_slots, lat_order, quad_weights, got, got_o, inv32, ffw32, tgt
    )
    scalars = (info, lat_order, quad_weights)

    saved, pieces = [], None
    for s in range(steps):
        units, inners, scales, *rest = forward_call(
            plan, s, scalars, state, avail, nums, inv_t, ffw, lt, weights, nb, links, pieces
        )
        fill = lambda: slopes_call(plan, s, inners, scales)
        if s < steps - 1:
            pieces, slopes = to_members(rest[2], fill)
            nums = counts_call(plan, s, scalars, [rest[0], rest[1], avail, nums, inv_t])
            pieces, nums = lax.optimization_barrier((pieces, nums))
            if s:
                state = rest[3]
        else:
            counts, slopes = to_each(rest[0], fill)
        saved.append((units, slopes, scales))
    before, bstate = None, None
    wanted = [avail, tgt, *counts]
    for s in reversed(range(steps)):
        dzs, *rest = backward_call(plan, s, scalars, saved[s], wanted, weights, nb, (links, lt, ffw_t, inv), pieces, bstate)
        grads = lambda: grads_call(plan, s, chips, info, saved[s][0], dzs, nb, before, weights)
        if s == 0:
            before = grads()
        else:
            fill = lambda: (grads(), [masks_call(plan, s - 1, scalars, avail, tgt, counts)])
            pieces, (before, wanted) = to_members(rest[0], fill)
            if s == steps - 1:
                loss = rest[1]
            else:
                bstate = rest[1]
    mine, send = before
    blk = mine.shape[0] // chips
    groups = [[c * chips + n for n in range(chips)] for c in range(copies)]
    exchange = lambda a: lax.all_to_all(a, "lat", split_axis=0, concat_axis=0, tiled=True, axis_index_groups=groups)
    (parts,) = small_call(
        partial(pairs_kernel, chips, group),
        "pairs",
        [jax.ShapeDtypeStruct((chips, blk + 16, LANES), BF16)],
        [mine, across(send), loss],
    )
    reduced, loss = small_call(
        chips_kernel,
        "chips",
        [jax.ShapeDtypeStruct((chips, blk, LANES), BF16), jax.ShapeDtypeStruct((8, LANES), F32)],
        [exchange(parts)],
    )
    part = exchange(reduced).reshape(chips * blk, LANES)
    loss, norm, *results = update_call(plan, info, part, across(part), loss, params, means, squares)
    return (loss.reshape(()), norm.reshape(()), *results)


def make_plan(mesh, args):
    state, legendre, _, _, _, available, targets, w_first = args[:8]
    times, waves, _, degrees, chans = state.shape
    _, fields, lats, lons = available.shape
    hidden = w_first.shape[1]
    cores, chips_all = mesh.shape["tm"], mesh.shape["lat"]
    group = GROUP
    chips = group * times
    rows, rest = divmod(lats, 2 * group)
    fits = (
        cores == 2
        and times % cores == 0
        and chips_all == waves == lats
        and waves % chips == 0
        and rest == 0
        and fields == 8
        and lons == chans == degrees * lats
        and waves % 16 == 0
        and degrees % 16 == 0
        and chans % LANES == 0
        and hidden % LANES == 0
        and lons % SUB == 0
    )
    if not fits or legendre.shape != (waves, degrees, lats):
        return None
    steps = targets.shape[1]
    if steps < 3 or steps * rows * lons * (chans + 4 * hidden + LANES) * 4 > SAVED_LIMIT:
        return None
    return Plan(group, rows, waves, degrees, steps, fields, chans, hidden, lons), chips


def solution(mesh):
    in_specs = (
        P("tm", "lat", None, None, None),
        P("lat", None, None),
        P(),
        P(),
        P(),
        P("tm", None, "lat", None),
        P("tm", None, None),
    ) + (P(),) * 12

    def run(*args):
        made = make_plan(mesh, args)
        body = spread_device if made is None else partial(grouped_device, *made)
        return jax.shard_map(body, mesh=mesh, in_specs=in_specs, out_specs=(P(),) * 18, check_vma=False)(*args)

    return run
```

```python
from collections import namedtuple
from functools import partial
import math

import jax
import jax.numpy as jnp
from jax import lax
from jax.experimental import pallas as pl
from jax.experimental.pallas import tpu as pltpu
from jax.sharding import PartitionSpec as P

STEPS = 4


EPS_NORM = 1e-05
STEP_SCALE = 0.5
CLIP_NORM = 1.0
LEARN_RATE = 0.01
BETA_ONE = 0.9
BETA_TWO = 0.95
EPS_ADAM = 1e-08
DECAY = 0.1
HIGH = lax.Precision.HIGHEST


def wave_tables(wave_slots, lon_count):
    product = wave_slots[:, None] * jnp.arange(lon_count, dtype=jnp.int32)[None, :] % lon_count
    phase = product.astype(jnp.float32) * (2.0 * math.pi / lon_count)
    inverse = jnp.stack([jnp.cos(phase), -jnp.sin(phase)], axis=1)
    scale = jnp.where(wave_slots == 0, 1.0, 2.0).astype(jnp.float32) / lon_count
    return (inverse.astype(jnp.bfloat16), (inverse * scale[:, None, None]).astype(jnp.bfloat16))


def layer_spans(chans, hidden):
    gains = [(0, chans), (chans, hidden), (chans + hidden, hidden)]
    biases = [(0, hidden), (hidden, hidden), (2 * hidden, chans)]
    return list(zip(gains, biases))


def norm_gain(x, gain):
    centre = x - jnp.mean(x, axis=-1, keepdims=True)
    return centre * lax.rsqrt(jnp.mean(centre * centre, axis=-1, keepdims=True) + EPS_NORM) * gain


def corrector_forward(x, weights, norm_bias):
    spans = layer_spans(weights[0].shape[0], weights[0].shape[1])
    saved = []
    for k in range(3):
        (gstart, gwidth), (bstart, bwidth) = spans[k]
        h_low = norm_gain(x, 1.0 + norm_bias[0, gstart : gstart + gwidth]).astype(jnp.bfloat16)
        z_val = (
            jnp.dot(h_low, weights[k], preferred_element_type=jnp.float32)
            + norm_bias[1, bstart : bstart + bwidth]
        )
        saved.append((x, h_low, z_val))
        x = jax.nn.gelu(z_val, approximate=False) if k < 2 else z_val
    return (x, saved)


def corrector_backward(grad, saved, weights, norm_bias):
    spans = layer_spans(weights[0].shape[0], weights[0].shape[1])
    weight_grads = [None, None, None]
    gain_parts = [None, None, None]
    bias_parts = [None, None, None]
    for k in (2, 1, 0):
        (gstart, gwidth), (bstart, bwidth) = spans[k]
        x, h_low, z_val = saved[k]
        if k < 2:
            grad = jax.vjp(partial(jax.nn.gelu, approximate=False), z_val)[1](grad)[0]
        grad_low = grad.astype(jnp.bfloat16)
        weight_grads[k] = lax.dot_general(
            h_low, grad_low, (((0,), (0,)), ((), ())), preferred_element_type=jnp.float32
        )
        bias_parts[k] = jnp.sum(grad_low, axis=0, dtype=jnp.float32)
        back_h = lax.dot_general(
            grad_low, weights[k], (((1,), (1,)), ((), ())), preferred_element_type=jnp.float32
        )
        grad, gain_parts[k] = jax.vjp(norm_gain, x, 1.0 + norm_bias[0, gstart : gstart + gwidth])[
            1
        ](back_h)
    vector_grad = jnp.stack([jnp.concatenate(gain_parts), jnp.concatenate(bias_parts)])
    return (grad, (weight_grads[0], weight_grads[1], weight_grads[2], vector_grad))


def adamw(weight, mean, square, grad):
    mean_new = BETA_ONE * mean + (1.0 - BETA_ONE) * grad
    square_new = BETA_TWO * square + (1.0 - BETA_TWO) * grad * grad
    weight_new = weight - LEARN_RATE * (
        mean_new / (jnp.sqrt(square_new) + EPS_ADAM) + DECAY * weight
    )
    return (weight_new, mean_new, square_new)


def spread_device(
    spectral_state,
    legendre,
    wave_slots,
    lat_order,
    quad_weights,
    available,
    targets,
    w_first,
    w_mid,
    w_last,
    norm_bias,
    mean_first,
    mean_mid,
    mean_last,
    mean_bias,
    square_first,
    square_mid,
    square_last,
    square_bias,
):
    tdev, wdev, _, degrees, chans = spectral_state.shape
    fields = available.shape[1]
    rows_dev = available.shape[2]
    lon_count = available.shape[3]
    levels = chans // fields
    lat_index = lax.axis_index("lat")
    slots = lax.dynamic_slice_in_dim(wave_slots, lat_index * wdev, wdev)
    finv, ffw = wave_tables(wave_slots, lon_count)
    keep = (jnp.arange(degrees, dtype=jnp.int32)[None, :] >= slots[:, None]).astype(jnp.bfloat16)
    plg = jnp.take(legendre, lat_order, axis=2) * keep[:, :, None]
    qrow = jnp.take(quad_weights, lat_order)
    qlocal = lax.dynamic_slice_in_dim(qrow, lat_index * rows_dev, rows_dev)
    colw = qlocal[None, None, :, None] * available.astype(jnp.float32)
    den_part = jnp.sum(colw, axis=(2, 3))
    params = (w_first, w_mid, w_last, norm_bias)
    weights = (
        w_first.astype(jnp.bfloat16),
        w_mid.astype(jnp.bfloat16),
        w_last.astype(jnp.bfloat16),
    )

    def legendre_sum(piece):
        return jnp.einsum("mnr,tmprc->tmpnc", plg, piece, preferred_element_type=jnp.float32)

    def fourier_sum(table, piece):
        return jnp.einsum("mpk,tmprc->trkc", table, piece, preferred_element_type=jnp.float32)

    def to_grid(state):
        sums = jnp.einsum(
            "mnr,tmpnc->tmprc", plg, state.astype(jnp.bfloat16), preferred_element_type=jnp.float32
        ).astype(jnp.bfloat16)
        return fourier_sum(
            finv, lax.all_to_all(sums, "lat", split_axis=3, concat_axis=1, tiled=True)
        )

    def column_pass(grid):
        out, saved = corrector_forward(grid.reshape(-1, chans), weights, norm_bias)
        return (out.reshape(grid.shape), saved)

    states = []
    nums = []
    den_total = den_part
    state = spectral_state
    for s in range(STEPS):
        states.append(state)
        grid = to_grid(state)
        out, saved = column_pass(grid)
        pred = grid + STEP_SCALE * out
        num_part = jnp.einsum(
            "tfrk,trkfl->tf",
            colw,
            pred.reshape(tdev, rows_dev, lon_count, fields, levels),
            precision=HIGH,
        )
        num_total, den_total = lax.psum((num_part, den_part), "lat")
        nums.append(num_total)
        tend = (out * qlocal[None, :, None, None]).astype(jnp.bfloat16)
        coeff = jnp.einsum("mpk,trkc->tmprc", ffw, tend, preferred_element_type=jnp.float32).astype(
            jnp.bfloat16
        )
        spec = legendre_sum(lax.all_to_all(coeff, "lat", split_axis=1, concat_axis=3, tiled=True))
        state = state + STEP_SCALE * spec
    num_all = jnp.stack(nums)
    bias = num_all / (levels * den_total[None]) - jnp.moveaxis(targets, 1, 0)
    loss = lax.psum(jnp.sum(bias * bias) / STEPS, "tm")
    grad_bias = 2.0 * bias / (STEPS * levels * den_total[None])
    totals = tuple((jnp.zeros_like(p) for p in params))
    back_state = None
    for s in reversed(range(STEPS)):
        grid = to_grid(states[s])
        out, saved = column_pass(grid)
        scaled = jnp.moveaxis(colw * grad_bias[s][:, :, None, None], 1, 3)
        back_pred = jnp.broadcast_to(scaled[..., None], scaled.shape + (levels,)).reshape(
            grid.shape
        )
        back_out = STEP_SCALE * back_pred
        if back_state is not None:
            back_spec = (STEP_SCALE * back_state).astype(jnp.bfloat16)
            back_coeff = jnp.einsum(
                "mnr,tmpnc->tmprc", plg, back_spec, preferred_element_type=jnp.float32
            ).astype(jnp.bfloat16)
            back_tend = fourier_sum(
                ffw, lax.all_to_all(back_coeff, "lat", split_axis=3, concat_axis=1, tiled=True)
            )
            back_out = back_out + qlocal[None, :, None, None] * back_tend
        back_in, grads = corrector_backward(back_out.reshape(-1, chans), saved, weights, norm_bias)
        totals = tuple((a + b for a, b in zip(totals, grads)))
        if s > 0:
            back_grid = (back_pred + back_in.reshape(grid.shape)).astype(jnp.bfloat16)
            back_sums = jnp.einsum(
                "mpk,trkc->tmprc", finv, back_grid, preferred_element_type=jnp.float32
            ).astype(jnp.bfloat16)
            back_low = legendre_sum(
                lax.all_to_all(back_sums, "lat", split_axis=1, concat_axis=3, tiled=True)
            )
            back_state = back_low if back_state is None else back_state + back_low
    means = (mean_first, mean_mid, mean_last, mean_bias)
    squares = (square_first, square_mid, square_last, square_bias)
    grads = lax.psum(totals, ("tm", "lat"))
    grad_norm = jnp.sqrt(sum((jnp.sum(g * g) for g in grads)))
    factor = CLIP_NORM / jnp.maximum(grad_norm, CLIP_NORM)
    results = [adamw(w, a, b, g * factor) for w, a, b, g in zip(params, means, squares, grads)]
    masters = [r[0] for r in results]
    new_means = [r[1] for r in results]
    new_squares = [r[2] for r in results]
    halves = [w.astype(jnp.bfloat16) for w in masters]
    return (
        loss,
        grad_norm,
        masters[0],
        masters[1],
        masters[2],
        masters[3],
        new_means[0],
        new_means[1],
        new_means[2],
        new_means[3],
        new_squares[0],
        new_squares[1],
        new_squares[2],
        new_squares[3],
        halves[0],
        halves[1],
        halves[2],
        halves[3],
    )


F32 = jnp.float32
BF16 = jnp.bfloat16
VM = pltpu.VMEM
LANES = 128
GROUP = 2
SUB = 256
CHUNK = 32
ROWS_BLOCK = 4
UPDATE_ROWS = 32
VMEM_LIMIT = 10 << 20
SAVED_LIMIT = 96 << 20


Plan = namedtuple("Plan", ("group", "rows", "waves", "degrees", "steps", "fields", "chans", "hidden", "lons"))


def dot(a, b, dims=((1,), (0,))):
    return lax.dot_general(a, b, (dims, ((), ())), preferred_element_type=F32)


def norm_unit(x, eps):
    centre = x - jnp.mean(x, axis=-1, keepdims=True)
    scale = lax.rsqrt(jnp.mean(centre * centre, axis=-1, keepdims=True) + eps)
    return centre * scale, scale


def gelu_parts(z):
    arg = z * math.sqrt(0.5)
    return arg, 1.0 + lax.erf(arg)


def slope_twice(z):
    arg, cdf = gelu_parts(z)
    return cdf + (z * math.sqrt(2.0 / math.pi)) * jnp.exp2(arg * arg * -math.log2(math.e))


def wide(scale, width):
    return jnp.concatenate([scale] * (width // LANES), axis=1)


def whole(a):
    return pl.BlockSpec(a.shape, lambda *_: (0,) * len(a.shape))


def fold(v):
    return jnp.sum(v.reshape(v.shape[0] // 8, 8, v.shape[1]), axis=0)


def field_mask(fields, chans):
    lane = lax.broadcasted_iota(jnp.int32, (fields, chans), 1)
    row = lax.broadcasted_iota(jnp.int32, (fields, chans), 0) * (chans // fields)
    return (lane >= row) & (lane < row + chans // fields)


def splits(nb, chans, hidden):
    gains = [1.0 + nb[0:1, a:b] for a, b in ((0, chans), (chans, chans + hidden), (chans + hidden, chans + 2 * hidden))]
    biases = [nb[1:2, a:b] for a, b in ((0, hidden), (hidden, 2 * hidden), (2 * hidden, 2 * hidden + chans))]
    return gains, biases


def stagger(chains):
    live, waiting = [], list(chains)
    while live or waiting:
        if waiting:
            live.append(waiting.pop(0))
        for chain in list(live):
            if next(chain, live) is live:
                live.remove(chain)


def pair_rows(plan):
    return ROWS_BLOCK if plan.rows % ROWS_BLOCK == 0 else 1


def row_weight(plan, info, order, quad, row):
    return quad[order[(info[1] * 2 + info[0]) * plan.rows + row]]


def pack_kernel(info, state_in, seen_in, legendre_in, keep, send, state, seen, legendre, sems):
    pairs = ((state_in, state), (seen_in, seen), (legendre_in, legendre))
    loads = [pltpu.make_async_copy(a, b, sems.at[n]) for n, (a, b) in enumerate(pairs)]
    for load in loads:
        load.start()
    for load in loads:
        load.wait()
    times, _, parts, degrees, chans = state.shape
    fields = seen.shape[1]
    lats = legendre.shape[2]
    iota = lambda d, s: lax.broadcasted_iota(jnp.int32, s, d)
    repeat = (iota(1, (lats, chans)) % lats == iota(0, (lats, chans))).astype(F32).astype(BF16)
    line = dot(legendre[0], repeat)
    line = jnp.where(iota(1, (degrees, chans)) // lats == iota(0, (degrees, chans)), line, 0.0)
    line = jnp.sum(line, axis=0, keepdims=True)
    half = fields // parts
    blank = jnp.zeros((keep.shape[1] - 2 * degrees - half - 1, chans), F32)
    mine = info[0] == 0
    for t in range(times):
        rows = []
        for p in range(parts):
            x = state[t, 0, p]
            hi = x.astype(BF16).astype(F32)
            there = [seen[t, f].astype(F32) for f in range(p * half, (p + 1) * half)]
            rows.append(jnp.concatenate([hi, x - hi, *there, line, blank], axis=0))
        keep[t] = jnp.where(mine, rows[0], rows[1]).astype(BF16)
        send[t] = jnp.where(mine, rows[1], rows[0]).astype(BF16)


def pack_call(info, state, seen, legendre, deep):
    times, _, _, _, chans = state.shape
    ins = [pltpu.with_memory_space_constraint(a, pltpu.HBM) for a in (state, seen, legendre)]
    return pl.pallas_call(
        pack_kernel,
        out_shape=[VM((times, deep, chans), BF16)] * 2,
        grid_spec=pltpu.PrefetchScalarGridSpec(
            num_scalar_prefetch=1,
            grid=(1,),
            in_specs=[pl.BlockSpec(memory_space=pltpu.HBM)] * 3,
            out_specs=[pl.BlockSpec(memory_space=VM)] * 2,
            scratch_shapes=[VM(a.shape, a.dtype) for a in ins] + [pltpu.SemaphoreType.DMA((3,))],
        ),
        compiler_params=kernel_params(),
        name="pack",
    )(info, *ins)


def unpack_state(plan, ref, p, state):
    waves, degrees = plan.waves, plan.degrees
    for j in range(waves):
        high = ref[j, 0:degrees, :].astype(F32)
        state[p, pl.ds(j * degrees, degrees), :] = high + ref[j, degrees : 2 * degrees, :].astype(F32)


def links_kernel(plan, info, slots, order, got, inv, ffw, wanted, state, links, lt, table, ffw_t, tgt):
    group, rows, waves, degrees, _, fields, chans, _, _ = plan
    members = 2 * group
    core, member = info[0], info[1]
    span = waves * degrees
    mine = rows * waves
    half = fields // 2
    lats = rows * members
    leg = jnp.zeros((waves, chans), F32)
    row_of = lax.broadcasted_iota(jnp.int32, (waves, chans), 0)
    pick = lax.broadcasted_iota(jnp.int32, (8, chans), 0) == half
    unpack_state(plan, got, core, state)
    for j in range(waves):
        tail = got[j, 2 * degrees : 2 * degrees + 8, :].astype(F32)
        line = jnp.sum(jnp.where(pick, tail, 0.0), axis=0, keepdims=True)
        leg = jnp.where(row_of == j, line, leg)
    iota = lambda d, s: lax.broadcasted_iota(jnp.int32, s, d)
    shape = (span, span)
    r0, r1 = iota(0, shape), iota(1, shape)
    expand = (iota(0, (span, waves)) // degrees == iota(1, (span, waves))).astype(F32).astype(BF16)
    rep = dot(expand, leg.astype(BF16))
    rep = jnp.where(r1 // lats == r0 % degrees, rep, 0.0).astype(BF16)
    lat_lane = jnp.zeros((8, span), jnp.int32)
    lane = iota(1, (8, span)) // waves
    for role in range(members):
        other = (member ^ (role & (group - 1))) * 2 + (core ^ (role // group))
        for r in range(rows):
            lat_lane = jnp.where(lane == role * rows + r, order[other * rows + r], lat_lane)
    wave_row = jnp.zeros(shape, jnp.int32)
    for j in range(waves):
        wave_row = jnp.where(r0 // degrees == j, slots[j], wave_row)
    choose = (r0 % lats == lat_lane[0:1, :]).astype(F32).astype(BF16)
    plg = dot(rep, choose)
    plg = jnp.where((r0 // degrees == r1 % waves) & (r0 % degrees >= wave_row), plg, 0.0)
    links[...] = plg.astype(BF16)
    lt[...] = plg[:, 0:mine].T.astype(BF16)
    table[...] = inv[...].T.astype(BF16)
    ffw_t[...] = ffw[...].T.astype(BF16)
    tgt[...] = wanted[...]


def fields_kernel(plan, info, order, quad, held, got, got_o, state, avail, nums):
    _, rows, _, degrees, steps, fields, chans, _, _ = plan
    core, member = info[0], info[1]
    half = fields // 2
    unpack_state(plan, got_o, 1 - core, state)
    spot = member * 2 + core
    den = jnp.zeros((fields, chans), F32)
    for r in range(rows):
        src = spot * rows + r
        a = got[src, 2 * degrees : 2 * degrees + 8, :].astype(F32)
        b = got_o[src, 2 * degrees : 2 * degrees + 8, :].astype(F32)
        first = jnp.where(core == 0, a, b)[0:half]
        second = jnp.where(core == 0, b, a)[0:half]
        both = jnp.concatenate([first, second], axis=0)
        avail[r] = both.astype(BF16)
        den += quad[order[src]] * both
    nums[...] = jnp.zeros_like(nums)
    nums[steps * fields :, :] = jnp.broadcast_to(jnp.sum(den, axis=1, keepdims=True), (fields, nums.shape[1]))


def links_call(plan, info, slots, order, got, inv, ffw, wanted):
    group, rows, waves, degrees, _, _, chans, _, lons = plan
    span, mine = waves * degrees, rows * waves
    shapes = [
        VM((2, span, chans), F32),
        VM((span, 2 * group * mine), BF16),
        VM((mine, span), BF16),
        VM((lons, 2 * waves), BF16),
        VM((lons, 2 * waves), BF16),
        VM(wanted.shape, F32),
    ]
    return step_call(
        partial(links_kernel, plan), "links", 1, shapes, [got, inv, ffw, wanted], (info, slots, order), (span, 2 * span)
    )


def fields_call(plan, scalars, state, got, got_o):
    shapes = [
        VM(state.shape, F32),
        VM((plan.rows, plan.fields, plan.lons), BF16),
        VM(((plan.steps + 1) * plan.fields, LANES), F32),
    ]
    work = (plan.waves * plan.degrees, 8)
    return step_call(partial(fields_kernel, plan), "fields", 1, shapes, [state, got, got_o], scalars, work, (), {3: 0})


def kernel_params():
    return pltpu.CompilerParams(vmem_limit_bytes=VMEM_LIMIT)


def write_count(plan, step, nums_in, nums, acc):
    fields, chans = plan.fields, plan.chans
    kept = jnp.where(field_mask(fields, chans), acc, 0.0)
    nums[...] = nums_in[...]
    nums[step * fields : (step + 1) * fields, :] = jnp.broadcast_to(
        jnp.sum(kept, axis=1, keepdims=True), (fields, LANES)
    )


def weighted_sum(weights, values):
    hi = values.astype(BF16)
    lo = (values - hi.astype(F32)).astype(BF16)
    return dot(weights, hi) + dot(weights, lo)


def forward_kernel(plan, step, info, order, quad, *refs):
    group, rows, waves, _, steps, fields, chans, hidden, lons = plan
    first, last = step == 0, step == steps - 1
    rows_blk = pair_rows(plan)
    refs = list(refs)
    take = lambda: refs.pop(0)
    state, table, ffw, lt, w1, w2, w3, nb = [take() for _ in range(8)]
    if last:
        avail, nums_in = take(), take()
    if not first:
        links = take()
        pieces = [take() for _ in range(2 * group)]
    units, inners, scales = [take() for _ in range(3)]
    if last:
        nums = take()
    else:
        sums, outs, y_out = [take() for _ in range(3)]
        if not first:
            state_out = take()
    if last:
        sums, num_acc = take(), take()
    i = pl.program_id(0)

    @pl.when(i == 0)
    def _():
        for p in range(2):
            st = state[p]
            if not first:
                spec = dot(links[...], jnp.concatenate([piece[p] for piece in pieces], axis=0))
                st = st + STEP_SCALE * spec
                if not last:
                    state_out[p] = st
            sums[p] = dot(lt[...], st.astype(BF16)).astype(BF16)
        if last:
            num_acc[...] = jnp.zeros_like(num_acc)

    gains, biases = splits(nb, chans, hidden)
    spans = ((0, chans), (chans, hidden), (chans + hidden, hidden))
    weights = (w1, w2, w3)

    def row_chain(rr):
        row = i * rows_blk + rr
        at = pl.ds(pl.multiple_of(row * waves, waves), waves)
        rhs = jnp.concatenate([sums[0, at, :], sums[1, at, :]], axis=0)
        q = row_weight(plan, info, order, quad, row)
        grid = dot(table[...], rhs)
        yield
        x = [grid[c : c + CHUNK] for c in range(0, lons, CHUNK)]
        for k in range(3):
            low = []
            for n, part in enumerate(x):
                cs = pl.ds(pl.multiple_of(row * lons + n * CHUNK, CHUNK), CHUNK)
                if k:
                    part = part + biases[k - 1]
                    inners[cs, (k - 1) * hidden : k * hidden] = part
                    part = part * gelu_parts(part)[1]
                unit, scale = norm_unit(part, 4.0 * EPS_NORM if k else EPS_NORM)
                units[cs, spans[k][0] : spans[k][0] + spans[k][1]] = unit
                scales[cs, k * LANES : (k + 1) * LANES] = jnp.broadcast_to(scale, (CHUNK, LANES))
                low.append((unit * gains[k]).astype(BF16))
            yield
            z = dot(jnp.concatenate(low, axis=0), weights[k][...])
            x = [z[c : c + CHUNK] for c in range(0, lons, CHUNK)]
            yield
        if last:
            pred = grid + STEP_SCALE * (z + biases[2])
            yield
            num_acc[...] += q * weighted_sum(avail[row], pred)
        else:
            tends = []
            for n, part in enumerate(x):
                cs = pl.ds(pl.multiple_of(row * lons + n * CHUNK, CHUNK), CHUNK)
                out = part + biases[2]
                outs[cs, :] = out
                tends.append((out * q).astype(BF16))
            yield
            coeff = dot(ffw[...], jnp.concatenate(tends, axis=0)).astype(BF16)
            y_out[0, at, :] = coeff[:waves]
            y_out[1, at, :] = coeff[waves:]
        yield

    stagger([row_chain(rr) for rr in range(rows_blk)])

    if last:

        @pl.when(i == pl.num_programs(0) - 1)
        def _():
            write_count(plan, step, nums_in, nums, num_acc[...])


def step_call(kernel, name, grid, shapes, ins, scalars, work, scratch=(), aliases=None):
    cols, flops = work
    return pl.pallas_call(
        kernel,
        out_shape=shapes,
        grid_spec=pltpu.PrefetchScalarGridSpec(
            num_scalar_prefetch=len(scalars),
            grid=(grid,),
            in_specs=[pl.BlockSpec(memory_space=VM)] * len(ins),
            out_specs=[pl.BlockSpec(memory_space=VM)] * len(shapes),
            scratch_shapes=list(scratch),
        ),
        input_output_aliases=aliases or {},
        compiler_params=kernel_params(),
        cost_estimate=pl.CostEstimate(flops=cols * flops, bytes_accessed=cols * 8192, transcendentals=cols * 1024),
        name=name,
    )(*scalars, *ins)


def forward_call(plan, step, scalars, state, avail, nums, table, ffw, lt, weights, nb, links, pieces):
    group, rows, waves, _, steps, fields, chans, hidden, lons = plan
    first, last = step == 0, step == steps - 1
    rows_blk = pair_rows(plan)
    cols = rows * lons
    ins = [state, table, ffw, lt, *weights, nb]
    if last:
        ins += [avail, nums]
    if not first:
        ins += [links, *pieces]
    shapes = [VM((cols, width), F32) for width in (chans + 2 * hidden, 2 * hidden, 3 * LANES)]
    sums = (2, rows * waves, chans)
    scratch = []
    if last:
        shapes.append(VM(nums.shape, F32))
        scratch = [VM(sums, BF16), VM((fields, chans), F32)]
    else:
        shapes += [VM(sums, BF16), VM((cols, chans), F32), VM(sums, BF16)]
        if not first:
            shapes.append(VM(state.shape, F32))
    flops = 2 * hidden * (2 * chans + hidden)
    return step_call(
        partial(forward_kernel, plan, step), f"forward_{step}", rows // rows_blk, shapes, ins, scalars, (cols, flops), scratch
    )


def slopes_kernel(plan, inners, scales, slopes):
    rows, hidden, lons = plan.rows, plan.hidden, plan.lons
    i = pl.program_id(0)
    for n in range(lons // CHUNK):
        cs = pl.ds(pl.multiple_of(i * lons + n * CHUNK, CHUNK), CHUNK)
        for k in range(2):
            at = slice(k * hidden, (k + 1) * hidden)
            scale = wide(scales[cs, (k + 1) * LANES : (k + 2) * LANES], hidden)
            slopes[cs, at] = slope_twice(inners[cs, at]) * scale


def slopes_call(plan, step, inners, scales):
    work = (plan.rows * plan.lons, 16 * plan.hidden)
    return step_call(
        partial(slopes_kernel, plan), f"slopes_{step}", plan.rows, [VM(inners.shape, F32)], [inners, scales], (), work, (), {0: 0}
    )[0]


def counts_kernel(plan, step, info, order, quad, sums, outs, avail, nums_in, table, nums):
    rows, waves, fields, chans, lons = plan.rows, plan.waves, plan.fields, plan.chans, plan.lons
    acc = jnp.zeros((fields, chans), F32)
    for row in range(rows):
        at = slice(row * waves, (row + 1) * waves)
        grid = dot(table[...], jnp.concatenate([sums[0, at, :], sums[1, at, :]], axis=0))
        pred = grid + STEP_SCALE * outs[row * lons : (row + 1) * lons, :]
        acc = acc + row_weight(plan, info, order, quad, row) * weighted_sum(avail[row], pred)
    write_count(plan, step, nums_in, nums, acc)


def counts_call(plan, step, scalars, ins):
    work = (plan.rows * plan.lons, 8 * plan.chans)
    return step_call(partial(counts_kernel, plan, step), f"counts_{step}", 1, [VM(ins[3].shape, F32)], ins, scalars, work)[0]


def packed_parts(plan):
    parts, at = [], 0
    sizes = ((plan.chans, plan.hidden), (plan.hidden, plan.hidden), (plan.hidden, plan.chans))
    for which, (rows, cols) in enumerate(sizes):
        for tile in range(cols // LANES):
            parts.append((which, tile, at, rows))
            at += rows
    return parts, at


def packed_block(plan, chips):
    vectors = 2 * (plan.chans + 2 * plan.hidden) // LANES
    need = packed_parts(plan)[1] + vectors
    return -(-need // (2 * chips * 16)) * 16


def both_halves(at, rows, half):
    out, done = [], 0
    while done < rows:
        h = (at + done) // half
        n = min(rows - done, (h + 1) * half - at - done)
        out.append((h, at + done - h * half, done, n))
        done += n
    return out


def shares(plan, step, counts, tgt):
    steps, fields, chans = plan.steps, plan.fields, plan.chans
    levels = chans // fields

    def total(s):
        acc = [c[s * fields : (s + 1) * fields, :] for c in counts]
        while len(acc) > 1:
            acc = [a + b for a, b in zip(acc[::2], acc[1::2])]
        return acc[0]

    den = total(steps)
    bias_of = lambda s: total(s) / (levels * den) - tgt[s * fields : (s + 1) * fields, :]
    gb = 2.0 * bias_of(step) / (steps * levels * den)
    gb = jnp.where(field_mask(fields, chans), wide(gb, chans), 0.0)
    hi = gb.astype(BF16).astype(F32)
    return jnp.concatenate([hi, gb - hi], axis=0).astype(BF16), bias_of


def spread_share(avail, gmask, row):
    av2 = jnp.concatenate([avail[row].astype(F32)] * 2, axis=0).astype(BF16)
    return dot(av2, gmask, ((0,), (0,)))


def masks_kernel(plan, step, info, order, quad, avail, tgt, *refs):
    rows, lons = plan.rows, plan.lons
    counts, out = refs[:-1], refs[-1]
    gmask, _ = shares(plan, step, counts, tgt)
    for row in range(rows):
        out[row * lons : (row + 1) * lons, :] = row_weight(plan, info, order, quad, row) * spread_share(avail, gmask, row)


def masks_call(plan, step, scalars, avail, tgt, counts):
    cols = plan.rows * plan.lons
    shapes = [VM((cols, plan.chans), F32)]
    work = (cols, 32 * plan.chans)
    return step_call(partial(masks_kernel, plan, step), f"masks_{step}", 1, shapes, [avail, tgt, *counts], scalars, work)[0]


def backward_kernel(plan, step, info, order, quad, *refs):
    group, rows, waves, _, steps, fields, chans, hidden, lons = plan
    first, last = step == steps - 1, step == 0
    fresh = step == steps - 2
    rows_blk = pair_rows(plan)
    members = 2 * group
    levels = chans // fields
    refs = list(refs)
    take = lambda: refs.pop(0)
    units, slopes, scales, w2, w3, nb = [take() for _ in range(6)]
    if first:
        avail, tgt = take(), take()
        counts = [take() for _ in range(members)]
    else:
        masks = take()
        links, lt, ffw_t = [take() for _ in range(3)]
        pieces = [take() for _ in range(members)]
        if not fresh:
            bstate = take()
    if not last:
        w1, inv = take(), take()
    dzs = take()
    if not last:
        b_out = take()
        if not first:
            bstate_out = take()
    if first:
        loss, gmask = take(), take()
    else:
        coef = take()
    i = pl.program_id(0)

    @pl.when(i == 0)
    def _():
        if first:
            gmask[...], bias_of = shares(plan, step, counts, tgt)
            sq = bias_of(0) * bias_of(0)
            for s in range(1, steps):
                sq = sq + bias_of(s) * bias_of(s)
            loss[...] = jnp.broadcast_to(jnp.sum(sq, axis=0, keepdims=True) / steps, loss.shape)
        else:
            for p in range(2):
                st = dot(links[...], jnp.concatenate([piece[p] for piece in pieces], axis=0))
                if not fresh:
                    st = bstate[p] + st
                if not last:
                    bstate_out[p] = st
                coef[p] = dot(lt[...], (STEP_SCALE * st).astype(BF16)).astype(BF16)

    gains, _ = splits(nb, chans, hidden)

    def norm_back(back, gain, unit):
        low = back * gain
        m1 = jnp.mean(low, axis=-1, keepdims=True)
        m2 = jnp.mean(low * unit, axis=-1, keepdims=True)
        return low - m1 - unit * m2

    def row_chain(rr):
        row = i * rows_blk + rr
        at = pl.ds(pl.multiple_of(row * waves, waves), waves)
        q = row_weight(plan, info, order, quad, row)
        chunks = [pl.ds(pl.multiple_of(row * lons + c, CHUNK), CHUNK) for c in range(0, lons, CHUNK)]
        cut = lambda v: [v[c : c + CHUNK] for c in range(0, lons, CHUNK)]
        if first:
            mask = cut(spread_share(avail, gmask[...], row))
        else:
            tend = dot(ffw_t[...], jnp.concatenate([coef[0, at, :], coef[1, at, :]], axis=0))
        yield
        dpreds, low = [], []
        for n, cs in enumerate(chunks):
            dpred = q * mask[n] if first else masks[cs, :]
            dout = STEP_SCALE * dpred
            if first:
                dpreds.append(dpred)
            else:
                dout = dout + q * cut(tend)[n]
            low.append(dout.astype(BF16))
            dzs[cs, 2 * hidden :] = low[-1]
        yield
        for k, weight in ((2, w3), (1, w2)):
            back = dot(jnp.concatenate(low, axis=0), weight[...], ((1,), (1,)))
            yield
            low = []
            span = slice(chans + (k - 1) * hidden, chans + k * hidden)
            inner = slice((k - 1) * hidden, k * hidden)
            for cs, part in zip(chunks, cut(back)):
                dx = norm_back(part, gains[k], units[cs, span])
                low.append((dx * slopes[cs, inner]).astype(BF16))
                dzs[cs, inner] = low[-1]
            yield
        if not last:
            back = dot(jnp.concatenate(low, axis=0), w1[...], ((1,), (1,)))
            yield
            grids = []
            for n, (cs, part) in enumerate(zip(chunks, cut(back))):
                dx = norm_back(part, gains[0], units[cs, 0:chans])
                dpred = dpreds[n] if first else masks[cs, :]
                grids.append((dpred + dx * wide(scales[cs, 0:LANES], chans)).astype(BF16))
            yield
            coeff = dot(inv[...], jnp.concatenate(grids, axis=0)).astype(BF16)
            b_out[0, at, :] = coeff[:waves]
            b_out[1, at, :] = coeff[waves:]
            yield

    stagger([row_chain(rr) for rr in range(rows_blk)])


def backward_call(plan, step, scalars, saved, wanted, weights, nb, tables, pieces, bstate):
    group, rows, waves, degrees, steps, fields, chans, hidden, lons = plan
    first, last = step == steps - 1, step == 0
    rows_blk = pair_rows(plan)
    links, lt, ffw_t, inv = tables
    ins = [*saved, *weights[1:], nb, *wanted]
    if not first:
        ins += [links, lt, ffw_t, *pieces]
        if step != steps - 2:
            ins.append(bstate)
    if not last:
        ins += [weights[0], inv]
    sums = (2, rows * waves, chans)
    shapes = [VM((rows * lons, 2 * hidden + chans), BF16)]
    if not last:
        shapes.append(VM(sums, BF16))
        if not first:
            shapes.append(VM((2, waves * degrees, chans), F32))
    if first:
        shapes.append(VM((8, LANES), F32))
    flops = 2 * hidden * (2 * chans + hidden)
    return step_call(
        partial(backward_kernel, plan, step),
        f"backward_{step}",
        rows // rows_blk,
        shapes,
        ins,
        scalars,
        (rows * lons, flops),
        [VM((2 * fields, chans), BF16) if first else VM(sums, BF16)],
    )


def grads_kernel(plan, step, info, *refs):
    _, rows, _, _, steps, _, chans, hidden, lons = plan
    first, last = step == steps - 1, step == 0
    refs = list(refs)
    take = lambda: refs.pop(0)
    units, dzs, nb = [take() for _ in range(3)]
    before = None if first else [take() for _ in range(4)]
    if last:
        weights = [take() for _ in range(3)]
        mine, send = take(), take()
    grads = [take() for _ in range(4)]
    gains, _ = splits(nb, chans, hidden)
    ins = ((0, chans), (chans, hidden), (chans + hidden, hidden))
    outs = ((0, hidden), (hidden, hidden), (2 * hidden, chans))
    for k in range(3):
        a, b = ins[k][0], outs[k][0]
        unit = slice(a, a + ins[k][1])
        slot = slice(b, b + outs[k][1])
        low = [(units[c : c + CHUNK, unit] * gains[k]).astype(BF16) for c in range(0, rows * lons, CHUNK)]
        new = dot(jnp.concatenate(low, axis=0), dzs[:, slot], ((0,), (0,)))
        bias = fold(dzs[0:CHUNK, slot].astype(F32))
        for c in range(CHUNK, rows * lons, CHUNK):
            bias = bias + fold(dzs[c : c + CHUNK, slot].astype(F32))
        if not first:
            new = before[k][...] + new
            bias = before[3][:, slot] + bias
        grads[k][...] = new
        grads[3][:, slot] = bias
    if not last:
        return
    half = mine.shape[0]
    parts, at = packed_parts(plan)
    lines = []
    for k in range(3):
        prod = grads[k][...] * weights[k][...].astype(F32)
        thin = prod[:, 0:LANES]
        for tile in range(1, prod.shape[1] // LANES):
            thin = thin + prod[:, tile * LANES : (tile + 1) * LANES]
        lines.append(jnp.sum(thin.T, axis=0, keepdims=True) / gains[k])
    tail = []
    for line in (jnp.concatenate(lines, axis=1), jnp.sum(grads[3][...], axis=0, keepdims=True)):
        tail += [line[:, c : c + LANES] for c in range(0, line.shape[1], LANES)]
    tail = jnp.concatenate([*tail, jnp.zeros((2 * half - at - len(tail), LANES), F32)], axis=0)

    def pack(halves):
        for which, tile, start, count in parts:
            for h, dst, src, n in both_halves(start, count, half):
                part = grads[which][src : src + n, tile * LANES : (tile + 1) * LANES]
                halves[h][dst : dst + n, :] = part.astype(halves[h].dtype)
        halves[1][at - half :, :] = tail.astype(halves[1].dtype)

    pl.when(info[0] == 0)(lambda: pack((mine, send)))
    pl.when(info[0] == 1)(lambda: pack((send, mine)))


def grads_call(plan, step, chips, info, units, dzs, nb, before, weights):
    _, rows, _, _, steps, _, chans, hidden, lons = plan
    first, last = step == steps - 1, step == 0
    ins = [units, dzs, nb]
    aliases = {}
    if not first:
        ins += before
    sums = [VM(s, F32) for s in ((chans, hidden), (hidden, hidden), (hidden, chans), (8, 2 * hidden + chans))]
    if last:
        ins += weights
        half = chips * packed_block(plan, chips)
        shapes, scratch = [VM((half, LANES), F32), VM((half, LANES), BF16)], sums
    else:
        shapes, scratch = sums, []
        if not first:
            aliases = {4 + n: n for n in range(4)}
    flops = 2 * hidden * (2 * chans + hidden)
    return step_call(
        partial(grads_kernel, plan, step), f"grads_{step}", 1, shapes, ins, (info,), (rows * lons, flops), scratch, aliases
    )


def pairs_kernel(chips, group, mine, got, loss, out):
    blk = mine.shape[0] // chips
    share = loss[...] * (1.0 / group)
    row = lax.broadcasted_iota(jnp.int32, share.shape, 0)
    high = share.astype(BF16).astype(F32)
    rest = share - high
    mid = rest.astype(BF16).astype(F32)
    lines = jnp.where(row == 0, high, jnp.where(row == 1, mid, jnp.where(row == 2, rest - mid, 0.0)))
    lines = jnp.concatenate([lines, jnp.zeros_like(lines)], axis=0).astype(BF16)
    for c in range(chips):
        at = slice(c * blk, (c + 1) * blk)
        out[c, 0:blk, :] = (mine[at, :] + got[at, :].astype(F32)).astype(BF16)
        out[c, blk:, :] = lines


def chips_kernel(got, out, loss):
    chips, blk = out.shape[0], out.shape[1]
    total = got[0].astype(F32)
    for c in range(1, chips):
        total = total + got[c].astype(F32)
    low = total[0:blk].astype(BF16)
    for c in range(chips):
        out[c] = low
    loss[...] = jnp.broadcast_to(jnp.sum(total[blk:], axis=0, keepdims=True), loss.shape)


def update_kernel(plan, info, part, part_o, loss, *refs):
    params, means, squares = refs[0:4], refs[4:8], refs[8:12]
    scalars = refs[12:14]
    outs = [refs[14 + 4 * k : 18 + 4 * k] for k in range(4)]
    packed, sems = refs[30], refs[31]
    stage = [refs[32 + 4 * k : 36 + 4 * k] for k in range(4)]
    ones = refs[48:50]
    packed[info[0]] = part[...]
    packed[1 - info[0]] = part_o[...]
    half = packed.shape[1]
    acc = jnp.zeros((16, LANES), F32)
    for h in range(2):
        g = packed[h].astype(F32)
        acc = acc + jnp.sum((g * g).reshape(half // 16, 16, LANES), axis=0)
    total = jnp.sum(jnp.sum(acc, axis=0, keepdims=True), axis=1, keepdims=True)
    root = jnp.sqrt(total)
    ones[0][...] = loss[0:1, 0:1]
    ones[1][...] = root
    singles = [pltpu.make_async_copy(ones[n], scalars[n], sems.at[16 + n]) for n in range(2)]
    for copy in singles:
        copy.start()
    factor = jnp.broadcast_to(CLIP_NORM / jnp.maximum(root, CLIP_NORM), (1, LANES))

    def apply(which, rs, cs, g):
        g = g * factor
        w = params[which][rs, cs]
        a = BETA_ONE * means[which][rs, cs] + (1.0 - BETA_ONE) * g
        b = BETA_TWO * squares[which][rs, cs] + (1.0 - BETA_TWO) * g * g
        w = w - LEARN_RATE * (a / (b * lax.rsqrt(b) + EPS_ADAM) + DECAY * w)
        for k, value in enumerate((w, a, b, w.astype(BF16))):
            stage[k][which][rs, cs] = value

    def copies(which):
        return [
            pltpu.make_async_copy(stage[k][which], outs[k][which], sems.at[4 * which + k]) for k in range(4)
        ]

    parts, at = packed_parts(plan)
    for n, (which, tile, start, count) in enumerate(parts):
        cs = slice(tile * LANES, (tile + 1) * LANES)
        for h, src, dst, size in both_halves(start, count, half):
            for c in range(0, size, UPDATE_ROWS):
                n_rows = min(UPDATE_ROWS, size - c)
                g = packed[h, src + c : src + c + n_rows, :].astype(F32)
                apply(which, slice(dst + c, dst + c + n_rows), cs, g)
        if n + 1 == len(parts) or parts[n + 1][0] != which:
            for copy in copies(which):
                copy.start()
    tiles = (plan.chans + 2 * plan.hidden) // LANES
    rows = packed[1, at - half : at - half + 2 * tiles, :].astype(F32)
    for tile in range(tiles):
        g = jnp.concatenate([rows[tile : tile + 1], rows[tiles + tile : tiles + tile + 1]], axis=0)
        apply(3, slice(0, 2), slice(tile * LANES, (tile + 1) * LANES), g)
    for copy in copies(3):
        copy.start()
    for copy in singles:
        copy.wait()
    for which in range(4):
        for copy in copies(which):
            copy.wait()


def update_call(plan, info, part, part_o, loss, params, means, squares):
    kinds = (F32, F32, F32, BF16)
    hbm = pl.BlockSpec(memory_space=pl.ANY)
    vmem = pl.BlockSpec(memory_space=VM)
    return pl.pallas_call(
        partial(update_kernel, plan),
        out_shape=[jax.ShapeDtypeStruct((1, 1), F32)] * 2 + [jax.ShapeDtypeStruct(w.shape, kind) for kind in kinds for w in params],
        grid_spec=pltpu.PrefetchScalarGridSpec(
            num_scalar_prefetch=1,
            grid=(1,),
            in_specs=[vmem] * 15,
            out_specs=[hbm] * 18,
            scratch_shapes=[VM((2, *part.shape), BF16), pltpu.SemaphoreType.DMA((18,))]
            + [VM(w.shape, kind) for kind in kinds for w in params]
            + [VM((1, 1), F32)] * 2,
        ),
        compiler_params=kernel_params(),
        name="update",
    )(info, part, part_o, loss, *params, *means, *squares)


def small_call(kernel, name, shapes, ins, scalars=(), scratch=()):
    return pl.pallas_call(
        kernel,
        out_shape=shapes,
        grid_spec=pltpu.PrefetchScalarGridSpec(
            num_scalar_prefetch=len(scalars),
            grid=(1,),
            in_specs=[whole(a) for a in ins],
            out_specs=[whole(a) for a in shapes],
            scratch_shapes=list(scratch),
        ),
        compiler_params=kernel_params(),
        name=name,
    )(*scalars, *ins)


def grouped_device(
    plan,
    chips,
    spectral_state,
    legendre,
    wave_slots,
    lat_order,
    quad_weights,
    available,
    targets,
    *flat,
):
    group, rows, waves, degrees, steps, fields, chans, hidden, lons = plan
    params, means, squares = flat[0:4], flat[4:8], flat[8:12]
    weights = [w.astype(BF16) for w in params[:3]]
    nb = params[3]
    tdev = spectral_state.shape[0]
    copies = waves // chips
    core = lax.axis_index("tm")
    chip = lax.axis_index("lat")
    member = chip % group
    info = jnp.stack([core, member]).astype(jnp.int32)
    swap = [(0, 1), (1, 0)]
    across = lambda a: lax.ppermute(a, "tm", swap)

    def to_members(a, fill):
        out = [a]
        bit = 1
        while bit < group:
            out += [lax.ppermute(v, "lat", [(n, n ^ bit) for n in range(waves)]) for v in out]
            bit *= 2
        away, filled = lax.optimization_barrier((out[1:], fill()))
        out = [a, *away]
        return out + [across(v) for v in out], filled

    def to_each(a, fill):
        places = [(c, n) for c in range(2) for n in range(waves)]
        out = []
        for other, m in [(c, n) for c in range(2) for n in range(group)][1:]:
            if other and not m:
                out.append(across(a))
            else:
                pairs = [(c * waves + n, (c ^ other) * waves + (n ^ m)) for c, n in places]
                out.append(lax.ppermute(a, ("tm", "lat"), pairs))
        out, filled = lax.optimization_barrier((out, fill()))
        return [a, *out], filled

    deep = -(-(2 * degrees + fields // 2 + 1) // 8) * 8
    keep, send = pack_call(info, spectral_state, available, legendre, deep)
    other = across(send)
    times = jnp.concatenate([jnp.where(core == 0, keep, other), jnp.where(core == 0, other, keep)], axis=0)
    spread = jnp.broadcast_to(times[None, :, None], (copies, 2 * tdev, group, *times.shape[1:]))
    got = lax.all_to_all(spread.reshape(waves, *times.shape[1:]), "lat", split_axis=0, concat_axis=0, tiled=True)
    got_o = across(got)

    def table(scaled):
        product = wave_slots[:, None] * jnp.arange(lons, dtype=jnp.int32)[None, :] % lons
        phase = product.astype(F32) * (2.0 * math.pi / lons)
        inverse = jnp.concatenate([jnp.cos(phase), -jnp.sin(phase)], axis=0)
        if not scaled:
            return inverse
        scale = jnp.where(wave_slots == 0, 1.0, 2.0).astype(F32) / lons
        return inverse * jnp.concatenate([scale, scale])[:, None]

    inv32, ffw32 = table(False), table(True)
    inv, ffw = inv32.astype(BF16), ffw32.astype(BF16)
    theirs = across(targets)
    tgt_all = jnp.concatenate([jnp.where(core == 0, targets, theirs), jnp.where(core == 0, theirs, targets)], axis=0)
    tgt = lax.dynamic_index_in_dim(tgt_all, (chip // group) % (2 * tdev), axis=0, keepdims=False)
    tgt = jnp.broadcast_to(tgt.reshape(steps * fields, 1), (steps * fields, LANES))
    made = links_call(plan, info, wave_slots, lat_order, got, inv32, ffw32, tgt)
    got_o, (state, links, lt, inv_t, ffw_t, tgt) = lax.optimization_barrier((got_o, made))
    scalars = (info, lat_order, quad_weights)
    state, avail, nums = fields_call(plan, scalars, state, got, got_o)

    saved, pieces = [], None
    for s in range(steps):
        units, inners, scales, *rest = forward_call(
            plan, s, scalars, state, avail, nums, inv_t, ffw, lt, weights, nb, links, pieces
        )
        fill = lambda: slopes_call(plan, s, inners, scales)
        if s < steps - 1:
            pieces, slopes = to_members(rest[2], fill)
            nums = counts_call(plan, s, scalars, [rest[0], rest[1], avail, nums, inv_t])
            pieces, nums = lax.optimization_barrier((pieces, nums))
            if s:
                state = rest[3]
        else:
            counts, slopes = to_each(rest[0], fill)
        saved.append((units, slopes, scales))
    before, bstate = None, None
    wanted = [avail, tgt, *counts]
    for s in reversed(range(steps)):
        dzs, *rest = backward_call(plan, s, scalars, saved[s], wanted, weights, nb, (links, lt, ffw_t, inv), pieces, bstate)
        grads = lambda: grads_call(plan, s, chips, info, saved[s][0], dzs, nb, before, weights)
        if s == 0:
            before = grads()
        else:
            fill = lambda: (grads(), [masks_call(plan, s - 1, scalars, avail, tgt, counts)])
            pieces, (before, wanted) = to_members(rest[0], fill)
            if s == steps - 1:
                loss = rest[1]
            else:
                bstate = rest[1]
    mine, send = before
    blk = mine.shape[0] // chips
    groups = [[c * chips + n for n in range(chips)] for c in range(copies)]
    exchange = lambda a: lax.all_to_all(a, "lat", split_axis=0, concat_axis=0, tiled=True, axis_index_groups=groups)
    (parts,) = small_call(
        partial(pairs_kernel, chips, group),
        "pairs",
        [jax.ShapeDtypeStruct((chips, blk + 16, LANES), BF16)],
        [mine, across(send), loss],
    )
    reduced, loss = small_call(
        chips_kernel,
        "chips",
        [jax.ShapeDtypeStruct((chips, blk, LANES), BF16), jax.ShapeDtypeStruct((8, LANES), F32)],
        [exchange(parts)],
    )
    part = exchange(reduced).reshape(chips * blk, LANES)
    loss, norm, *results = update_call(plan, info, part, across(part), loss, params, means, squares)
    return (loss.reshape(()), norm.reshape(()), *results)


def make_plan(mesh, args):
    state, legendre, _, _, _, available, targets, w_first = args[:8]
    times, waves, _, degrees, chans = state.shape
    _, fields, lats, lons = available.shape
    hidden = w_first.shape[1]
    cores, chips_all = mesh.shape["tm"], mesh.shape["lat"]
    group = GROUP
    chips = group * times
    rows, rest = divmod(lats, 2 * group)
    fits = (
        cores == 2
        and times % cores == 0
        and chips_all == waves == lats
        and waves % chips == 0
        and rest == 0
        and fields == 8
        and lons == chans == degrees * lats
        and waves % 16 == 0
        and degrees % 16 == 0
        and chans % LANES == 0
        and hidden % LANES == 0
        and lons % SUB == 0
    )
    if not fits or legendre.shape != (waves, degrees, lats):
        return None
    steps = targets.shape[1]
    if steps < 3 or steps * rows * lons * (chans + 4 * hidden + LANES) * 4 > SAVED_LIMIT:
        return None
    return Plan(group, rows, waves, degrees, steps, fields, chans, hidden, lons), chips


def solution(mesh):
    in_specs = (
        P("tm", "lat", None, None, None),
        P("lat", None, None),
        P(),
        P(),
        P(),
        P("tm", None, "lat", None),
        P("tm", None, None),
    ) + (P(),) * 12

    def run(*args):
        made = make_plan(mesh, args)
        body = spread_device if made is None else partial(grouped_device, *made)
        return jax.shard_map(body, mesh=mesh, in_specs=in_specs, out_specs=(P(),) * 18, check_vma=False)(*args)

    return run
```

```python
from collections import namedtuple
from functools import partial
import math

import jax
import jax.numpy as jnp
from jax import lax
from jax.experimental import pallas as pl
from jax.experimental.pallas import tpu as pltpu
from jax.sharding import PartitionSpec as P

STEPS = 4


EPS_NORM = 1e-05
STEP_SCALE = 0.5
CLIP_NORM = 1.0
LEARN_RATE = 0.01
BETA_ONE = 0.9
BETA_TWO = 0.95
EPS_ADAM = 1e-08
DECAY = 0.1
HIGH = lax.Precision.HIGHEST


def wave_tables(wave_slots, lon_count):
    product = wave_slots[:, None] * jnp.arange(lon_count, dtype=jnp.int32)[None, :] % lon_count
    phase = product.astype(jnp.float32) * (2.0 * math.pi / lon_count)
    inverse = jnp.stack([jnp.cos(phase), -jnp.sin(phase)], axis=1)
    scale = jnp.where(wave_slots == 0, 1.0, 2.0).astype(jnp.float32) / lon_count
    return (inverse.astype(jnp.bfloat16), (inverse * scale[:, None, None]).astype(jnp.bfloat16))


def layer_spans(chans, hidden):
    gains = [(0, chans), (chans, hidden), (chans + hidden, hidden)]
    biases = [(0, hidden), (hidden, hidden), (2 * hidden, chans)]
    return list(zip(gains, biases))


def norm_gain(x, gain):
    centre = x - jnp.mean(x, axis=-1, keepdims=True)
    return centre * lax.rsqrt(jnp.mean(centre * centre, axis=-1, keepdims=True) + EPS_NORM) * gain


def corrector_forward(x, weights, norm_bias):
    spans = layer_spans(weights[0].shape[0], weights[0].shape[1])
    saved = []
    for k in range(3):
        (gstart, gwidth), (bstart, bwidth) = spans[k]
        h_low = norm_gain(x, 1.0 + norm_bias[0, gstart : gstart + gwidth]).astype(jnp.bfloat16)
        z_val = (
            jnp.dot(h_low, weights[k], preferred_element_type=jnp.float32)
            + norm_bias[1, bstart : bstart + bwidth]
        )
        saved.append((x, h_low, z_val))
        x = jax.nn.gelu(z_val, approximate=False) if k < 2 else z_val
    return (x, saved)


def corrector_backward(grad, saved, weights, norm_bias):
    spans = layer_spans(weights[0].shape[0], weights[0].shape[1])
    weight_grads = [None, None, None]
    gain_parts = [None, None, None]
    bias_parts = [None, None, None]
    for k in (2, 1, 0):
        (gstart, gwidth), (bstart, bwidth) = spans[k]
        x, h_low, z_val = saved[k]
        if k < 2:
            grad = jax.vjp(partial(jax.nn.gelu, approximate=False), z_val)[1](grad)[0]
        grad_low = grad.astype(jnp.bfloat16)
        weight_grads[k] = lax.dot_general(
            h_low, grad_low, (((0,), (0,)), ((), ())), preferred_element_type=jnp.float32
        )
        bias_parts[k] = jnp.sum(grad_low, axis=0, dtype=jnp.float32)
        back_h = lax.dot_general(
            grad_low, weights[k], (((1,), (1,)), ((), ())), preferred_element_type=jnp.float32
        )
        grad, gain_parts[k] = jax.vjp(norm_gain, x, 1.0 + norm_bias[0, gstart : gstart + gwidth])[
            1
        ](back_h)
    vector_grad = jnp.stack([jnp.concatenate(gain_parts), jnp.concatenate(bias_parts)])
    return (grad, (weight_grads[0], weight_grads[1], weight_grads[2], vector_grad))


def adamw(weight, mean, square, grad):
    mean_new = BETA_ONE * mean + (1.0 - BETA_ONE) * grad
    square_new = BETA_TWO * square + (1.0 - BETA_TWO) * grad * grad
    weight_new = weight - LEARN_RATE * (
        mean_new / (jnp.sqrt(square_new) + EPS_ADAM) + DECAY * weight
    )
    return (weight_new, mean_new, square_new)


def spread_device(
    spectral_state,
    legendre,
    wave_slots,
    lat_order,
    quad_weights,
    available,
    targets,
    w_first,
    w_mid,
    w_last,
    norm_bias,
    mean_first,
    mean_mid,
    mean_last,
    mean_bias,
    square_first,
    square_mid,
    square_last,
    square_bias,
):
    tdev, wdev, _, degrees, chans = spectral_state.shape
    fields = available.shape[1]
    rows_dev = available.shape[2]
    lon_count = available.shape[3]
    levels = chans // fields
    lat_index = lax.axis_index("lat")
    slots = lax.dynamic_slice_in_dim(wave_slots, lat_index * wdev, wdev)
    finv, ffw = wave_tables(wave_slots, lon_count)
    keep = (jnp.arange(degrees, dtype=jnp.int32)[None, :] >= slots[:, None]).astype(jnp.bfloat16)
    plg = jnp.take(legendre, lat_order, axis=2) * keep[:, :, None]
    qrow = jnp.take(quad_weights, lat_order)
    qlocal = lax.dynamic_slice_in_dim(qrow, lat_index * rows_dev, rows_dev)
    colw = qlocal[None, None, :, None] * available.astype(jnp.float32)
    den_part = jnp.sum(colw, axis=(2, 3))
    params = (w_first, w_mid, w_last, norm_bias)
    weights = (
        w_first.astype(jnp.bfloat16),
        w_mid.astype(jnp.bfloat16),
        w_last.astype(jnp.bfloat16),
    )

    def legendre_sum(piece):
        return jnp.einsum("mnr,tmprc->tmpnc", plg, piece, preferred_element_type=jnp.float32)

    def fourier_sum(table, piece):
        return jnp.einsum("mpk,tmprc->trkc", table, piece, preferred_element_type=jnp.float32)

    def to_grid(state):
        sums = jnp.einsum(
            "mnr,tmpnc->tmprc", plg, state.astype(jnp.bfloat16), preferred_element_type=jnp.float32
        ).astype(jnp.bfloat16)
        return fourier_sum(
            finv, lax.all_to_all(sums, "lat", split_axis=3, concat_axis=1, tiled=True)
        )

    def column_pass(grid):
        out, saved = corrector_forward(grid.reshape(-1, chans), weights, norm_bias)
        return (out.reshape(grid.shape), saved)

    states = []
    nums = []
    den_total = den_part
    state = spectral_state
    for s in range(STEPS):
        states.append(state)
        grid = to_grid(state)
        out, saved = column_pass(grid)
        pred = grid + STEP_SCALE * out
        num_part = jnp.einsum(
            "tfrk,trkfl->tf",
            colw,
            pred.reshape(tdev, rows_dev, lon_count, fields, levels),
            precision=HIGH,
        )
        num_total, den_total = lax.psum((num_part, den_part), "lat")
        nums.append(num_total)
        tend = (out * qlocal[None, :, None, None]).astype(jnp.bfloat16)
        coeff = jnp.einsum("mpk,trkc->tmprc", ffw, tend, preferred_element_type=jnp.float32).astype(
            jnp.bfloat16
        )
        spec = legendre_sum(lax.all_to_all(coeff, "lat", split_axis=1, concat_axis=3, tiled=True))
        state = state + STEP_SCALE * spec
    num_all = jnp.stack(nums)
    bias = num_all / (levels * den_total[None]) - jnp.moveaxis(targets, 1, 0)
    loss = lax.psum(jnp.sum(bias * bias) / STEPS, "tm")
    grad_bias = 2.0 * bias / (STEPS * levels * den_total[None])
    totals = tuple((jnp.zeros_like(p) for p in params))
    back_state = None
    for s in reversed(range(STEPS)):
        grid = to_grid(states[s])
        out, saved = column_pass(grid)
        scaled = jnp.moveaxis(colw * grad_bias[s][:, :, None, None], 1, 3)
        back_pred = jnp.broadcast_to(scaled[..., None], scaled.shape + (levels,)).reshape(
            grid.shape
        )
        back_out = STEP_SCALE * back_pred
        if back_state is not None:
            back_spec = (STEP_SCALE * back_state).astype(jnp.bfloat16)
            back_coeff = jnp.einsum(
                "mnr,tmpnc->tmprc", plg, back_spec, preferred_element_type=jnp.float32
            ).astype(jnp.bfloat16)
            back_tend = fourier_sum(
                ffw, lax.all_to_all(back_coeff, "lat", split_axis=3, concat_axis=1, tiled=True)
            )
            back_out = back_out + qlocal[None, :, None, None] * back_tend
        back_in, grads = corrector_backward(back_out.reshape(-1, chans), saved, weights, norm_bias)
        totals = tuple((a + b for a, b in zip(totals, grads)))
        if s > 0:
            back_grid = (back_pred + back_in.reshape(grid.shape)).astype(jnp.bfloat16)
            back_sums = jnp.einsum(
                "mpk,trkc->tmprc", finv, back_grid, preferred_element_type=jnp.float32
            ).astype(jnp.bfloat16)
            back_low = legendre_sum(
                lax.all_to_all(back_sums, "lat", split_axis=1, concat_axis=3, tiled=True)
            )
            back_state = back_low if back_state is None else back_state + back_low
    means = (mean_first, mean_mid, mean_last, mean_bias)
    squares = (square_first, square_mid, square_last, square_bias)
    grads = lax.psum(totals, ("tm", "lat"))
    grad_norm = jnp.sqrt(sum((jnp.sum(g * g) for g in grads)))
    factor = CLIP_NORM / jnp.maximum(grad_norm, CLIP_NORM)
    results = [adamw(w, a, b, g * factor) for w, a, b, g in zip(params, means, squares, grads)]
    masters = [r[0] for r in results]
    new_means = [r[1] for r in results]
    new_squares = [r[2] for r in results]
    halves = [w.astype(jnp.bfloat16) for w in masters]
    return (
        loss,
        grad_norm,
        masters[0],
        masters[1],
        masters[2],
        masters[3],
        new_means[0],
        new_means[1],
        new_means[2],
        new_means[3],
        new_squares[0],
        new_squares[1],
        new_squares[2],
        new_squares[3],
        halves[0],
        halves[1],
        halves[2],
        halves[3],
    )


F32 = jnp.float32
BF16 = jnp.bfloat16
VM = pltpu.VMEM
LANES = 128
GROUP = 2
SUB = 256
CHUNK = 32
ROWS_BLOCK = 4
UPDATE_ROWS = 32
VMEM_LIMIT = 10 << 20
SAVED_LIMIT = 96 << 20


Plan = namedtuple("Plan", ("group", "rows", "waves", "degrees", "steps", "fields", "chans", "hidden", "lons"))


def dot(a, b, dims=((1,), (0,))):
    return lax.dot_general(a, b, (dims, ((), ())), preferred_element_type=F32)


def norm_unit(x, eps):
    centre = x - jnp.mean(x, axis=-1, keepdims=True)
    scale = lax.rsqrt(jnp.mean(centre * centre, axis=-1, keepdims=True) + eps)
    return centre * scale, scale


def gelu_parts(z):
    arg = z * math.sqrt(0.5)
    return arg, 1.0 + lax.erf(arg)


def slope_twice(z):
    arg, cdf = gelu_parts(z)
    return cdf + (z * math.sqrt(2.0 / math.pi)) * jnp.exp2(arg * arg * -math.log2(math.e))


def wide(scale, width):
    return jnp.concatenate([scale] * (width // LANES), axis=1)


def whole(a):
    return pl.BlockSpec(a.shape, lambda *_: (0,) * len(a.shape))


def fold(v):
    return jnp.sum(v.reshape(v.shape[0] // 8, 8, v.shape[1]), axis=0)


def field_mask(fields, chans):
    lane = lax.broadcasted_iota(jnp.int32, (fields, chans), 1)
    row = lax.broadcasted_iota(jnp.int32, (fields, chans), 0) * (chans // fields)
    return (lane >= row) & (lane < row + chans // fields)


def splits(nb, chans, hidden):
    gains = [1.0 + nb[0:1, a:b] for a, b in ((0, chans), (chans, chans + hidden), (chans + hidden, chans + 2 * hidden))]
    biases = [nb[1:2, a:b] for a, b in ((0, hidden), (hidden, 2 * hidden), (2 * hidden, 2 * hidden + chans))]
    return gains, biases


def stagger(chains):
    live, waiting = [], list(chains)
    while live or waiting:
        if waiting:
            live.append(waiting.pop(0))
        for chain in list(live):
            if next(chain, live) is live:
                live.remove(chain)


def pair_rows(plan):
    return ROWS_BLOCK if plan.rows % ROWS_BLOCK == 0 else 1


def row_weight(plan, info, order, quad, row):
    return quad[order[(info[1] * 2 + info[0]) * plan.rows + row]]


def pack_kernel(info, state_in, seen_in, legendre_in, keep, send, state, seen, legendre, sems):
    pairs = ((state_in, state), (seen_in, seen), (legendre_in, legendre))
    loads = [pltpu.make_async_copy(a, b, sems.at[n]) for n, (a, b) in enumerate(pairs)]
    for load in loads:
        load.start()
    for load in loads:
        load.wait()
    times, _, parts, degrees, chans = state.shape
    fields = seen.shape[1]
    lats = legendre.shape[2]
    iota = lambda d, s: lax.broadcasted_iota(jnp.int32, s, d)
    repeat = (iota(1, (lats, chans)) % lats == iota(0, (lats, chans))).astype(F32).astype(BF16)
    line = dot(legendre[0], repeat)
    line = jnp.where(iota(1, (degrees, chans)) // lats == iota(0, (degrees, chans)), line, 0.0)
    line = jnp.sum(line, axis=0, keepdims=True)
    half = fields // parts
    blank = jnp.zeros((keep.shape[1] - 2 * degrees - half - 1, chans), F32)
    mine = info[0] == 0
    for t in range(times):
        rows = []
        for p in range(parts):
            x = state[t, 0, p]
            hi = x.astype(BF16).astype(F32)
            there = [seen[t, f].astype(F32) for f in range(p * half, (p + 1) * half)]
            rows.append(jnp.concatenate([hi, x - hi, *there, line, blank], axis=0))
        keep[t] = jnp.where(mine, rows[0], rows[1]).astype(BF16)
        send[t] = jnp.where(mine, rows[1], rows[0]).astype(BF16)


def pack_call(info, state, seen, legendre, deep):
    times, _, _, _, chans = state.shape
    ins = [pltpu.with_memory_space_constraint(a, pltpu.HBM) for a in (state, seen, legendre)]
    return pl.pallas_call(
        pack_kernel,
        out_shape=[VM((times, deep, chans), BF16)] * 2,
        grid_spec=pltpu.PrefetchScalarGridSpec(
            num_scalar_prefetch=1,
            grid=(1,),
            in_specs=[pl.BlockSpec(memory_space=pltpu.HBM)] * 3,
            out_specs=[pl.BlockSpec(memory_space=VM)] * 2,
            scratch_shapes=[VM(a.shape, a.dtype) for a in ins] + [pltpu.SemaphoreType.DMA((3,))],
        ),
        compiler_params=kernel_params(),
        name="pack",
    )(info, *ins)


def unpack_state(plan, ref, p, state):
    waves, degrees = plan.waves, plan.degrees
    for j in range(waves):
        high = ref[j, 0:degrees, :].astype(F32)
        state[p, pl.ds(j * degrees, degrees), :] = high + ref[j, degrees : 2 * degrees, :].astype(F32)


def links_kernel(plan, info, slots, order, got, inv, ffw, wanted, state, links, lt, table, ffw_t, tgt):
    group, rows, waves, degrees, _, fields, chans, _, _ = plan
    members = 2 * group
    core, member = info[0], info[1]
    span = waves * degrees
    mine = rows * waves
    half = fields // 2
    lats = rows * members
    leg = jnp.zeros((waves, chans), F32)
    row_of = lax.broadcasted_iota(jnp.int32, (waves, chans), 0)
    pick = lax.broadcasted_iota(jnp.int32, (8, chans), 0) == half
    unpack_state(plan, got, core, state)
    for j in range(waves):
        tail = got[j, 2 * degrees : 2 * degrees + 8, :].astype(F32)
        line = jnp.sum(jnp.where(pick, tail, 0.0), axis=0, keepdims=True)
        leg = jnp.where(row_of == j, line, leg)
    iota = lambda d, s: lax.broadcasted_iota(jnp.int32, s, d)
    shape = (span, span)
    r0, r1 = iota(0, shape), iota(1, shape)
    expand = (iota(0, (span, waves)) // degrees == iota(1, (span, waves))).astype(F32).astype(BF16)
    rep = dot(expand, leg.astype(BF16))
    rep = jnp.where(r1 // lats == r0 % degrees, rep, 0.0).astype(BF16)
    lat_lane = jnp.zeros((8, span), jnp.int32)
    lane = iota(1, (8, span)) // waves
    for role in range(members):
        other = (member ^ (role & (group - 1))) * 2 + (core ^ (role // group))
        for r in range(rows):
            lat_lane = jnp.where(lane == role * rows + r, order[other * rows + r], lat_lane)
    wave_row = jnp.zeros(shape, jnp.int32)
    for j in range(waves):
        wave_row = jnp.where(r0 // degrees == j, slots[j], wave_row)
    choose = (r0 % lats == lat_lane[0:1, :]).astype(F32).astype(BF16)
    plg = dot(rep, choose)
    plg = jnp.where((r0 // degrees == r1 % waves) & (r0 % degrees >= wave_row), plg, 0.0)
    links[...] = plg.astype(BF16)
    lt[...] = plg[:, 0:mine].T.astype(BF16)
    table[...] = inv[...].T.astype(BF16)
    ffw_t[...] = ffw[...].T.astype(BF16)
    tgt[...] = wanted[...]


def fields_kernel(plan, info, order, quad, held, got, got_o, state, avail, nums):
    _, rows, _, degrees, steps, fields, chans, _, _ = plan
    core, member = info[0], info[1]
    half = fields // 2
    unpack_state(plan, got_o, 1 - core, state)
    spot = member * 2 + core
    den = jnp.zeros((fields, chans), F32)
    for r in range(rows):
        src = spot * rows + r
        a = got[src, 2 * degrees : 2 * degrees + 8, :].astype(F32)
        b = got_o[src, 2 * degrees : 2 * degrees + 8, :].astype(F32)
        first = jnp.where(core == 0, a, b)[0:half]
        second = jnp.where(core == 0, b, a)[0:half]
        both = jnp.concatenate([first, second], axis=0)
        avail[r] = both.astype(BF16)
        den += quad[order[src]] * both
    nums[...] = jnp.zeros_like(nums)
    nums[steps * fields :, :] = jnp.broadcast_to(jnp.sum(den, axis=1, keepdims=True), (fields, nums.shape[1]))


def links_call(plan, info, slots, order, got, inv, ffw, wanted):
    group, rows, waves, degrees, _, _, chans, _, lons = plan
    span, mine = waves * degrees, rows * waves
    shapes = [
        VM((2, span, chans), F32),
        VM((span, 2 * group * mine), BF16),
        VM((mine, span), BF16),
        VM((lons, 2 * waves), BF16),
        VM((lons, 2 * waves), BF16),
        VM(wanted.shape, F32),
    ]
    return step_call(
        partial(links_kernel, plan), "links", 1, shapes, [got, inv, ffw, wanted], (info, slots, order), (span, 2 * span)
    )


def fields_call(plan, scalars, state, got, got_o):
    shapes = [
        VM(state.shape, F32),
        VM((plan.rows, plan.fields, plan.lons), BF16),
        VM(((plan.steps + 1) * plan.fields, LANES), F32),
    ]
    work = (plan.waves * plan.degrees, 8)
    return step_call(partial(fields_kernel, plan), "fields", 1, shapes, [state, got, got_o], scalars, work, (), {3: 0})


def kernel_params():
    return pltpu.CompilerParams(vmem_limit_bytes=VMEM_LIMIT)


def write_count(plan, step, nums_in, nums, acc):
    fields, chans = plan.fields, plan.chans
    kept = jnp.where(field_mask(fields, chans), acc, 0.0)
    nums[...] = nums_in[...]
    nums[step * fields : (step + 1) * fields, :] = jnp.broadcast_to(
        jnp.sum(kept, axis=1, keepdims=True), (fields, LANES)
    )


def weighted_sum(weights, values):
    hi = values.astype(BF16)
    lo = (values - hi.astype(F32)).astype(BF16)
    return dot(weights, hi) + dot(weights, lo)


def forward_kernel(plan, step, info, order, quad, *refs):
    group, rows, waves, _, steps, fields, chans, hidden, lons = plan
    first, last = step == 0, step == steps - 1
    rows_blk = pair_rows(plan)
    refs = list(refs)
    take = lambda: refs.pop(0)
    state = [take() for _ in range(2 if first else 1)]
    table, ffw, lt, w1, w2, w3, nb = [take() for _ in range(7)]
    if last:
        avail, nums_in = take(), take()
    if not first:
        links = take()
        pieces = [take() for _ in range(2 * group)]
    units, inners, scales = [take() for _ in range(3)]
    if last:
        nums = take()
    else:
        sums, outs, y_out = [take() for _ in range(3)]
        if not first:
            state_out = take()
    if last:
        sums, num_acc = take(), take()
    i = pl.program_id(0)

    @pl.when(i == 0)
    def _():
        for p, ref in zip((info[0], 1 - info[0]), state if first else ()):
            high = ref[:, 0 : plan.degrees, :].reshape(waves * plan.degrees, chans)
            sums[p] = dot(lt[...], high).astype(BF16)
        for p in range(0 if first else 2):
            spec = dot(links[...], jnp.concatenate([piece[p] for piece in pieces], axis=0))
            st = state[0][p] + STEP_SCALE * spec
            if not last:
                state_out[p] = st
            sums[p] = dot(lt[...], st.astype(BF16)).astype(BF16)
        if last:
            num_acc[...] = jnp.zeros_like(num_acc)

    gains, biases = splits(nb, chans, hidden)
    spans = ((0, chans), (chans, hidden), (chans + hidden, hidden))
    weights = (w1, w2, w3)

    def row_chain(rr):
        row = i * rows_blk + rr
        at = pl.ds(pl.multiple_of(row * waves, waves), waves)
        rhs = jnp.concatenate([sums[0, at, :], sums[1, at, :]], axis=0)
        q = row_weight(plan, info, order, quad, row)
        grid = dot(table[...], rhs)
        yield
        x = [grid[c : c + CHUNK] for c in range(0, lons, CHUNK)]
        for k in range(3):
            low = []
            for n, part in enumerate(x):
                cs = pl.ds(pl.multiple_of(row * lons + n * CHUNK, CHUNK), CHUNK)
                if k:
                    part = part + biases[k - 1]
                    inners[cs, (k - 1) * hidden : k * hidden] = part
                    part = part * gelu_parts(part)[1]
                unit, scale = norm_unit(part, 4.0 * EPS_NORM if k else EPS_NORM)
                units[cs, spans[k][0] : spans[k][0] + spans[k][1]] = unit
                scales[cs, k * LANES : (k + 1) * LANES] = jnp.broadcast_to(scale, (CHUNK, LANES))
                low.append((unit * gains[k]).astype(BF16))
            yield
            z = dot(jnp.concatenate(low, axis=0), weights[k][...])
            x = [z[c : c + CHUNK] for c in range(0, lons, CHUNK)]
            yield
        if last:
            pred = grid + STEP_SCALE * (z + biases[2])
            yield
            num_acc[...] += q * weighted_sum(avail[row], pred)
        else:
            tends = []
            for n, part in enumerate(x):
                cs = pl.ds(pl.multiple_of(row * lons + n * CHUNK, CHUNK), CHUNK)
                out = part + biases[2]
                outs[cs, :] = out
                tends.append((out * q).astype(BF16))
            yield
            coeff = dot(ffw[...], jnp.concatenate(tends, axis=0)).astype(BF16)
            y_out[0, at, :] = coeff[:waves]
            y_out[1, at, :] = coeff[waves:]
        yield

    stagger([row_chain(rr) for rr in range(rows_blk)])

    if last:

        @pl.when(i == pl.num_programs(0) - 1)
        def _():
            write_count(plan, step, nums_in, nums, num_acc[...])


def step_call(kernel, name, grid, shapes, ins, scalars, work, scratch=(), aliases=None):
    cols, flops = work
    return pl.pallas_call(
        kernel,
        out_shape=shapes,
        grid_spec=pltpu.PrefetchScalarGridSpec(
            num_scalar_prefetch=len(scalars),
            grid=(grid,),
            in_specs=[pl.BlockSpec(memory_space=VM)] * len(ins),
            out_specs=[pl.BlockSpec(memory_space=VM)] * len(shapes),
            scratch_shapes=list(scratch),
        ),
        input_output_aliases=aliases or {},
        compiler_params=kernel_params(),
        cost_estimate=pl.CostEstimate(flops=cols * flops, bytes_accessed=cols * 8192, transcendentals=cols * 1024),
        name=name,
    )(*scalars, *ins)


def forward_call(plan, step, scalars, state, avail, nums, table, ffw, lt, weights, nb, links, pieces):
    group, rows, waves, _, steps, fields, chans, hidden, lons = plan
    first, last = step == 0, step == steps - 1
    rows_blk = pair_rows(plan)
    cols = rows * lons
    ins = [*state, table, ffw, lt, *weights, nb]
    if last:
        ins += [avail, nums]
    if not first:
        ins += [links, *pieces]
    shapes = [VM((cols, width), F32) for width in (chans + 2 * hidden, 2 * hidden, 3 * LANES)]
    sums = (2, rows * waves, chans)
    scratch = []
    if last:
        shapes.append(VM(nums.shape, F32))
        scratch = [VM(sums, BF16), VM((fields, chans), F32)]
    else:
        shapes += [VM(sums, BF16), VM((cols, chans), F32), VM(sums, BF16)]
        if not first:
            shapes.append(VM(state[0].shape, F32))
    flops = 2 * hidden * (2 * chans + hidden)
    return step_call(
        partial(forward_kernel, plan, step), f"forward_{step}", rows // rows_blk, shapes, ins, scalars, (cols, flops), scratch
    )


def slopes_kernel(plan, inners, scales, slopes):
    rows, hidden, lons = plan.rows, plan.hidden, plan.lons
    i = pl.program_id(0)
    for n in range(lons // CHUNK):
        cs = pl.ds(pl.multiple_of(i * lons + n * CHUNK, CHUNK), CHUNK)
        for k in range(2):
            at = slice(k * hidden, (k + 1) * hidden)
            scale = wide(scales[cs, (k + 1) * LANES : (k + 2) * LANES], hidden)
            slopes[cs, at] = slope_twice(inners[cs, at]) * scale


def slopes_call(plan, step, inners, scales):
    work = (plan.rows * plan.lons, 16 * plan.hidden)
    return step_call(
        partial(slopes_kernel, plan), f"slopes_{step}", plan.rows, [VM(inners.shape, F32)], [inners, scales], (), work, (), {0: 0}
    )[0]


def counts_kernel(plan, step, info, order, quad, sums, outs, avail, nums_in, table, nums):
    rows, waves, fields, chans, lons = plan.rows, plan.waves, plan.fields, plan.chans, plan.lons
    acc = jnp.zeros((fields, chans), F32)
    for row in range(rows):
        at = slice(row * waves, (row + 1) * waves)
        grid = dot(table[...], jnp.concatenate([sums[0, at, :], sums[1, at, :]], axis=0))
        pred = grid + STEP_SCALE * outs[row * lons : (row + 1) * lons, :]
        acc = acc + row_weight(plan, info, order, quad, row) * weighted_sum(avail[row], pred)
    write_count(plan, step, nums_in, nums, acc)


def counts_call(plan, step, scalars, ins):
    work = (plan.rows * plan.lons, 8 * plan.chans)
    return step_call(partial(counts_kernel, plan, step), f"counts_{step}", 1, [VM(ins[3].shape, F32)], ins, scalars, work)[0]


def packed_parts(plan):
    parts, at = [], 0
    sizes = ((plan.chans, plan.hidden), (plan.hidden, plan.hidden), (plan.hidden, plan.chans))
    for which, (rows, cols) in enumerate(sizes):
        for tile in range(cols // LANES):
            parts.append((which, tile, at, rows))
            at += rows
    return parts, at


def packed_block(plan, chips):
    vectors = 2 * (plan.chans + 2 * plan.hidden) // LANES
    need = packed_parts(plan)[1] + vectors
    return -(-need // (2 * chips * 16)) * 16


def both_halves(at, rows, half):
    out, done = [], 0
    while done < rows:
        h = (at + done) // half
        n = min(rows - done, (h + 1) * half - at - done)
        out.append((h, at + done - h * half, done, n))
        done += n
    return out


def shares(plan, step, counts, tgt):
    steps, fields, chans = plan.steps, plan.fields, plan.chans
    levels = chans // fields

    def total(s):
        acc = [c[s * fields : (s + 1) * fields, :] for c in counts]
        while len(acc) > 1:
            acc = [a + b for a, b in zip(acc[::2], acc[1::2])]
        return acc[0]

    den = total(steps)
    bias_of = lambda s: total(s) / (levels * den) - tgt[s * fields : (s + 1) * fields, :]
    gb = 2.0 * bias_of(step) / (steps * levels * den)
    gb = jnp.where(field_mask(fields, chans), wide(gb, chans), 0.0)
    hi = gb.astype(BF16).astype(F32)
    return jnp.concatenate([hi, gb - hi], axis=0).astype(BF16), bias_of


def spread_share(avail, gmask, row):
    av2 = jnp.concatenate([avail[row].astype(F32)] * 2, axis=0).astype(BF16)
    return dot(av2, gmask, ((0,), (0,)))


def masks_kernel(plan, step, info, order, quad, avail, tgt, *refs):
    rows, lons = plan.rows, plan.lons
    counts, out = refs[:-1], refs[-1]
    gmask, _ = shares(plan, step, counts, tgt)
    for row in range(rows):
        out[row * lons : (row + 1) * lons, :] = row_weight(plan, info, order, quad, row) * spread_share(avail, gmask, row)


def masks_call(plan, step, scalars, avail, tgt, counts):
    cols = plan.rows * plan.lons
    shapes = [VM((cols, plan.chans), F32)]
    work = (cols, 32 * plan.chans)
    return step_call(partial(masks_kernel, plan, step), f"masks_{step}", 1, shapes, [avail, tgt, *counts], scalars, work)[0]


def backward_kernel(plan, step, info, order, quad, *refs):
    group, rows, waves, _, steps, fields, chans, hidden, lons = plan
    first, last = step == steps - 1, step == 0
    fresh = step == steps - 2
    rows_blk = pair_rows(plan)
    members = 2 * group
    levels = chans // fields
    refs = list(refs)
    take = lambda: refs.pop(0)
    units, slopes, scales, w2, w3, nb = [take() for _ in range(6)]
    if first:
        avail, tgt = take(), take()
        counts = [take() for _ in range(members)]
    else:
        masks = take()
        links, lt, ffw_t = [take() for _ in range(3)]
        pieces = [take() for _ in range(members)]
        if not fresh:
            bstate = take()
    if not last:
        w1, inv = take(), take()
    dzs = take()
    if not last:
        b_out = take()
        if not first:
            bstate_out = take()
    if first:
        loss, gmask = take(), take()
    else:
        coef = take()
    i = pl.program_id(0)

    @pl.when(i == 0)
    def _():
        if first:
            gmask[...], bias_of = shares(plan, step, counts, tgt)
            sq = bias_of(0) * bias_of(0)
            for s in range(1, steps):
                sq = sq + bias_of(s) * bias_of(s)
            loss[...] = jnp.broadcast_to(jnp.sum(sq, axis=0, keepdims=True) / steps, loss.shape)
        else:
            for p in range(2):
                st = dot(links[...], jnp.concatenate([piece[p] for piece in pieces], axis=0))
                if not fresh:
                    st = bstate[p] + st
                if not last:
                    bstate_out[p] = st
                coef[p] = dot(lt[...], (STEP_SCALE * st).astype(BF16)).astype(BF16)

    gains, _ = splits(nb, chans, hidden)

    def norm_back(back, gain, unit):
        low = back * gain
        m1 = jnp.mean(low, axis=-1, keepdims=True)
        m2 = jnp.mean(low * unit, axis=-1, keepdims=True)
        return low - m1 - unit * m2

    def row_chain(rr):
        row = i * rows_blk + rr
        at = pl.ds(pl.multiple_of(row * waves, waves), waves)
        q = row_weight(plan, info, order, quad, row)
        chunks = [pl.ds(pl.multiple_of(row * lons + c, CHUNK), CHUNK) for c in range(0, lons, CHUNK)]
        cut = lambda v: [v[c : c + CHUNK] for c in range(0, lons, CHUNK)]
        if first:
            mask = cut(spread_share(avail, gmask[...], row))
        else:
            tend = dot(ffw_t[...], jnp.concatenate([coef[0, at, :], coef[1, at, :]], axis=0))
        yield
        dpreds, low = [], []
        for n, cs in enumerate(chunks):
            dpred = q * mask[n] if first else masks[cs, :]
            dout = STEP_SCALE * dpred
            if first:
                dpreds.append(dpred)
            else:
                dout = dout + q * cut(tend)[n]
            low.append(dout.astype(BF16))
            dzs[cs, 2 * hidden :] = low[-1]
        yield
        for k, weight in ((2, w3), (1, w2)):
            back = dot(jnp.concatenate(low, axis=0), weight[...], ((1,), (1,)))
            yield
            low = []
            span = slice(chans + (k - 1) * hidden, chans + k * hidden)
            inner = slice((k - 1) * hidden, k * hidden)
            for cs, part in zip(chunks, cut(back)):
                dx = norm_back(part, gains[k], units[cs, span])
                low.append((dx * slopes[cs, inner]).astype(BF16))
                dzs[cs, inner] = low[-1]
            yield
        if not last:
            back = dot(jnp.concatenate(low, axis=0), w1[...], ((1,), (1,)))
            yield
            grids = []
            for n, (cs, part) in enumerate(zip(chunks, cut(back))):
                dx = norm_back(part, gains[0], units[cs, 0:chans])
                dpred = dpreds[n] if first else masks[cs, :]
                grids.append((dpred + dx * wide(scales[cs, 0:LANES], chans)).astype(BF16))
            yield
            coeff = dot(inv[...], jnp.concatenate(grids, axis=0)).astype(BF16)
            b_out[0, at, :] = coeff[:waves]
            b_out[1, at, :] = coeff[waves:]
            yield

    stagger([row_chain(rr) for rr in range(rows_blk)])


def backward_call(plan, step, scalars, saved, wanted, weights, nb, tables, pieces, bstate):
    group, rows, waves, degrees, steps, fields, chans, hidden, lons = plan
    first, last = step == steps - 1, step == 0
    rows_blk = pair_rows(plan)
    links, lt, ffw_t, inv = tables
    ins = [*saved, *weights[1:], nb, *wanted]
    if not first:
        ins += [links, lt, ffw_t, *pieces]
        if step != steps - 2:
            ins.append(bstate)
    if not last:
        ins += [weights[0], inv]
    sums = (2, rows * waves, chans)
    shapes = [VM((rows * lons, 2 * hidden + chans), BF16)]
    if not last:
        shapes.append(VM(sums, BF16))
        if not first:
            shapes.append(VM((2, waves * degrees, chans), F32))
    if first:
        shapes.append(VM((8, LANES), F32))
    flops = 2 * hidden * (2 * chans + hidden)
    return step_call(
        partial(backward_kernel, plan, step),
        f"backward_{step}",
        rows // rows_blk,
        shapes,
        ins,
        scalars,
        (rows * lons, flops),
        [VM((2 * fields, chans), BF16) if first else VM(sums, BF16)],
    )


def grads_kernel(plan, step, info, *refs):
    _, rows, _, _, steps, _, chans, hidden, lons = plan
    first, last = step == steps - 1, step == 0
    refs = list(refs)
    take = lambda: refs.pop(0)
    units, dzs, nb = [take() for _ in range(3)]
    before = None if first else [take() for _ in range(4)]
    if last:
        weights = [take() for _ in range(3)]
        mine, send = take(), take()
    grads = [take() for _ in range(4)]
    gains, _ = splits(nb, chans, hidden)
    ins = ((0, chans), (chans, hidden), (chans + hidden, hidden))
    outs = ((0, hidden), (hidden, hidden), (2 * hidden, chans))
    for k in range(3):
        a, b = ins[k][0], outs[k][0]
        unit = slice(a, a + ins[k][1])
        slot = slice(b, b + outs[k][1])
        low = [(units[c : c + CHUNK, unit] * gains[k]).astype(BF16) for c in range(0, rows * lons, CHUNK)]
        new = dot(jnp.concatenate(low, axis=0), dzs[:, slot], ((0,), (0,)))
        bias = fold(dzs[0:CHUNK, slot].astype(F32))
        for c in range(CHUNK, rows * lons, CHUNK):
            bias = bias + fold(dzs[c : c + CHUNK, slot].astype(F32))
        if not first:
            new = before[k][...] + new
            bias = before[3][:, slot] + bias
        grads[k][...] = new
        grads[3][:, slot] = bias
    if not last:
        return
    half = mine.shape[0]
    parts, at = packed_parts(plan)
    lines = []
    for k in range(3):
        prod = grads[k][...] * weights[k][...].astype(F32)
        thin = prod[:, 0:LANES]
        for tile in range(1, prod.shape[1] // LANES):
            thin = thin + prod[:, tile * LANES : (tile + 1) * LANES]
        lines.append(jnp.sum(thin.T, axis=0, keepdims=True) / gains[k])
    tail = []
    for line in (jnp.concatenate(lines, axis=1), jnp.sum(grads[3][...], axis=0, keepdims=True)):
        tail += [line[:, c : c + LANES] for c in range(0, line.shape[1], LANES)]
    tail = jnp.concatenate([*tail, jnp.zeros((2 * half - at - len(tail), LANES), F32)], axis=0)

    def pack(halves):
        for which, tile, start, count in parts:
            for h, dst, src, n in both_halves(start, count, half):
                part = grads[which][src : src + n, tile * LANES : (tile + 1) * LANES]
                halves[h][dst : dst + n, :] = part.astype(halves[h].dtype)
        halves[1][at - half :, :] = tail.astype(halves[1].dtype)

    pl.when(info[0] == 0)(lambda: pack((mine, send)))
    pl.when(info[0] == 1)(lambda: pack((send, mine)))


def grads_call(plan, step, chips, info, units, dzs, nb, before, weights):
    _, rows, _, _, steps, _, chans, hidden, lons = plan
    first, last = step == steps - 1, step == 0
    ins = [units, dzs, nb]
    aliases = {}
    if not first:
        ins += before
    sums = [VM(s, F32) for s in ((chans, hidden), (hidden, hidden), (hidden, chans), (8, 2 * hidden + chans))]
    if last:
        ins += weights
        half = chips * packed_block(plan, chips)
        shapes, scratch = [VM((half, LANES), F32), VM((half, LANES), BF16)], sums
    else:
        shapes, scratch = sums, []
        if not first:
            aliases = {4 + n: n for n in range(4)}
    flops = 2 * hidden * (2 * chans + hidden)
    return step_call(
        partial(grads_kernel, plan, step), f"grads_{step}", 1, shapes, ins, (info,), (rows * lons, flops), scratch, aliases
    )


def pairs_kernel(chips, group, mine, got, loss, out):
    blk = mine.shape[0] // chips
    share = loss[...] * (1.0 / group)
    row = lax.broadcasted_iota(jnp.int32, share.shape, 0)
    high = share.astype(BF16).astype(F32)
    rest = share - high
    mid = rest.astype(BF16).astype(F32)
    lines = jnp.where(row == 0, high, jnp.where(row == 1, mid, jnp.where(row == 2, rest - mid, 0.0)))
    lines = jnp.concatenate([lines, jnp.zeros_like(lines)], axis=0).astype(BF16)
    for c in range(chips):
        at = slice(c * blk, (c + 1) * blk)
        out[c, 0:blk, :] = (mine[at, :] + got[at, :].astype(F32)).astype(BF16)
        out[c, blk:, :] = lines


def chips_kernel(got, out, loss):
    chips, blk = out.shape[0], out.shape[1]
    total = got[0].astype(F32)
    for c in range(1, chips):
        total = total + got[c].astype(F32)
    low = total[0:blk].astype(BF16)
    for c in range(chips):
        out[c] = low
    loss[...] = jnp.broadcast_to(jnp.sum(total[blk:], axis=0, keepdims=True), loss.shape)


def update_kernel(plan, info, part, part_o, loss, *refs):
    params, means, squares = refs[0:4], refs[4:8], refs[8:12]
    scalars = refs[12:14]
    outs = [refs[14 + 4 * k : 18 + 4 * k] for k in range(4)]
    packed, sems = refs[30], refs[31]
    stage = [refs[32 + 4 * k : 36 + 4 * k] for k in range(4)]
    ones = refs[48:50]
    packed[info[0]] = part[...]
    packed[1 - info[0]] = part_o[...]
    half = packed.shape[1]
    acc = jnp.zeros((16, LANES), F32)
    for h in range(2):
        g = packed[h].astype(F32)
        acc = acc + jnp.sum((g * g).reshape(half // 16, 16, LANES), axis=0)
    total = jnp.sum(jnp.sum(acc, axis=0, keepdims=True), axis=1, keepdims=True)
    root = jnp.sqrt(total)
    ones[0][...] = loss[0:1, 0:1]
    ones[1][...] = root
    singles = [pltpu.make_async_copy(ones[n], scalars[n], sems.at[16 + n]) for n in range(2)]
    for copy in singles:
        copy.start()
    factor = jnp.broadcast_to(CLIP_NORM / jnp.maximum(root, CLIP_NORM), (1, LANES))

    def apply(which, rs, cs, g):
        g = g * factor
        w = params[which][rs, cs]
        a = BETA_ONE * means[which][rs, cs] + (1.0 - BETA_ONE) * g
        b = BETA_TWO * squares[which][rs, cs] + (1.0 - BETA_TWO) * g * g
        w = w - LEARN_RATE * (a / (b * lax.rsqrt(b) + EPS_ADAM) + DECAY * w)
        for k, value in enumerate((w, a, b, w.astype(BF16))):
            stage[k][which][rs, cs] = value

    def copies(which):
        return [
            pltpu.make_async_copy(stage[k][which], outs[k][which], sems.at[4 * which + k]) for k in range(4)
        ]

    parts, at = packed_parts(plan)
    for n, (which, tile, start, count) in enumerate(parts):
        cs = slice(tile * LANES, (tile + 1) * LANES)
        for h, src, dst, size in both_halves(start, count, half):
            for c in range(0, size, UPDATE_ROWS):
                n_rows = min(UPDATE_ROWS, size - c)
                g = packed[h, src + c : src + c + n_rows, :].astype(F32)
                apply(which, slice(dst + c, dst + c + n_rows), cs, g)
        if n + 1 == len(parts) or parts[n + 1][0] != which:
            for copy in copies(which):
                copy.start()
    tiles = (plan.chans + 2 * plan.hidden) // LANES
    rows = packed[1, at - half : at - half + 2 * tiles, :].astype(F32)
    for tile in range(tiles):
        g = jnp.concatenate([rows[tile : tile + 1], rows[tiles + tile : tiles + tile + 1]], axis=0)
        apply(3, slice(0, 2), slice(tile * LANES, (tile + 1) * LANES), g)
    for copy in copies(3):
        copy.start()
    for copy in singles:
        copy.wait()
    for which in range(4):
        for copy in copies(which):
            copy.wait()


def update_call(plan, info, part, part_o, loss, params, means, squares):
    kinds = (F32, F32, F32, BF16)
    hbm = pl.BlockSpec(memory_space=pl.ANY)
    vmem = pl.BlockSpec(memory_space=VM)
    return pl.pallas_call(
        partial(update_kernel, plan),
        out_shape=[jax.ShapeDtypeStruct((1, 1), F32)] * 2 + [jax.ShapeDtypeStruct(w.shape, kind) for kind in kinds for w in params],
        grid_spec=pltpu.PrefetchScalarGridSpec(
            num_scalar_prefetch=1,
            grid=(1,),
            in_specs=[vmem] * 15,
            out_specs=[hbm] * 18,
            scratch_shapes=[VM((2, *part.shape), BF16), pltpu.SemaphoreType.DMA((18,))]
            + [VM(w.shape, kind) for kind in kinds for w in params]
            + [VM((1, 1), F32)] * 2,
        ),
        compiler_params=kernel_params(),
        name="update",
    )(info, part, part_o, loss, *params, *means, *squares)


def small_call(kernel, name, shapes, ins, scalars=(), scratch=()):
    return pl.pallas_call(
        kernel,
        out_shape=shapes,
        grid_spec=pltpu.PrefetchScalarGridSpec(
            num_scalar_prefetch=len(scalars),
            grid=(1,),
            in_specs=[whole(a) for a in ins],
            out_specs=[whole(a) for a in shapes],
            scratch_shapes=list(scratch),
        ),
        compiler_params=kernel_params(),
        name=name,
    )(*scalars, *ins)


def grouped_device(
    plan,
    chips,
    spectral_state,
    legendre,
    wave_slots,
    lat_order,
    quad_weights,
    available,
    targets,
    *flat,
):
    group, rows, waves, degrees, steps, fields, chans, hidden, lons = plan
    params, means, squares = flat[0:4], flat[4:8], flat[8:12]
    weights = [w.astype(BF16) for w in params[:3]]
    nb = params[3]
    tdev = spectral_state.shape[0]
    copies = waves // chips
    core = lax.axis_index("tm")
    chip = lax.axis_index("lat")
    member = chip % group
    info = jnp.stack([core, member]).astype(jnp.int32)
    swap = [(0, 1), (1, 0)]
    across = lambda a: lax.ppermute(a, "tm", swap)

    def to_members(a, fill):
        out = [a]
        bit = 1
        while bit < group:
            out += [lax.ppermute(v, "lat", [(n, n ^ bit) for n in range(waves)]) for v in out]
            bit *= 2
        away, filled = lax.optimization_barrier((out[1:], fill()))
        out = [a, *away]
        return out + [across(v) for v in out], filled

    def to_each(a, fill):
        places = [(c, n) for c in range(2) for n in range(waves)]
        out = []
        for other, m in [(c, n) for c in range(2) for n in range(group)][1:]:
            if other and not m:
                out.append(across(a))
            else:
                pairs = [(c * waves + n, (c ^ other) * waves + (n ^ m)) for c, n in places]
                out.append(lax.ppermute(a, ("tm", "lat"), pairs))
        out, filled = lax.optimization_barrier((out, fill()))
        return [a, *out], filled

    deep = -(-(2 * degrees + fields // 2 + 1) // 8) * 8
    keep, send = pack_call(info, spectral_state, available, legendre, deep)
    other = across(send)
    times = jnp.concatenate([jnp.where(core == 0, keep, other), jnp.where(core == 0, other, keep)], axis=0)
    spread = jnp.broadcast_to(times[None, :, None], (copies, 2 * tdev, group, *times.shape[1:]))
    got = lax.all_to_all(spread.reshape(waves, *times.shape[1:]), "lat", split_axis=0, concat_axis=0, tiled=True)
    got_o = across(got)

    def table(scaled):
        product = wave_slots[:, None] * jnp.arange(lons, dtype=jnp.int32)[None, :] % lons
        phase = product.astype(F32) * (2.0 * math.pi / lons)
        inverse = jnp.concatenate([jnp.cos(phase), -jnp.sin(phase)], axis=0)
        if not scaled:
            return inverse
        scale = jnp.where(wave_slots == 0, 1.0, 2.0).astype(F32) / lons
        return inverse * jnp.concatenate([scale, scale])[:, None]

    inv32, ffw32 = table(False), table(True)
    inv, ffw = inv32.astype(BF16), ffw32.astype(BF16)
    theirs = across(targets)
    tgt_all = jnp.concatenate([jnp.where(core == 0, targets, theirs), jnp.where(core == 0, theirs, targets)], axis=0)
    tgt = lax.dynamic_index_in_dim(tgt_all, (chip // group) % (2 * tdev), axis=0, keepdims=False)
    tgt = jnp.broadcast_to(tgt.reshape(steps * fields, 1), (steps * fields, LANES))
    made = links_call(plan, info, wave_slots, lat_order, got, inv32, ffw32, tgt)
    got_o, (state, links, lt, inv_t, ffw_t, tgt) = lax.optimization_barrier((got_o, made))
    scalars = (info, lat_order, quad_weights)

    saved, pieces, avail, nums = [], None, None, None
    for s in range(steps):
        units, inners, scales, *rest = forward_call(
            plan, s, scalars, [state] if s else [got, got_o], avail, nums, inv_t, ffw, lt, weights, nb, links, pieces
        )
        fill = lambda: slopes_call(plan, s, inners, scales)
        if s == 0:
            fields = lambda: fields_call(plan, scalars, state, got, got_o)
            pieces, (slopes, (state, avail, nums)) = to_members(rest[2], lambda: (fill(), fields()))
        elif s < steps - 1:
            pieces, slopes = to_members(rest[2], fill)
        if s < steps - 1:
            nums = counts_call(plan, s, scalars, [rest[0], rest[1], avail, nums, inv_t])
            pieces, nums = lax.optimization_barrier((pieces, nums))
            if s:
                state = rest[3]
        else:
            counts, slopes = to_each(rest[0], fill)
        saved.append((units, slopes, scales))
    before, bstate = None, None
    wanted = [avail, tgt, *counts]
    for s in reversed(range(steps)):
        dzs, *rest = backward_call(plan, s, scalars, saved[s], wanted, weights, nb, (links, lt, ffw_t, inv), pieces, bstate)
        grads = lambda: grads_call(plan, s, chips, info, saved[s][0], dzs, nb, before, weights)
        if s == 0:
            before = grads()
        else:
            fill = lambda: (grads(), [masks_call(plan, s - 1, scalars, avail, tgt, counts)])
            pieces, (before, wanted) = to_members(rest[0], fill)
            if s == steps - 1:
                loss = rest[1]
            else:
                bstate = rest[1]
    mine, send = before
    blk = mine.shape[0] // chips
    groups = [[c * chips + n for n in range(chips)] for c in range(copies)]
    exchange = lambda a: lax.all_to_all(a, "lat", split_axis=0, concat_axis=0, tiled=True, axis_index_groups=groups)
    (parts,) = small_call(
        partial(pairs_kernel, chips, group),
        "pairs",
        [jax.ShapeDtypeStruct((chips, blk + 16, LANES), BF16)],
        [mine, across(send), loss],
    )
    reduced, loss = small_call(
        chips_kernel,
        "chips",
        [jax.ShapeDtypeStruct((chips, blk, LANES), BF16), jax.ShapeDtypeStruct((8, LANES), F32)],
        [exchange(parts)],
    )
    part = exchange(reduced).reshape(chips * blk, LANES)
    loss, norm, *results = update_call(plan, info, part, across(part), loss, params, means, squares)
    return (loss.reshape(()), norm.reshape(()), *results)


def make_plan(mesh, args):
    state, legendre, _, _, _, available, targets, w_first = args[:8]
    times, waves, _, degrees, chans = state.shape
    _, fields, lats, lons = available.shape
    hidden = w_first.shape[1]
    cores, chips_all = mesh.shape["tm"], mesh.shape["lat"]
    group = GROUP
    chips = group * times
    rows, rest = divmod(lats, 2 * group)
    fits = (
        cores == 2
        and times % cores == 0
        and chips_all == waves == lats
        and waves % chips == 0
        and rest == 0
        and fields == 8
        and lons == chans == degrees * lats
        and waves % 16 == 0
        and degrees % 16 == 0
        and chans % LANES == 0
        and hidden % LANES == 0
        and lons % SUB == 0
    )
    if not fits or legendre.shape != (waves, degrees, lats):
        return None
    steps = targets.shape[1]
    if steps < 3 or steps * rows * lons * (chans + 4 * hidden + LANES) * 4 > SAVED_LIMIT:
        return None
    return Plan(group, rows, waves, degrees, steps, fields, chans, hidden, lons), chips


def solution(mesh):
    in_specs = (
        P("tm", "lat", None, None, None),
        P("lat", None, None),
        P(),
        P(),
        P(),
        P("tm", None, "lat", None),
        P("tm", None, None),
    ) + (P(),) * 12

    def run(*args):
        made = make_plan(mesh, args)
        body = spread_device if made is None else partial(grouped_device, *made)
        return jax.shard_map(body, mesh=mesh, in_specs=in_specs, out_specs=(P(),) * 18, check_vma=False)(*args)

    return run
```
